32 devices in a mesh: ctx: 16 (over z, y, x), head: 2 (over core).
Axes of the slice: x: 2, y: 2, z: 4, core: 2. Of those that a mesh axis runs over, the one named last changes fastest.
Arguments:
- banded_queries: bfloat16 [4096, 4096], P('ctx', 'head'), may hold values from -11.5 to 11.5
- banded_keys: bfloat16 [4096, 512], P('ctx', 'head'), may hold values from -11.5 to 11.5
- banded_values: bfloat16 [4096, 512], P('ctx', 'head'), may hold values from -6 to 6
- full_queries: bfloat16 [4096, 4096], P('ctx', 'head'), may hold values from -11.5 to 11.5
- full_keys: bfloat16 [4096, 512], P('ctx', 'head'), may hold values from -11.5 to 11.5
- full_values: bfloat16 [4096, 512], P('ctx', 'head'), may hold values from -6 to 6
- segment_ids: int32 [4096], P('ctx'), may hold values from 0 to 4095, as said below
- position_ids: int32 [4096], P('ctx'), may hold values from 0 to 8189, as said below
- out_weight: bfloat16 [4096, 2880], P('head'), may hold values from -0.09375 to 0.09375
Outputs:
- banded_out: bfloat16 [4096, 4096], P('ctx', 'head')
- projected: bfloat16 [4096, 2880], P(('ctx', 'head'))
The draws below stay inside these ranges and needn't reach their ends.
Inputs may be any that keep to these rules, and one draw needn't show every extreme that they name: `segment_ids`: never falling; a document's id is the index of its last token; every document holds 1 to 3072 tokens, and one holds exactly 3072. `position_ids`: within a document they rise by 1 or 2 from one token to the next.
All inputs are finite; a program needn't handle non-finite values.
Results may differ from the reference program's by a relative error of at most 0.015.
The reference program's roundings to bfloat16 on the way count: a program that leaves them out, or rounds other values in their place, can miss the bound.
Values may be sent and summed in bfloat16 or wider, within the bound.
No kernel may reach another device: no remote copies, remote signals or barrier semaphores. Data moves between devices by JAX's collectives and lax.ppermute only.
A program may use at most 64 MiB of HBM per device.

```python
import jax
import jax.numpy as jnp
from jax import lax

HEADS = 64
KV_HEADS = 8
HEAD_DIM = 64
D = 2880
WINDOW = 128
REACH = 12
TOK_DEV = 256
TOKENS = 4096
MOST = 3072
N_CTX = 16
N_HEAD = 2


def document_layout(key):
    key_first, key_kind, key_long, key_short, key_climb, key_offset = jax.random.split(key, 6)
    first_length = jax.random.randint(key_first, (), 1, min(MOST, TOKENS - MOST) + 1)
    kinds = jax.random.randint(key_kind, (TOKENS,), 0, 4)
    longer = jax.random.randint(key_long, (TOKENS,), max(MOST // 2, 1), MOST + 1)
    shorter = jax.random.randint(key_short, (TOKENS,), 1, max(MOST // 8, 1) + 1)
    lengths = jnp.where(kinds == 0, longer, shorter)
    lengths = lengths.at[0].set(first_length).at[1].set(MOST)
    doc_ends = jnp.cumsum(lengths)
    starts = doc_ends - lengths
    token_index = jnp.arange(TOKENS, dtype=jnp.int32)
    ordinal = jnp.searchsorted(doc_ends, token_index, side='right').astype(jnp.int32)
    segments = jnp.minimum(doc_ends[ordinal] - 1, TOKENS - 1).astype(jnp.int32)
    steps_drawn = jax.random.randint(key_climb, (TOKENS,), 1, 3)
    steps_drawn = jnp.where(ordinal == 1, 2, steps_drawn)
    climbs = jnp.cumsum(steps_drawn)
    offsets = jax.random.randint(key_offset, (TOKENS,), 0, 2048)
    offsets = offsets.at[1].set(2047)
    doc_first = starts[ordinal]
    positions = offsets[ordinal] + climbs - climbs[doc_first]
    return (segments, positions.astype(jnp.int32))


def drawn_pair(key):
    key_query, key_key = jax.random.split(key, 2)
    queries = jax.random.truncated_normal(key_query, -4.0, 4.0, (TOKENS, HEADS, HEAD_DIM), jnp.float32)
    key_rows = jax.random.truncated_normal(key_key, -4.0, 4.0, (TOKENS, KV_HEADS, HEAD_DIM), jnp.float32)
    return (queries.reshape(TOKENS, HEADS * HEAD_DIM), key_rows.reshape(TOKENS, KV_HEADS * HEAD_DIM))


def draw_banded_queries(key, part):
    return drawn_pair(jax.random.fold_in(key, 21))[0].astype(jnp.bfloat16)


def draw_banded_keys(key, part):
    return drawn_pair(jax.random.fold_in(key, 21))[1].astype(jnp.bfloat16)


def draw_full_queries(key, part):
    return drawn_pair(jax.random.fold_in(key, 22))[0].astype(jnp.bfloat16)


def draw_full_keys(key, part):
    return drawn_pair(jax.random.fold_in(key, 22))[1].astype(jnp.bfloat16)


def draw_segment_ids(key, part):
    return document_layout(jax.random.fold_in(key, 7))[0]


def draw_position_ids(key, part):
    return document_layout(jax.random.fold_in(key, 7))[1]


def block_scale(own_key, extent, cuts, least, top_value):
    def one(axis_at, shards_of):
        heights = jax.random.uniform(jax.random.fold_in(jax.random.fold_in(own_key, 6), axis_at), (shards_of,), jnp.float32, least / len(cuts), top_value / len(cuts))
        return jnp.repeat(jnp.exp(heights), extent[axis_at] // shards_of).reshape((-1,) + (1,) * (len(extent) - axis_at - 1))

    loudness = one(*cuts[0])
    for cut in cuts[1:]:
        loudness = loudness * one(*cut)
    return loudness


def bell_draw(key, shape, deviation, bound, pieces=(), kind=jnp.bfloat16):
    drawn = deviation * jax.random.normal(key, shape, jnp.float32)
    if pieces:
        drawn = drawn * block_scale(key, shape, pieces, -0.22, 0.18)
    return jnp.clip(drawn, -bound, bound).astype(kind)


def setup_inputs(seed: int = 0) -> dict:
    arg_keys = jax.random.split(jax.random.key(seed), 10)
    banded_queries = draw_banded_queries(jax.random.fold_in(arg_keys[9], 71), 0)
    banded_keys = draw_banded_keys(jax.random.fold_in(arg_keys[9], 71), 0)
    banded_values = bell_draw(arg_keys[2], (TOKENS, KV_HEADS * HEAD_DIM), 1.0, 6.0, ((0, 16), (1, 2)))
    full_queries = draw_full_queries(jax.random.fold_in(arg_keys[9], 71), 0)
    full_keys = draw_full_keys(jax.random.fold_in(arg_keys[9], 71), 0)
    full_values = bell_draw(arg_keys[5], (TOKENS, KV_HEADS * HEAD_DIM), 1.0, 6.0, ((0, 16), (1, 2)))
    segment_ids = draw_segment_ids(jax.random.fold_in(arg_keys[9], 71), 0)
    position_ids = draw_position_ids(jax.random.fold_in(arg_keys[9], 71), 0)
    out_weight = bell_draw(arg_keys[8], (HEADS * HEAD_DIM, D), (HEADS * HEAD_DIM) ** -0.5, 0.09375, ((0, 2),))
    return {"banded_queries": banded_queries, "banded_keys": banded_keys, "banded_values": banded_values, "full_queries": full_queries, "full_keys": full_keys, "full_values": full_values, "segment_ids": segment_ids, "position_ids": position_ids, "out_weight": out_weight}


theta_base = 150000.0
neg_fill = -1.0e30


def rotary(values_in, positions):
    row_count = values_in.shape[0]
    head_count = values_in.shape[1] // HEAD_DIM
    half_width = HEAD_DIM // 2
    frequency = theta_base ** (-2.0 * jnp.arange(half_width, dtype=jnp.float32) / HEAD_DIM)
    angles = positions.astype(jnp.float32)[:, None] * frequency[None, :]
    cosine = jnp.cos(angles)[:, None, :]
    sine_term = jnp.sin(angles)[:, None, :]
    spread = values_in.astype(jnp.float32).reshape(row_count, head_count, HEAD_DIM)
    leading = spread[..., :half_width]
    trailing = spread[..., half_width:]
    turned = jnp.concatenate([leading * cosine - trailing * sine_term, trailing * cosine + leading * sine_term], axis=-1)
    return turned.reshape(row_count, head_count * HEAD_DIM).astype(jnp.bfloat16)


def attend(queries, key_rows, value_rows, segment_ids, back_shards, window):
    group_size = HEADS // KV_HEADS
    pad_rows = back_shards * TOK_DEV
    span = (back_shards + 1) * TOK_DEV
    keys_padded = jnp.concatenate([jnp.zeros((pad_rows, key_rows.shape[1]), key_rows.dtype), key_rows], axis=0)
    values_padded = jnp.concatenate([jnp.zeros((pad_rows, value_rows.shape[1]), value_rows.dtype), value_rows], axis=0)
    segments_padded = jnp.concatenate([jnp.full((pad_rows,), -1, jnp.int32), segment_ids.astype(jnp.int32)])
    scale_factor = HEAD_DIM ** -0.5

    def one_shard(shard):
        row_start = (shard * TOK_DEV).astype(jnp.int32)
        query_block = lax.dynamic_slice_in_dim(queries, row_start, TOK_DEV, 0).astype(jnp.float32)
        query_block = query_block.reshape(TOK_DEV, KV_HEADS, group_size, HEAD_DIM)
        key_block = lax.dynamic_slice_in_dim(keys_padded, row_start, span, 0).astype(jnp.float32).reshape(span, KV_HEADS, HEAD_DIM)
        value_block = lax.dynamic_slice_in_dim(values_padded, row_start, span, 0).astype(jnp.float32).reshape(span, KV_HEADS, HEAD_DIM)
        query_segments = lax.dynamic_slice_in_dim(segment_ids.astype(jnp.int32), row_start, TOK_DEV, 0)
        key_segments = lax.dynamic_slice_in_dim(segments_padded, row_start, span, 0)
        query_index = row_start + jnp.arange(TOK_DEV, dtype=jnp.int32)
        key_index = row_start - pad_rows + jnp.arange(span, dtype=jnp.int32)
        allowed = (query_segments[:, None] == key_segments[None, :]) & (key_index[None, :] <= query_index[:, None])
        allowed = allowed & (key_index[None, :] >= 0) & (query_index[:, None] - key_index[None, :] < window)
        scores = jnp.einsum("qhgd,khd->hgqk", query_block, key_block) * scale_factor
        masked = jnp.where(allowed, scores, neg_fill)
        peak = jnp.max(masked, axis=-1, keepdims=True)
        weights = jnp.where(allowed, jnp.exp(masked - peak), 0.0)
        total = jnp.sum(weights, axis=-1, keepdims=True)
        rounded = lax.optimization_barrier(weights.astype(jnp.bfloat16)).astype(jnp.float32)
        mixed = jnp.einsum("hgqk,khd->hgqd", rounded, value_block) / total
        mixed = jnp.transpose(mixed, (2, 0, 1, 3)).reshape(TOK_DEV, HEADS * HEAD_DIM)
        return mixed.astype(jnp.bfloat16)

    blocks = lax.map(one_shard, jnp.arange(N_CTX, dtype=jnp.int32))
    return blocks.reshape(N_CTX * TOK_DEV, HEADS * HEAD_DIM)


def reference(banded_queries, banded_keys, banded_values, full_queries, full_keys, full_values, segment_ids, position_ids, out_weight):
    banded_q_rot = rotary(banded_queries, position_ids)
    banded_k_rot = rotary(banded_keys, position_ids)
    full_q_rot = rotary(full_queries, position_ids)
    full_k_rot = rotary(full_keys, position_ids)
    banded_out = attend(banded_q_rot, banded_k_rot, banded_values, segment_ids, 1, WINDOW)
    full_mixed = attend(full_q_rot, full_k_rot, full_values, segment_ids, REACH, MOST)
    group_width = HEADS * HEAD_DIM // N_HEAD
    summed = jnp.zeros((full_mixed.shape[0], D), jnp.float32)
    for group in range(N_HEAD):
        columns = full_mixed[:, group * group_width:(group + 1) * group_width]
        weight_rows = out_weight[group * group_width:(group + 1) * group_width]
        part_term = jnp.dot(columns, weight_rows, preferred_element_type=jnp.float32)
        summed = summed + lax.optimization_barrier(part_term.astype(jnp.bfloat16)).astype(jnp.float32)
    projected = summed.astype(jnp.bfloat16)
    return banded_out, projected
```

```python
import functools

import jax
import jax.numpy as jnp
from jax import lax
from jax.experimental import pallas as pl
from jax.experimental.pallas import tpu as pltpu
from jax.sharding import PartitionSpec as P

HEAD_DIM = 64
WINDOW = 128
REACH = 12
PLANE = 4
PAD = 16
AUG = 2 * HEAD_DIM

theta_base = 150000.0
neg_fill = -1e30
to_log2 = HEAD_DIM ** (-0.5) * 1.4426950408889634

f32 = jnp.float32
bf16 = jnp.bfloat16
VM = pl.BlockSpec(memory_space=pltpu.VMEM)


def al(start, size):
    return pl.ds(pl.multiple_of(start, size), size)


def rotate_rows(rows, cosine, sine_term):
    half = HEAD_DIM // 2
    out = []
    for at in range(0, rows.shape[0], HEAD_DIM):
        leading = rows[at : at + half]
        trailing = rows[at + half : at + HEAD_DIM]
        out.append(leading * cosine - trailing * sine_term)
        out.append(trailing * cosine + leading * sine_term)
    return jnp.concatenate(out, axis=0).astype(bf16)


def prepare_kernel(base, bk, bv, fk, fv, cosine, sine, seg, full_block, band_block, rim, meta):
    tokens, width = fk.shape
    cos, sin = cosine[...], sine[...]
    ids = seg[...]
    shifted = ids + 1
    row = lax.broadcasted_iota(jnp.int32, (PAD, tokens), 0)
    high = jnp.broadcast_to(shifted >> 7, (PAD, tokens))
    low = jnp.broadcast_to(shifted & 127, (PAD, tokens))
    id_rows = jnp.where(row == 0, high, jnp.where(row == 1, low, 0)).astype(f32).astype(bf16)
    for keys, values, block in ((fk, fv, full_block), (bk, bv, band_block)):
        block[0:width, :] = rotate_rows(keys[...].astype(f32).T, cos, sin)
        block[width : 2 * width, :] = values[...].astype(f32).T.astype(bf16)
        block[2 * width :, :] = id_rows
    rim[...] = band_block[:, tokens - WINDOW :]
    ids_f = ids.astype(f32)
    across = jnp.broadcast_to(ids_f, (tokens, tokens))
    down = across.T
    before = jnp.max(jnp.where(down < across, down, -1.0), axis=0, keepdims=True)
    first = before < 0.0
    begin = jnp.where(first, 0.0, before + 1.0 - base[0].astype(f32))
    mrow = lax.broadcasted_iota(jnp.int32, (8, tokens), 0)
    meta[...] = jnp.where(
        mrow == 0,
        jnp.broadcast_to(begin, (8, tokens)),
        jnp.where(mrow == 1, jnp.broadcast_to(first.astype(f32), (8, tokens)), jnp.broadcast_to(ids_f + 1.0, (8, tokens))),
    )


def prepare(base, bk, bv, fk, fv, cosine, sine, seg):
    tokens, width = fk.shape
    height = 2 * width + PAD
    return pl.pallas_call(
        prepare_kernel,
        out_shape=(
            jax.ShapeDtypeStruct((height, tokens), bf16),
            jax.ShapeDtypeStruct((height, tokens), bf16),
            jax.ShapeDtypeStruct((height, WINDOW), bf16),
            jax.ShapeDtypeStruct((8, tokens), f32),
        ),
        in_specs=[pl.BlockSpec(memory_space=pltpu.SMEM)] + [VM] * 7,
        out_specs=(VM,) * 4,
        name="prepare",
    )(base, bk, bv, fk, fv, cosine, sine, seg)


def two_deep(units, scores, outs, s0, s1, x0, x1):
    scores(0, s0, x0)

    def pair(i, _):
        u = 2 * i
        scores(u + 1, s1, x1)
        outs(u, s0, x0)
        scores(jnp.minimum(u + 2, units - 1), s0, x0)
        outs(u + 1, s1, x1)
        return 0

    lax.fori_loop(0, units // 2, pair, 0)


def column_peak(s):
    return jnp.broadcast_to(jnp.max(s, axis=0, keepdims=True), (8, s.shape[1]))


def transposed_keys(block, head, extra):
    kt = block[head * HEAD_DIM : (head + 1) * HEAD_DIM, :].astype(f32)
    return jnp.concatenate([kt, extra], axis=0).T.astype(bf16)


def mask_rows(block, width, own_id):
    tokens = block.shape[1]
    ids = block[2 * width : 2 * width + PAD, :].astype(f32)
    ids = ids[0:1] * 128.0 + ids[1:2]
    bar = jnp.where(ids < own_id, neg_fill, 0.0)
    row = lax.broadcasted_iota(jnp.int32, (HEAD_DIM, tokens), 0)
    return jnp.where(row == 0, jnp.broadcast_to(bar, row.shape), jnp.where(row == 1, 1.0, 0.0))


def own_kernel(group, fq, bq, cosine, sine, block, meta, fqt, bqt, peak, total, accum, keys, s0, s1, x0, x1):
    tokens, wide = fq.shape
    width = wide // group
    kv = width // HEAD_DIM
    cos, sin = cosine[...], sine[...]
    step = min(wide, 4 * AUG)
    for src, dst in ((fq, fqt), (bq, bqt)):
        for at in range(0, wide, step):
            dst[at : at + step, :] = rotate_rows(src[:, at : at + step].astype(f32).T, cos, sin)
    zero = jnp.zeros((HEAD_DIM, tokens), f32)
    for h in range(kv):
        keys[h * tokens : (h + 1) * tokens, :] = transposed_keys(block, h, zero)
    begin = jnp.broadcast_to(meta[0:1, :], (tokens, tokens)).astype(jnp.int32)
    r = lax.broadcasted_iota(jnp.int32, (tokens, tokens), 0)
    t = lax.broadcasted_iota(jnp.int32, (tokens, tokens), 1)

    def scores(u, buf, x):
        h = u // group
        q = fqt[al(u * HEAD_DIM, HEAD_DIM), :]
        k = keys[al(h * tokens, tokens), :][:, :HEAD_DIM]
        s = jnp.dot(k, q, preferred_element_type=f32)
        s = jnp.where((r >= begin) & (r <= t), s, neg_fill)
        buf[...] = s
        x[...] = column_peak(s)

    def outs(u, buf, x):
        h = u // group
        m = x[0:1]
        p = jnp.exp2(buf[...] * to_log2 - m * to_log2)
        peak[pl.ds(u, 1), :] = m
        total[pl.ds(u, 1), :] = jnp.sum(p, axis=0, keepdims=True)
        v = block[al(width + h * HEAD_DIM, HEAD_DIM), :]
        accum[al(u * HEAD_DIM, HEAD_DIM), :] = jnp.dot(v, p.astype(bf16), preferred_element_type=f32)

    two_deep(wide // HEAD_DIM, scores, outs, s0, s1, x0, x1)


def own(group, fq, bq, cosine, sine, block, meta):
    tokens, wide = fq.shape
    heads = wide // HEAD_DIM
    kv = heads // group
    return pl.pallas_call(
        functools.partial(own_kernel, group),
        out_shape=(
            jax.ShapeDtypeStruct((wide, tokens), bf16),
            jax.ShapeDtypeStruct((wide, tokens), bf16),
            jax.ShapeDtypeStruct((heads, tokens), f32),
            jax.ShapeDtypeStruct((heads, tokens), f32),
            jax.ShapeDtypeStruct((wide, tokens), f32),
        ),
        in_specs=[VM] * 6,
        out_specs=(VM,) * 5,
        scratch_shapes=[
            pltpu.VMEM((kv * tokens, AUG), bf16),
            pltpu.VMEM((tokens, tokens), f32),
            pltpu.VMEM((tokens, tokens), f32),
            pltpu.VMEM((8, tokens), f32),
            pltpu.VMEM((8, tokens), f32),
        ],
        compiler_params=pltpu.CompilerParams(vmem_limit_bytes=40 << 20),
        cost_estimate=pl.CostEstimate(
            flops=4 * heads * tokens * tokens * HEAD_DIM * 4, transcendentals=heads * tokens * tokens, bytes_accessed=12 * wide * tokens
        ),
        name="own",
    )(fq, bq, cosine, sine, block, meta)


def band_kernel(group, bqt, block, rim, meta, out, keys, vals, s0, s1, x0, x1):
    wide, tokens = bqt.shape
    width = wide // group
    kv = width // HEAD_DIM
    span = tokens + WINDOW
    zero = jnp.zeros((HEAD_DIM, tokens), f32)
    for h in range(kv):
        keys[h * span : h * span + WINDOW, :] = transposed_keys(rim, h, zero[:, :WINDOW])
        keys[h * span + WINDOW : (h + 1) * span, :] = transposed_keys(block, h, zero)
    vals[:, :WINDOW] = rim[width : 2 * width, :]
    vals[:, WINDOW:] = block[width : 2 * width, :]
    own_id = jnp.min(meta[2:3, :])
    ids = rim[2 * width : 2 * width + PAD, :].astype(f32)
    ids = ids[0:1] * 128.0 + ids[1:2]
    barred = jnp.sum((ids < own_id).astype(f32))
    begin = meta[0:1, :]
    first = meta[1:2, :]
    r = lax.broadcasted_iota(jnp.int32, (2 * WINDOW, 2 * WINDOW), 0).astype(f32)
    t = (lax.broadcasted_iota(jnp.int32, (1, 2 * WINDOW), 1) & (WINDOW - 1)).astype(f32)
    lo0 = jnp.where(first > 0.0, barred, begin + WINDOW)[:, :WINDOW]
    lo1 = begin[:, WINDOW:]
    lows = [jnp.maximum(jnp.concatenate([lo, lo], axis=1), t + 1.0) for lo in (lo0, lo1)]
    pairs = group // 2

    for half in range(2):
        low = jnp.broadcast_to(lows[half], r.shape)
        high = jnp.broadcast_to(t + WINDOW, r.shape)
        lanes = slice(half * WINDOW, (half + 1) * WINDOW)
        keep_lanes = slice(half * WINDOW, half * WINDOW + 2 * WINDOW)

        def scores(u, buf, x):
            h = u // pairs
            q = bqt[al(u * AUG, AUG), :]
            q = jnp.concatenate([q[:HEAD_DIM, lanes], q[HEAD_DIM:, lanes]], axis=1)
            k = keys[pl.ds(pl.multiple_of(h * span + half * WINDOW, WINDOW), 2 * WINDOW), :][:, :HEAD_DIM]
            s = jnp.dot(k, q, preferred_element_type=f32)
            s = jnp.where((r >= low) & (r <= high), s, neg_fill)
            buf[...] = s
            x[...] = column_peak(s)

        def outs(u, buf, x):
            h = u // pairs
            m = x[0:1]
            p = jnp.exp2(buf[...] * to_log2 - m * to_log2)
            total = jnp.sum(p, axis=0, keepdims=True)
            v = vals[al(h * HEAD_DIM, HEAD_DIM), keep_lanes]
            o = jnp.dot(v, p.astype(bf16), preferred_element_type=f32) / total
            o = jnp.concatenate([o[:, :WINDOW], o[:, WINDOW:]], axis=0)
            out[lanes, al(u * AUG, AUG)] = o.T.astype(bf16)

        two_deep(kv * pairs, scores, outs, s0, s1, x0, x1)


def band(group, bqt, block, rim, meta):
    wide, tokens = bqt.shape
    kv = wide // group // HEAD_DIM
    span = tokens + WINDOW
    return pl.pallas_call(
        functools.partial(band_kernel, group),
        out_shape=jax.ShapeDtypeStruct((tokens, wide), bf16),
        in_specs=[VM] * 4,
        out_specs=VM,
        scratch_shapes=[
            pltpu.VMEM((kv * span, AUG), bf16),
            pltpu.VMEM((kv * HEAD_DIM, span), bf16),
            pltpu.VMEM((2 * WINDOW, 2 * WINDOW), f32),
            pltpu.VMEM((2 * WINDOW, 2 * WINDOW), f32),
            pltpu.VMEM((8, 2 * WINDOW), f32),
            pltpu.VMEM((8, 2 * WINDOW), f32),
        ],
        compiler_params=pltpu.CompilerParams(vmem_limit_bytes=24 << 20),
        cost_estimate=pl.CostEstimate(
            flops=4 * wide * tokens * 2 * WINDOW * 4, transcendentals=wide // HEAD_DIM * tokens * 2 * WINDOW, bytes_accessed=4 * wide * tokens
        ),
        name="band",
    )(bqt, block, rim, meta)


def remote_update(group, fqt, blocks, meta, state_in, state_out, keys, s0, s1, x0, x1):
    wide, tokens = fqt.shape
    width = wide // group
    kv = width // HEAD_DIM
    count = len(blocks)
    span = count * tokens
    peak_in, total_in, accum_in = state_in
    peak, total, accum = state_out
    own_id = jnp.min(meta[2:3, :])
    for b, block in enumerate(blocks):
        extra = mask_rows(block, width, own_id)
        for h in range(kv):
            keys[h * span + b * tokens : h * span + (b + 1) * tokens, :] = transposed_keys(block, h, extra)
    row = lax.broadcasted_iota(jnp.int32, (HEAD_DIM, tokens), 0)
    other = jnp.where(meta[1:2, :] > 0.0, 0.0, neg_fill)
    query_rows = jnp.where(row == 0, 1.0, jnp.where(row == 1, jnp.broadcast_to(other, row.shape), 0.0)).astype(bf16)

    def scores(u, buf, x):
        h = u // group
        q = jnp.concatenate([fqt[al(u * HEAD_DIM, HEAD_DIM), :], query_rows], axis=0)
        s = jnp.dot(keys[al(h * span, span), :], q, preferred_element_type=f32)
        buf[...] = s
        x[...] = column_peak(s)

    def outs(u, buf, x):
        h = u // group
        old = peak_in[pl.ds(u, 1), :]
        m = jnp.maximum(old, x[0:1])
        scaled = m * to_log2
        factor = jnp.exp2(old * to_log2 - scaled)
        peak[pl.ds(u, 1), :] = m
        rows = al(u * HEAD_DIM, HEAD_DIM)
        t = total_in[pl.ds(u, 1), :] * factor
        a = accum_in[rows, :] * factor
        for b, block in enumerate(blocks):
            p = jnp.exp2(buf[b * tokens : (b + 1) * tokens, :] * to_log2 - scaled)
            t = t + jnp.sum(p, axis=0, keepdims=True)
            v = block[al(width + h * HEAD_DIM, HEAD_DIM), :]
            a = a + jnp.dot(v, p.astype(bf16), preferred_element_type=f32)
        total[pl.ds(u, 1), :] = t
        accum[rows, :] = a

    two_deep(wide // HEAD_DIM, scores, outs, s0, s1, x0, x1)


def remote_scratch(kv, tokens, count):
    span = count * tokens
    return [
        pltpu.VMEM((kv * span, AUG), bf16),
        pltpu.VMEM((span, tokens), f32),
        pltpu.VMEM((span, tokens), f32),
        pltpu.VMEM((8, tokens), f32),
        pltpu.VMEM((8, tokens), f32),
    ]


def remote_kernel(group, counts, fqt, *refs):
    n = len(counts)
    blocks = [ref.at[j] if c > 0 else ref for ref, c in zip(refs[:n], counts) for j in range(max(c, 1))]
    meta, peak_in, total_in, accum_in, peak, total, accum = refs[n : n + 7]
    remote_update(group, fqt, blocks, meta, (peak_in, total_in, accum_in), (peak, total, accum), *refs[n + 7 :])


def remote(group, fqt, parts, meta, state):
    wide, tokens = fqt.shape
    heads = wide // HEAD_DIM
    counts = tuple(p.shape[0] if p.ndim == 3 else 0 for p in parts)
    count = sum(max(c, 1) for c in counts)
    n = len(parts)
    return pl.pallas_call(
        functools.partial(remote_kernel, group, counts),
        out_shape=tuple(jax.ShapeDtypeStruct(x.shape, x.dtype) for x in state),
        in_specs=[VM] * (n + 5),
        out_specs=(VM,) * 3,
        scratch_shapes=remote_scratch(heads // group, tokens, count),
        input_output_aliases={n + 2 + i: i for i in range(3)},
        compiler_params=pltpu.CompilerParams(vmem_limit_bytes=40 << 20),
        cost_estimate=pl.CostEstimate(
            flops=4 * wide * tokens * tokens * count * 4, transcendentals=heads * tokens * tokens * count, bytes_accessed=20 * wide * tokens
        ),
        name="remote",
    )(fqt, *parts, meta, *state)


def last_kernel(group, counts, fqt, *refs):
    n = len(counts)
    blocks = [ref.at[j] if c > 0 else ref for ref, c in zip(refs[:n], counts) for j in range(max(c, 1))]
    meta, peak_in, total_in, accum_in, weight, out = refs[n : n + 6]
    keys, s0, s1, x0, x1, peak, total, accum, mixed, held, sem = refs[n + 6 :]
    copy = pltpu.make_async_copy(weight, held, sem)
    copy.start()
    remote_update(group, fqt, blocks, meta, (peak_in, total_in, accum_in), (peak, total, accum), keys, s0, s1, x0, x1)
    wide, tokens = fqt.shape
    for u in range(0, wide // AUG):
        a = accum[u * AUG : (u + 1) * AUG, :]
        a = jnp.concatenate([a[:HEAD_DIM] / total[2 * u : 2 * u + 1, :], a[HEAD_DIM:] / total[2 * u + 1 : 2 * u + 2, :]], axis=0)
        mixed[:, u * AUG : (u + 1) * AUG] = a.T.astype(bf16)
    copy.wait()
    columns = out.shape[1]
    step = 4 * AUG
    for at in range(0, columns, step):
        size = min(step, columns - at)
        out[:, at : at + size] = jnp.dot(mixed[...], held[:, at : at + size], preferred_element_type=f32).astype(bf16)


def last(group, fqt, parts, meta, state, weight):
    wide, tokens = fqt.shape
    heads = wide // HEAD_DIM
    counts = tuple(p.shape[0] if p.ndim == 3 else 0 for p in parts)
    count = sum(max(c, 1) for c in counts)
    n = len(parts)
    return pl.pallas_call(
        functools.partial(last_kernel, group, counts),
        out_shape=jax.ShapeDtypeStruct((tokens, weight.shape[1]), bf16),
        in_specs=[VM] * (n + 5) + [pl.BlockSpec(memory_space=pl.ANY)],
        out_specs=VM,
        scratch_shapes=remote_scratch(heads // group, tokens, count)
        + [
            pltpu.VMEM((heads, tokens), f32),
            pltpu.VMEM((heads, tokens), f32),
            pltpu.VMEM((wide, tokens), f32),
            pltpu.VMEM((tokens, wide), bf16),
            pltpu.VMEM(weight.shape, bf16),
            pltpu.SemaphoreType.DMA,
        ],
        compiler_params=pltpu.CompilerParams(vmem_limit_bytes=56 << 20),
        cost_estimate=pl.CostEstimate(
            flops=4 * wide * tokens * tokens * count * 4, transcendentals=heads * tokens * tokens * count, bytes_accessed=20 * wide * tokens
        ),
        name="last",
    )(fqt, *parts, meta, *state, weight)


def shifted_by(block, distance):
    size = lax.axis_size("ctx")
    return lax.ppermute(block, "ctx", [(i, i + distance) for i in range(size - distance)])


def swapped(block, bit):
    size = lax.axis_size("ctx")
    return lax.ppermute(block, "ctx", [(i, i ^ bit) for i in range(size)])


def body(banded_queries, banded_keys, banded_values, full_queries, full_keys, full_values, segment_ids, position_ids, out_weight):
    tokens = segment_ids.shape[0]
    group = banded_queries.shape[1] // banded_keys.shape[1]
    here = lax.axis_index("ctx")
    frequency = theta_base ** (-2.0 * jnp.arange(HEAD_DIM // 2, dtype=f32) / HEAD_DIM)
    angles = position_ids.astype(f32)[None, :] * frequency[:, None]
    cosine, sine = jnp.cos(angles), jnp.sin(angles)
    base = (here * tokens).astype(jnp.int32).reshape(1)

    full_block, band_block, rim, meta = prepare(
        base, banded_keys, banded_values, full_keys, full_values, cosine, sine, segment_ids.reshape(1, tokens)
    )
    far = [shifted_by(full_block, d * PLANE) for d in range(1, REACH // PLANE + 1)]
    rim = shifted_by(rim, 1)
    fqt, bqt, *state = own(group, full_queries, banded_queries, cosine, sine, full_block, meta)
    banded_out = band(group, bqt, band_block, rim, meta)

    def column(bit):
        ahead = (here & bit) == 0
        return jnp.stack(far[:-1] + [jnp.where(ahead, full_block, far[-1])])

    by_x = swapped(column(1), 1)
    by_y = swapped(column(2), 2)
    state = remote(group, fqt, far, meta, state)
    diag_x = swapped(by_y[1:], 1)
    diag_y = swapped(by_x[0], 2)
    state = remote(group, fqt, [by_x, by_y], meta, state)
    part = last(group, fqt, [diag_x, diag_y], meta, state, out_weight)

    sides = lax.axis_size("head")
    if sides != 2:
        return banded_out, lax.psum_scatter(part, "head", scatter_dimension=0, tiled=True)
    rows = tokens // 2
    side = lax.axis_index("head")
    mine = lax.dynamic_slice_in_dim(part, side * rows, rows, 0)
    theirs = lax.dynamic_slice_in_dim(part, (1 - side) * rows, rows, 0)
    theirs = lax.ppermute(theirs, "head", [(0, 1), (1, 0)])
    projected = (mine.astype(f32) + theirs.astype(f32)).astype(bf16)
    return banded_out, projected


def solution(mesh):
    return jax.shard_map(
        body,
        mesh=mesh,
        in_specs=(
            P("ctx", "head"),
            P("ctx", "head"),
            P("ctx", "head"),
            P("ctx", "head"),
            P("ctx", "head"),
            P("ctx", "head"),
            P("ctx"),
            P("ctx"),
            P("head", None),
        ),
        out_specs=(P("ctx", "head"), P(("ctx", "head"), None)),
        check_vma=False,
    )
```

```python
import functools

import jax
import jax.numpy as jnp
from jax import lax
from jax.experimental import pallas as pl
from jax.experimental.pallas import tpu as pltpu
from jax.sharding import PartitionSpec as P

HEAD_DIM = 64
WINDOW = 128
REACH = 12
PLANE = 4
PAD = 16
AUG = 2 * HEAD_DIM

theta_base = 150000.0
neg_fill = -1e30
to_log2 = HEAD_DIM ** (-0.5) * 1.4426950408889634

f32 = jnp.float32
bf16 = jnp.bfloat16
VM = pl.BlockSpec(memory_space=pltpu.VMEM)


def al(start, size):
    return pl.ds(pl.multiple_of(start, size), size)


def rotate_rows(rows, cosine, sine_term):
    half = HEAD_DIM // 2
    out = []
    for at in range(0, rows.shape[0], HEAD_DIM):
        leading = rows[at : at + half]
        trailing = rows[at + half : at + HEAD_DIM]
        out.append(leading * cosine - trailing * sine_term)
        out.append(trailing * cosine + leading * sine_term)
    return jnp.concatenate(out, axis=0).astype(bf16)


def prepare_kernel(base, bk, bv, fk, fv, cosine, sine, seg, full_block, band_block, rim, meta):
    tokens, width = fk.shape
    cos, sin = cosine[...], sine[...]
    ids = seg[...]
    shifted = ids + 1
    row = lax.broadcasted_iota(jnp.int32, (PAD, tokens), 0)
    high = jnp.broadcast_to(shifted >> 7, (PAD, tokens))
    low = jnp.broadcast_to(shifted & 127, (PAD, tokens))
    id_rows = jnp.where(row == 0, high, jnp.where(row == 1, low, 0)).astype(f32).astype(bf16)
    for keys, values, block in ((fk, fv, full_block), (bk, bv, band_block)):
        block[0:width, :] = rotate_rows(keys[...].astype(f32).T, cos, sin)
        block[width : width + PAD, :] = id_rows
        block[width + PAD :, :] = values[...].astype(f32).T.astype(bf16)
    rim[...] = band_block[:, tokens - WINDOW :]
    ids_f = ids.astype(f32)
    across = jnp.broadcast_to(ids_f, (tokens, tokens))
    down = across.T
    before = jnp.max(jnp.where(down < across, down, -1.0), axis=0, keepdims=True)
    first = before < 0.0
    begin = jnp.where(first, 0.0, before + 1.0 - base[0].astype(f32))
    mrow = lax.broadcasted_iota(jnp.int32, (8, tokens), 0)
    meta[...] = jnp.where(
        mrow == 0,
        jnp.broadcast_to(begin, (8, tokens)),
        jnp.where(mrow == 1, jnp.broadcast_to(first.astype(f32), (8, tokens)), jnp.broadcast_to(ids_f + 1.0, (8, tokens))),
    )


def prepare(base, bk, bv, fk, fv, cosine, sine, seg):
    tokens, width = fk.shape
    height = 2 * width + PAD
    return pl.pallas_call(
        prepare_kernel,
        out_shape=(
            jax.ShapeDtypeStruct((height, tokens), bf16),
            jax.ShapeDtypeStruct((height, tokens), bf16),
            jax.ShapeDtypeStruct((height, WINDOW), bf16),
            jax.ShapeDtypeStruct((8, tokens), f32),
        ),
        in_specs=[pl.BlockSpec(memory_space=pltpu.SMEM)] + [VM] * 7,
        out_specs=(VM,) * 4,
        compiler_params=pltpu.CompilerParams(vmem_limit_bytes=16 << 20),
        name="prepare",
    )(base, bk, bv, fk, fv, cosine, sine, seg)


def two_deep(units, scores, outs, s0, s1, x0, x1):
    scores(0, s0, x0)

    def pair(i, _):
        u = 2 * i
        scores(u + 1, s1, x1)
        outs(u, s0, x0)
        scores(jnp.minimum(u + 2, units - 1), s0, x0)
        outs(u + 1, s1, x1)
        return 0

    lax.fori_loop(0, units // 2, pair, 0)


def column_peak(s):
    return jnp.broadcast_to(jnp.max(s, axis=0, keepdims=True), (8, s.shape[1]))


def transposed_keys(rows, extra):
    return jnp.concatenate([rows.astype(f32), extra], axis=0).T.astype(bf16)


def ids_of(rows):
    rows = rows.astype(f32)
    return rows[0:1] * 128.0 + rows[1:2]


def mask_rows(ids, own_id):
    bar = jnp.where(ids < own_id, neg_fill, 0.0)
    row = lax.broadcasted_iota(jnp.int32, (HEAD_DIM, ids.shape[1]), 0)
    return jnp.where(row == 0, jnp.broadcast_to(bar, row.shape), jnp.where(row == 1, 1.0, 0.0))


def rotate_into(src, dst, cos, sin):
    wide = src.shape[1]
    step = min(wide, 4 * AUG)
    for at in range(0, wide, step):
        dst[at : at + step, :] = rotate_rows(src[:, at : at + step].astype(f32).T, cos, sin)


def own_kernel(group, fq, cosine, sine, block, meta, fqt, peak, total, accum, keys, bias, s0, s1, x0, x1):
    tokens, wide = fq.shape
    width = wide // group
    kv = width // HEAD_DIM
    rotate_into(fq, fqt, cosine[...], sine[...])
    zero = jnp.zeros((HEAD_DIM, tokens), f32)
    for h in range(kv):
        keys[h * tokens : (h + 1) * tokens, :] = transposed_keys(block[h * HEAD_DIM : (h + 1) * HEAD_DIM, :], zero)
    begin = jnp.broadcast_to(meta[0:1, :], (tokens, tokens)).astype(jnp.int32)
    r = lax.broadcasted_iota(jnp.int32, (tokens, tokens), 0)
    t = lax.broadcasted_iota(jnp.int32, (tokens, tokens), 1)
    bias[...] = jnp.where((r >= begin) & (r <= t), 0.0, neg_fill)
    several = s0.shape[0] // tokens

    def scores(u, buf, x):
        h = u * several // group
        k = keys[al(h * tokens, tokens), :][:, :HEAD_DIM]
        for g in range(several):
            q = fqt[al((u * several + g) * HEAD_DIM, HEAD_DIM), :]
            s = jnp.dot(k, q, preferred_element_type=f32) + bias[...]
            buf[g * tokens : (g + 1) * tokens, :] = s
            x[8 * g : 8 * g + 8, :] = column_peak(s)

    def outs(u, buf, x):
        h = u * several // group
        v = block[pl.ds(pl.multiple_of(width + PAD + h * HEAD_DIM, PAD), HEAD_DIM), :]
        for g in range(several):
            at = u * several + g
            m = x[8 * g : 8 * g + 1, :]
            p = jnp.exp2(buf[g * tokens : (g + 1) * tokens, :] * to_log2 - m * to_log2)
            peak[pl.ds(at, 1), :] = m
            total[pl.ds(at, 1), :] = jnp.sum(p, axis=0, keepdims=True)
            accum[al(at * HEAD_DIM, HEAD_DIM), :] = jnp.dot(v, p.astype(bf16), preferred_element_type=f32)

    two_deep(wide // HEAD_DIM // several, scores, outs, s0, s1, x0, x1)


def own(group, fq, cosine, sine, block, meta):
    tokens, wide = fq.shape
    heads = wide // HEAD_DIM
    kv = heads // group
    several = 4
    return pl.pallas_call(
        functools.partial(own_kernel, group),
        out_shape=(
            jax.ShapeDtypeStruct((wide, tokens), bf16),
            jax.ShapeDtypeStruct((heads, tokens), f32),
            jax.ShapeDtypeStruct((heads, tokens), f32),
            jax.ShapeDtypeStruct((wide, tokens), f32),
        ),
        in_specs=[VM] * 5,
        out_specs=(VM,) * 4,
        scratch_shapes=[
            pltpu.VMEM((kv * tokens, AUG), bf16),
            pltpu.VMEM((tokens, tokens), f32),
            pltpu.VMEM((several * tokens, tokens), f32),
            pltpu.VMEM((several * tokens, tokens), f32),
            pltpu.VMEM((8 * several, tokens), f32),
            pltpu.VMEM((8 * several, tokens), f32),
        ],
        compiler_params=pltpu.CompilerParams(vmem_limit_bytes=24 << 20),
        cost_estimate=pl.CostEstimate(
            flops=4 * heads * tokens * tokens * HEAD_DIM * 4, transcendentals=heads * tokens * tokens, bytes_accessed=12 * wide * tokens
        ),
        name="own",
    )(fq, cosine, sine, block, meta)


def band_kernel(group, bq, cosine, sine, block, rim, meta, out, bqt, keys, vals, bias, s0, s1, x0, x1):
    tokens, wide = bq.shape
    width = wide // group
    kv = width // HEAD_DIM
    span = tokens + WINDOW
    tile = 2 * WINDOW
    rotate_into(bq, bqt, cosine[...], sine[...])
    zero = jnp.zeros((HEAD_DIM, tokens), f32)
    for h in range(kv):
        rows = slice(h * HEAD_DIM, (h + 1) * HEAD_DIM)
        keys[h * span : h * span + WINDOW, :] = transposed_keys(rim[rows, :], zero[:, :WINDOW])
        keys[h * span + WINDOW : (h + 1) * span, :] = transposed_keys(block[rows, :], zero)
    vals[:, :WINDOW] = rim[width + PAD :, :]
    vals[:, WINDOW:] = block[width + PAD :, :]
    own_id = jnp.min(meta[2:3, :])
    barred = jnp.sum((ids_of(rim[width : width + PAD, :]) < own_id).astype(f32))
    begin = meta[0:1, :]
    first = meta[1:2, :]
    r = lax.broadcasted_iota(jnp.int32, (tile, tile), 0).astype(f32)
    t = (lax.broadcasted_iota(jnp.int32, (1, tile), 1) & (WINDOW - 1)).astype(f32)
    halves = tokens // WINDOW
    for half in range(halves):
        lo = begin + float(WINDOW - half * WINDOW)
        if half == 0:
            lo = jnp.where(first > 0.0, barred, lo)
        lo = lo[:, half * WINDOW : (half + 1) * WINDOW]
        low = jnp.maximum(jnp.concatenate([lo, lo], axis=1), t + 1.0)
        bias[half * tile : (half + 1) * tile, :] = jnp.where((r >= low) & (r <= t + WINDOW), 0.0, neg_fill)
    pairs = group // 2
    several = s0.shape[0] // tile // halves

    def scores(u, buf, x):
        h = u * several // pairs
        for half in range(halves):
            k = keys[pl.ds(pl.multiple_of(h * span + half * WINDOW, WINDOW), tile), :][:, :HEAD_DIM]
            for g in range(several):
                q = bqt[al((u * several + g) * AUG, AUG), :][:, half * WINDOW : (half + 1) * WINDOW]
                q = jnp.concatenate([q[:HEAD_DIM], q[HEAD_DIM:]], axis=1)
                s = jnp.dot(k, q, preferred_element_type=f32) + bias[half * tile : (half + 1) * tile, :]
                at = half * several + g
                buf[at * tile : (at + 1) * tile, :] = s
                x[8 * at : 8 * at + 8, :] = column_peak(s)

    def outs(u, buf, x):
        h = u * several // pairs
        for half in range(halves):
            v = vals[al(h * HEAD_DIM, HEAD_DIM), half * WINDOW : half * WINDOW + tile]
            for g in range(several):
                at = half * several + g
                m = x[8 * at : 8 * at + 1, :]
                p = jnp.exp2(buf[at * tile : (at + 1) * tile, :] * to_log2 - m * to_log2)
                total = jnp.sum(p, axis=0, keepdims=True)
                o = jnp.dot(v, p.astype(bf16), preferred_element_type=f32) / total
                o = jnp.concatenate([o[:, :WINDOW], o[:, WINDOW:]], axis=0)
                out[half * WINDOW : (half + 1) * WINDOW, al((u * several + g) * AUG, AUG)] = o.T.astype(bf16)

    two_deep(kv * pairs // several, scores, outs, s0, s1, x0, x1)


def band(group, bq, cosine, sine, block, rim, meta):
    tokens, wide = bq.shape
    kv = wide // group // HEAD_DIM
    span = tokens + WINDOW
    several = 2
    tiles = several * (tokens // WINDOW)
    return pl.pallas_call(
        functools.partial(band_kernel, group),
        out_shape=jax.ShapeDtypeStruct((tokens, wide), bf16),
        in_specs=[VM] * 6,
        out_specs=VM,
        scratch_shapes=[
            pltpu.VMEM((wide, tokens), bf16),
            pltpu.VMEM((kv * span, AUG), bf16),
            pltpu.VMEM((kv * HEAD_DIM, span), bf16),
            pltpu.VMEM((tokens // WINDOW * 2 * WINDOW, 2 * WINDOW), f32),
            pltpu.VMEM((tiles * 2 * WINDOW, 2 * WINDOW), f32),
            pltpu.VMEM((tiles * 2 * WINDOW, 2 * WINDOW), f32),
            pltpu.VMEM((8 * tiles, 2 * WINDOW), f32),
            pltpu.VMEM((8 * tiles, 2 * WINDOW), f32),
        ],
        compiler_params=pltpu.CompilerParams(vmem_limit_bytes=24 << 20),
        cost_estimate=pl.CostEstimate(
            flops=4 * wide * tokens * 2 * WINDOW * 4, transcendentals=wide // HEAD_DIM * tokens * 2 * WINDOW, bytes_accessed=4 * wide * tokens
        ),
        name="band",
    )(bq, cosine, sine, block, rim, meta)


def remote_update(group, fqt, shards, meta, state_in, state_out, keys, s0, s1, x0, x1):
    wide, tokens = fqt.shape
    width = wide // group
    kv = width // HEAD_DIM
    span = len(shards) * tokens
    peak_in, total_in, accum_in = state_in
    peak, total, accum = state_out
    own_id = jnp.min(meta[2:3, :])
    for b, (kref, krow, _, _) in enumerate(shards):
        extra = mask_rows(ids_of(kref[krow + width : krow + width + PAD, :]), own_id)
        for h in range(kv):
            rows = kref[krow + h * HEAD_DIM : krow + (h + 1) * HEAD_DIM, :]
            keys[h * span + b * tokens : h * span + (b + 1) * tokens, :] = transposed_keys(rows, extra)
    row = lax.broadcasted_iota(jnp.int32, (HEAD_DIM, tokens), 0)
    other = jnp.where(meta[1:2, :] > 0.0, 0.0, neg_fill)
    query_rows = jnp.where(row == 0, 1.0, jnp.where(row == 1, jnp.broadcast_to(other, row.shape), 0.0)).astype(bf16)

    several = s0.shape[0] // span

    def scores(u, buf, x):
        h = u * several // group
        k = keys[al(h * span, span), :]
        for g in range(several):
            q = jnp.concatenate([fqt[al((u * several + g) * HEAD_DIM, HEAD_DIM), :], query_rows], axis=0)
            s = jnp.dot(k, q, preferred_element_type=f32)
            buf[g * span : (g + 1) * span, :] = s
            x[8 * g : 8 * g + 8, :] = column_peak(s)

    def outs(u, buf, x):
        h = u * several // group
        for g in range(several):
            at = u * several + g
            old = peak_in[pl.ds(at, 1), :]
            m = jnp.maximum(old, x[8 * g : 8 * g + 1, :])
            scaled = m * to_log2
            factor = jnp.exp2(old * to_log2 - scaled)
            peak[pl.ds(at, 1), :] = m
            rows = al(at * HEAD_DIM, HEAD_DIM)
            t = total_in[pl.ds(at, 1), :] * factor
            a = accum_in[rows, :] * factor
            for b, (_, _, vref, vrow) in enumerate(shards):
                p = jnp.exp2(buf[g * span + b * tokens : g * span + (b + 1) * tokens, :] * to_log2 - scaled)
                t = t + jnp.sum(p, axis=0, keepdims=True)
                v = vref[pl.ds(pl.multiple_of(vrow + h * HEAD_DIM, PAD), HEAD_DIM), :]
                a = a + jnp.dot(v, p.astype(bf16), preferred_element_type=f32)
            total[pl.ds(at, 1), :] = t
            accum[rows, :] = a

    two_deep(wide // HEAD_DIM // several, scores, outs, s0, s1, x0, x1)


def remote_scratch(kv, tokens, count):
    span = count * tokens
    several = 4 if count == 1 else 2 if count == 2 else 1
    return [
        pltpu.VMEM((kv * span, AUG), bf16),
        pltpu.VMEM((several * span, tokens), f32),
        pltpu.VMEM((several * span, tokens), f32),
        pltpu.VMEM((8 * several, tokens), f32),
        pltpu.VMEM((8 * several, tokens), f32),
    ]


def placed(shards, refs):
    return [(refs[ka], kr, refs[va], vr) for ka, kr, va, vr in shards]


def remote_kernel(group, shards, n, fqt, *refs):
    meta, peak_in, total_in, accum_in, peak, total, accum = refs[n : n + 7]
    remote_update(group, fqt, placed(shards, refs), meta, (peak_in, total_in, accum_in), (peak, total, accum), *refs[n + 7 :])


def remote(group, fqt, arrays, shards, meta, state):
    wide, tokens = fqt.shape
    heads = wide // HEAD_DIM
    count = len(shards)
    n = len(arrays)
    return pl.pallas_call(
        functools.partial(remote_kernel, group, shards, n),
        out_shape=tuple(jax.ShapeDtypeStruct(x.shape, x.dtype) for x in state),
        in_specs=[VM] * (n + 5),
        out_specs=(VM,) * 3,
        scratch_shapes=remote_scratch(heads // group, tokens, count),
        input_output_aliases={n + 2 + i: i for i in range(3)},
        compiler_params=pltpu.CompilerParams(vmem_limit_bytes=24 << 20),
        cost_estimate=pl.CostEstimate(
            flops=4 * wide * tokens * tokens * count * 4, transcendentals=heads * tokens * tokens * count, bytes_accessed=20 * wide * tokens
        ),
        name="remote",
    )(fqt, *arrays, meta, *state)


def last_kernel(group, shards, n, side, fqt, *refs):
    meta, peak_in, total_in, accum_in, weight, mine, theirs = refs[n : n + 7]
    keys, s0, s1, x0, x1, peak, total, accum, mixed, held, sem = refs[n + 7 :]
    copy = pltpu.make_async_copy(weight, held, sem)
    copy.start()
    remote_update(group, fqt, placed(shards, refs), meta, (peak_in, total_in, accum_in), (peak, total, accum), keys, s0, s1, x0, x1)
    wide, tokens = fqt.shape
    rows = tokens // 2
    for u in range(wide // HEAD_DIM):
        at = slice(u * HEAD_DIM, (u + 1) * HEAD_DIM)
        mixed[at, :] = (accum[at, :] / total[u : u + 1, :]).astype(bf16)
    copy.wait()
    first = side[0] == 0
    columns = held.shape[0]
    step = 4 * AUG
    for at in range(0, columns, step):
        size = min(step, columns - at)
        part = jnp.dot(held[at : at + size, :], mixed[...], preferred_element_type=f32).astype(bf16)
        low, high = part[:, :rows], part[:, rows:]
        mine[at : at + size, :] = jnp.where(first, low, high)
        theirs[at : at + size, :] = jnp.where(first, high, low)


def last(group, side, fqt, arrays, shards, meta, state, weight):
    wide, tokens = fqt.shape
    heads = wide // HEAD_DIM
    count = len(shards)
    n = len(arrays)
    return pl.pallas_call(
        functools.partial(last_kernel, group, shards, n),
        out_shape=(jax.ShapeDtypeStruct((weight.shape[0], tokens // 2), bf16),) * 2,
        in_specs=[pl.BlockSpec(memory_space=pltpu.SMEM)] + [VM] * (n + 5) + [pl.BlockSpec(memory_space=pl.ANY)],
        out_specs=(VM, VM),
        scratch_shapes=remote_scratch(heads // group, tokens, count)
        + [
            pltpu.VMEM((heads, tokens), f32),
            pltpu.VMEM((heads, tokens), f32),
            pltpu.VMEM((wide, tokens), f32),
            pltpu.VMEM((wide, tokens), bf16),
            pltpu.VMEM(weight.shape, bf16),
            pltpu.SemaphoreType.DMA,
        ],
        compiler_params=pltpu.CompilerParams(vmem_limit_bytes=40 << 20),
        cost_estimate=pl.CostEstimate(
            flops=4 * wide * tokens * tokens * count * 4, transcendentals=heads * tokens * tokens * count, bytes_accessed=20 * wide * tokens
        ),
        name="last",
    )(side, fqt, *arrays, meta, *state, weight)


def shifted_by(block, distance):
    size = lax.axis_size("ctx")
    return lax.ppermute(block, "ctx", [(i, i + distance) for i in range(size - distance)])


def swapped(block, bit):
    size = lax.axis_size("ctx")
    return lax.ppermute(block, "ctx", [(i, i ^ bit) for i in range(size)])


def body(banded_queries, banded_keys, banded_values, full_queries, full_keys, full_values, segment_ids, position_ids, out_weight):
    tokens = segment_ids.shape[0]
    width = full_keys.shape[1]
    height = 2 * width + PAD
    vrow = width + PAD
    group = banded_queries.shape[1] // banded_keys.shape[1]
    here = lax.axis_index("ctx")
    frequency = theta_base ** (-2.0 * jnp.arange(HEAD_DIM // 2, dtype=f32) / HEAD_DIM)
    angles = position_ids.astype(f32)[None, :] * frequency[:, None]
    cosine, sine = jnp.cos(angles), jnp.sin(angles)
    base = (here * tokens).astype(jnp.int32).reshape(1)
    side = lax.axis_index("head")

    block, band_block, rim, meta = prepare(
        base, banded_keys, banded_values, full_keys, full_values, cosine, sine, segment_ids.reshape(1, tokens)
    )
    z1 = shifted_by(block, PLANE)
    rim = shifted_by(rim, 1)
    fqt, *state = own(group, full_queries, cosine, sine, block, meta)
    z1, rim, block, state = lax.optimization_barrier((z1, rim, block, state))

    x1 = swapped(z1, 1)
    y1 = swapped(z1, 2)
    z2 = shifted_by(block, 2 * PLANE)
    z3 = shifted_by(block, 3 * PLANE)
    banded_out = band(group, banded_queries, cosine, sine, band_block, rim, meta)
    state = remote(group, fqt, [z1], ((0, 0, 0, vrow),), meta, state)
    z2, z3, x1, y1, block, state, banded_out = lax.optimization_barrier((z2, z3, x1, y1, block, state, banded_out))

    def farthest(bit):
        return jnp.where((here & bit) == 0, block, z3)

    x2 = swapped(jnp.concatenate([z2, farthest(1), y1[:vrow]]), 1)
    y2 = swapped(jnp.concatenate([z2, farthest(2), x1[vrow:]]), 2)
    state = remote(
        group, fqt, [x1, y1, z2, z3], tuple((a, 0, a, vrow) for a in range(4)), meta, state
    )
    x2, y2, state = lax.optimization_barrier((x2, y2, state))

    dx = swapped(y2[height : 2 * height], 1)
    dy = swapped(x2[:height], 2)
    state = remote(
        group,
        fqt,
        [x2, y2],
        ((0, 0, 0, vrow), (0, height, 0, height + vrow), (1, 0, 1, vrow), (1, height, 1, height + vrow), (0, 2 * height, 1, 2 * height)),
        meta,
        state,
    )
    dx, dy, state = lax.optimization_barrier((dx, dy, state))
    mine, theirs = last(
        group, side.reshape(1).astype(jnp.int32), fqt, [dx, dy], ((0, 0, 0, vrow), (1, 0, 1, vrow)), meta, state, out_weight.T
    )

    sides = lax.axis_size("head")
    if sides != 2:
        part = jnp.concatenate([jnp.where(side == 0, mine, theirs), jnp.where(side == 0, theirs, mine)], axis=1).T
        return banded_out, lax.psum_scatter(part, "head", scatter_dimension=0, tiled=True)
    theirs = lax.ppermute(theirs, "head", [(0, 1), (1, 0)])
    projected = (mine.astype(f32) + theirs.astype(f32)).astype(bf16)
    return banded_out, projected.T


def solution(mesh):
    return jax.shard_map(
        body,
        mesh=mesh,
        in_specs=(
            P("ctx", "head"),
            P("ctx", "head"),
            P("ctx", "head"),
            P("ctx", "head"),
            P("ctx", "head"),
            P("ctx", "head"),
            P("ctx"),
            P("ctx"),
            P("head", None),
        ),
        out_specs=(P("ctx", "head"), P(("ctx", "head"), None)),
        check_vma=False,
    )
```

```python
import functools

import jax
import jax.numpy as jnp
from jax import lax
from jax.experimental import pallas as pl
from jax.experimental.pallas import tpu as pltpu
from jax.sharding import PartitionSpec as P

HEAD_DIM = 64
WINDOW = 128
REACH = 12
PLANE = 4
PAD = 16
AUG = 2 * HEAD_DIM

theta_base = 150000.0
neg_fill = -1e30
to_log2 = HEAD_DIM ** (-0.5) * 1.4426950408889634

f32 = jnp.float32
bf16 = jnp.bfloat16
VM = pl.BlockSpec(memory_space=pltpu.VMEM)


def al(start, size):
    return pl.ds(pl.multiple_of(start, size), size)


def rotate_rows(rows, cosine, sine_term):
    half = HEAD_DIM // 2
    out = []
    for at in range(0, rows.shape[0], HEAD_DIM):
        leading = rows[at : at + half]
        trailing = rows[at + half : at + HEAD_DIM]
        out.append(leading * cosine - trailing * sine_term)
        out.append(trailing * cosine + leading * sine_term)
    return jnp.concatenate(out, axis=0).astype(bf16)


def write_block(block, rows, id_rows, cos, sin):
    width = rows.shape[0] // 2
    block[0:width, :] = rotate_rows(rows[:width], cos, sin)
    block[width : width + PAD, :] = id_rows
    block[width + PAD :, :] = rows[width:].astype(bf16)


def prepare_kernel(base, frequency, kv, ids_pos, block, band_block, rim, meta, cosine, sine):
    tokens = kv.shape[0]
    angles = ids_pos[1:2, :].astype(f32) * frequency[...]
    cos, sin = jnp.cos(angles), jnp.sin(angles)
    cosine[...] = cos
    sine[...] = sin
    ids = ids_pos[0:1, :]
    shifted = ids + 1
    row = lax.broadcasted_iota(jnp.int32, (PAD, tokens), 0)
    high = jnp.broadcast_to(shifted >> 7, (PAD, tokens))
    low = jnp.broadcast_to(shifted & 127, (PAD, tokens))
    id_rows = jnp.where(row == 0, high, jnp.where(row == 1, low, 0)).astype(f32).astype(bf16)
    half = kv.shape[1] // 2
    write_block(block, kv[:, :half].astype(f32).T, id_rows, cos, sin)
    write_block(band_block, kv[:, half:].astype(f32).T, id_rows, cos, sin)
    rim[...] = band_block[:, tokens - WINDOW :]
    ids_f = ids.astype(f32)
    across = jnp.broadcast_to(ids_f, (tokens, tokens))
    down = across.T
    before = jnp.max(jnp.where(down < across, down, -1.0), axis=0, keepdims=True)
    first = before < 0.0
    begin = jnp.where(first, 0.0, before + 1.0 - base[0].astype(f32))
    mrow = lax.broadcasted_iota(jnp.int32, (8, tokens), 0)
    meta[...] = jnp.where(
        mrow == 0,
        jnp.broadcast_to(begin, (8, tokens)),
        jnp.where(mrow == 1, jnp.broadcast_to(first.astype(f32), (8, tokens)), jnp.broadcast_to(ids_f + 1.0, (8, tokens))),
    )


def prepare(base, frequency, kv, ids_pos):
    tokens, every = kv.shape
    height = every // 2 + PAD
    half = HEAD_DIM // 2
    return pl.pallas_call(
        prepare_kernel,
        out_shape=(
            jax.ShapeDtypeStruct((height, tokens), bf16),
            jax.ShapeDtypeStruct((height, tokens), bf16),
            jax.ShapeDtypeStruct((height, WINDOW), bf16),
            jax.ShapeDtypeStruct((8, tokens), f32),
            jax.ShapeDtypeStruct((half, tokens), f32),
            jax.ShapeDtypeStruct((half, tokens), f32),
        ),
        in_specs=[pl.BlockSpec(memory_space=pltpu.SMEM)] + [VM] * 3,
        out_specs=(VM,) * 6,
        compiler_params=pltpu.CompilerParams(vmem_limit_bytes=8 << 20),
        name="prepare",
    )(base, frequency, kv, ids_pos)


def two_deep(units, scores, outs, s0, s1, x0, x1):
    scores(0, s0, x0)

    def pair(i, _):
        u = 2 * i
        scores(u + 1, s1, x1)
        outs(u, s0, x0)
        scores(jnp.minimum(u + 2, units - 1), s0, x0)
        outs(u + 1, s1, x1)
        return 0

    lax.fori_loop(0, units // 2, pair, 0)


def column_peak(s):
    return jnp.broadcast_to(jnp.max(s, axis=0, keepdims=True), (8, s.shape[1]))


def transposed_keys(rows, extra):
    return jnp.concatenate([rows.astype(f32), extra], axis=0).T.astype(bf16)


def ids_of(rows):
    rows = rows.astype(f32)
    return rows[0:1] * 128.0 + rows[1:2]


def mask_rows(ids, own_id):
    bar = jnp.where(ids < own_id, neg_fill, 0.0)
    row = lax.broadcasted_iota(jnp.int32, (HEAD_DIM, ids.shape[1]), 0)
    return jnp.where(row == 0, jnp.broadcast_to(bar, row.shape), jnp.where(row == 1, 1.0, 0.0))


def rotate_into(src, dst, cos, sin):
    wide = src.shape[1]
    step = min(wide, 4 * AUG)
    for at in range(0, wide, step):
        dst[at : at + step, :] = rotate_rows(src[:, at : at + step].astype(f32).T, cos, sin)


def own_kernel(group, fq, cosine, sine, block, meta, fqt, peak, total, accum, keys, bias, s0, s1, x0, x1):
    tokens, wide = fq.shape
    width = wide // group
    kv = width // HEAD_DIM
    rotate_into(fq, fqt, cosine[...], sine[...])
    zero = jnp.zeros((HEAD_DIM, tokens), f32)
    for h in range(kv):
        keys[h * tokens : (h + 1) * tokens, :] = transposed_keys(block[h * HEAD_DIM : (h + 1) * HEAD_DIM, :], zero)
    begin = jnp.broadcast_to(meta[0:1, :], (tokens, tokens)).astype(jnp.int32)
    r = lax.broadcasted_iota(jnp.int32, (tokens, tokens), 0)
    t = lax.broadcasted_iota(jnp.int32, (tokens, tokens), 1)
    bias[...] = jnp.where((r >= begin) & (r <= t), 0.0, neg_fill)
    several = s0.shape[0] // tokens

    def scores(u, buf, x):
        h = u * several // group
        k = keys[al(h * tokens, tokens), :][:, :HEAD_DIM]
        for g in range(several):
            q = fqt[al((u * several + g) * HEAD_DIM, HEAD_DIM), :]
            s = jnp.dot(k, q, preferred_element_type=f32) + bias[...]
            buf[g * tokens : (g + 1) * tokens, :] = s
            x[8 * g : 8 * g + 8, :] = column_peak(s)

    def outs(u, buf, x):
        h = u * several // group
        v = block[pl.ds(pl.multiple_of(width + PAD + h * HEAD_DIM, PAD), HEAD_DIM), :]
        for g in range(several):
            at = u * several + g
            m = x[8 * g : 8 * g + 1, :]
            p = jnp.exp2(buf[g * tokens : (g + 1) * tokens, :] * to_log2 - m * to_log2)
            peak[pl.ds(at, 1), :] = m
            total[pl.ds(at, 1), :] = jnp.sum(p, axis=0, keepdims=True)
            accum[al(at * HEAD_DIM, HEAD_DIM), :] = jnp.dot(v, p.astype(bf16), preferred_element_type=f32)

    two_deep(wide // HEAD_DIM // several, scores, outs, s0, s1, x0, x1)


def own(group, fq, cosine, sine, block, meta):
    tokens, wide = fq.shape
    heads = wide // HEAD_DIM
    kv = heads // group
    several = 4
    return pl.pallas_call(
        functools.partial(own_kernel, group),
        out_shape=(
            jax.ShapeDtypeStruct((wide, tokens), bf16),
            jax.ShapeDtypeStruct((heads, tokens), f32),
            jax.ShapeDtypeStruct((heads, tokens), f32),
            jax.ShapeDtypeStruct((wide, tokens), f32),
        ),
        in_specs=[VM] * 5,
        out_specs=(VM,) * 4,
        scratch_shapes=[
            pltpu.VMEM((kv * tokens, AUG), bf16),
            pltpu.VMEM((tokens, tokens), f32),
            pltpu.VMEM((several * tokens, tokens), f32),
            pltpu.VMEM((several * tokens, tokens), f32),
            pltpu.VMEM((8 * several, tokens), f32),
            pltpu.VMEM((8 * several, tokens), f32),
        ],
        compiler_params=pltpu.CompilerParams(vmem_limit_bytes=16 << 20),
        cost_estimate=pl.CostEstimate(
            flops=4 * heads * tokens * tokens * HEAD_DIM * 4, transcendentals=heads * tokens * tokens, bytes_accessed=12 * wide * tokens
        ),
        name="own",
    )(fq, cosine, sine, block, meta)


def band_kernel(group, bq, cosine, sine, block, rim, meta, out, bqt, keys, vals, bias, s0, s1, x0, x1):
    tokens, wide = bq.shape
    width = wide // group
    kv = width // HEAD_DIM
    span = tokens + WINDOW
    tile = 2 * WINDOW
    rotate_into(bq, bqt, cosine[...], sine[...])
    zero = jnp.zeros((HEAD_DIM, tokens), f32)
    for h in range(kv):
        rows = slice(h * HEAD_DIM, (h + 1) * HEAD_DIM)
        keys[h * span : h * span + WINDOW, :] = transposed_keys(rim[rows, :], zero[:, :WINDOW])
        keys[h * span + WINDOW : (h + 1) * span, :] = transposed_keys(block[rows, :], zero)
    vals[:, :WINDOW] = rim[width + PAD :, :]
    vals[:, WINDOW:] = block[width + PAD :, :]
    own_id = jnp.min(meta[2:3, :])
    barred = jnp.sum((ids_of(rim[width : width + PAD, :]) < own_id).astype(f32))
    begin = meta[0:1, :]
    first = meta[1:2, :]
    r = lax.broadcasted_iota(jnp.int32, (tile, tile), 0).astype(f32)
    t = (lax.broadcasted_iota(jnp.int32, (1, tile), 1) & (WINDOW - 1)).astype(f32)
    halves = tokens // WINDOW
    for half in range(halves):
        lo = begin + float(WINDOW - half * WINDOW)
        if half == 0:
            lo = jnp.where(first > 0.0, barred, lo)
        lo = lo[:, half * WINDOW : (half + 1) * WINDOW]
        low = jnp.maximum(jnp.concatenate([lo, lo], axis=1), t + 1.0)
        bias[half * tile : (half + 1) * tile, :] = jnp.where((r >= low) & (r <= t + WINDOW), 0.0, neg_fill)
    pairs = group // 2
    several = s0.shape[0] // tile // halves

    def scores(u, buf, x):
        h = u * several // pairs
        for half in range(halves):
            k = keys[pl.ds(pl.multiple_of(h * span + half * WINDOW, WINDOW), tile), :][:, :HEAD_DIM]
            for g in range(several):
                q = bqt[al((u * several + g) * AUG, AUG), :][:, half * WINDOW : (half + 1) * WINDOW]
                q = jnp.concatenate([q[:HEAD_DIM], q[HEAD_DIM:]], axis=1)
                s = jnp.dot(k, q, preferred_element_type=f32) + bias[half * tile : (half + 1) * tile, :]
                at = half * several + g
                buf[at * tile : (at + 1) * tile, :] = s
                x[8 * at : 8 * at + 8, :] = column_peak(s)

    def outs(u, buf, x):
        h = u * several // pairs
        for half in range(halves):
            v = vals[al(h * HEAD_DIM, HEAD_DIM), half * WINDOW : half * WINDOW + tile]
            for g in range(several):
                at = half * several + g
                m = x[8 * at : 8 * at + 1, :]
                p = jnp.exp2(buf[at * tile : (at + 1) * tile, :] * to_log2 - m * to_log2)
                total = jnp.sum(p, axis=0, keepdims=True)
                o = jnp.dot(v, p.astype(bf16), preferred_element_type=f32) / total
                o = jnp.concatenate([o[:, :WINDOW], o[:, WINDOW:]], axis=0)
                out[half * WINDOW : (half + 1) * WINDOW, al((u * several + g) * AUG, AUG)] = o.T.astype(bf16)

    two_deep(kv * pairs // several, scores, outs, s0, s1, x0, x1)


def band(group, bq, cosine, sine, block, rim, meta):
    tokens, wide = bq.shape
    kv = wide // group // HEAD_DIM
    span = tokens + WINDOW
    several = 2
    tiles = several * (tokens // WINDOW)
    return pl.pallas_call(
        functools.partial(band_kernel, group),
        out_shape=jax.ShapeDtypeStruct((tokens, wide), bf16),
        in_specs=[VM] * 6,
        out_specs=VM,
        scratch_shapes=[
            pltpu.VMEM((wide, tokens), bf16),
            pltpu.VMEM((kv * span, AUG), bf16),
            pltpu.VMEM((kv * HEAD_DIM, span), bf16),
            pltpu.VMEM((tokens // WINDOW * 2 * WINDOW, 2 * WINDOW), f32),
            pltpu.VMEM((tiles * 2 * WINDOW, 2 * WINDOW), f32),
            pltpu.VMEM((tiles * 2 * WINDOW, 2 * WINDOW), f32),
            pltpu.VMEM((8 * tiles, 2 * WINDOW), f32),
            pltpu.VMEM((8 * tiles, 2 * WINDOW), f32),
        ],
        compiler_params=pltpu.CompilerParams(vmem_limit_bytes=16 << 20),
        cost_estimate=pl.CostEstimate(
            flops=4 * wide * tokens * 2 * WINDOW * 4, transcendentals=wide // HEAD_DIM * tokens * 2 * WINDOW, bytes_accessed=4 * wide * tokens
        ),
        name="band",
    )(bq, cosine, sine, block, rim, meta)


def remote_update(group, fqt, shards, meta, state_in, state_out, keys, s0, s1, x0, x1):
    wide, tokens = fqt.shape
    width = wide // group
    kv = width // HEAD_DIM
    span = len(shards) * tokens
    peak_in, total_in, accum_in = state_in
    peak, total, accum = state_out
    own_id = jnp.min(meta[2:3, :])
    for b, (kref, krow, _, _) in enumerate(shards):
        extra = mask_rows(ids_of(kref[krow + width : krow + width + PAD, :]), own_id)
        for h in range(kv):
            rows = kref[krow + h * HEAD_DIM : krow + (h + 1) * HEAD_DIM, :]
            keys[h * span + b * tokens : h * span + (b + 1) * tokens, :] = transposed_keys(rows, extra)
    row = lax.broadcasted_iota(jnp.int32, (HEAD_DIM, tokens), 0)
    other = jnp.where(meta[1:2, :] > 0.0, 0.0, neg_fill)
    query_rows = jnp.where(row == 0, 1.0, jnp.where(row == 1, jnp.broadcast_to(other, row.shape), 0.0)).astype(bf16)

    several = s0.shape[0] // span

    def scores(u, buf, x):
        h = u * several // group
        k = keys[al(h * span, span), :]
        for g in range(several):
            q = jnp.concatenate([fqt[al((u * several + g) * HEAD_DIM, HEAD_DIM), :], query_rows], axis=0)
            s = jnp.dot(k, q, preferred_element_type=f32)
            buf[g * span : (g + 1) * span, :] = s
            x[8 * g : 8 * g + 8, :] = column_peak(s)

    def outs(u, buf, x):
        h = u * several // group
        for g in range(several):
            at = u * several + g
            old = peak_in[pl.ds(at, 1), :]
            m = jnp.maximum(old, x[8 * g : 8 * g + 1, :])
            scaled = m * to_log2
            factor = jnp.exp2(old * to_log2 - scaled)
            peak[pl.ds(at, 1), :] = m
            rows = al(at * HEAD_DIM, HEAD_DIM)
            t = total_in[pl.ds(at, 1), :] * factor
            a = accum_in[rows, :] * factor
            for b, (_, _, vref, vrow) in enumerate(shards):
                p = jnp.exp2(buf[g * span + b * tokens : g * span + (b + 1) * tokens, :] * to_log2 - scaled)
                t = t + jnp.sum(p, axis=0, keepdims=True)
                v = vref[pl.ds(pl.multiple_of(vrow + h * HEAD_DIM, PAD), HEAD_DIM), :]
                a = a + jnp.dot(v, p.astype(bf16), preferred_element_type=f32)
            total[pl.ds(at, 1), :] = t
            accum[rows, :] = a

    two_deep(wide // HEAD_DIM // several, scores, outs, s0, s1, x0, x1)


def remote_scratch(kv, tokens, count):
    span = count * tokens
    several = 4 if count < 3 else 2
    return [
        pltpu.VMEM((kv * span, AUG), bf16),
        pltpu.VMEM((several * span, tokens), f32),
        pltpu.VMEM((several * span, tokens), f32),
        pltpu.VMEM((8 * several, tokens), f32),
        pltpu.VMEM((8 * several, tokens), f32),
    ]


def placed(shards, refs):
    return [(refs[ka], kr, refs[va], vr) for ka, kr, va, vr in shards]


def remote_kernel(group, shards, n, fqt, *refs):
    meta, peak_in, total_in, accum_in, peak, total, accum = refs[n : n + 7]
    remote_update(group, fqt, placed(shards, refs), meta, (peak_in, total_in, accum_in), (peak, total, accum), *refs[n + 7 :])


def remote(group, fqt, arrays, shards, meta, state):
    wide, tokens = fqt.shape
    heads = wide // HEAD_DIM
    count = len(shards)
    n = len(arrays)
    return pl.pallas_call(
        functools.partial(remote_kernel, group, shards, n),
        out_shape=tuple(jax.ShapeDtypeStruct(x.shape, x.dtype) for x in state),
        in_specs=[VM] * (n + 5),
        out_specs=(VM,) * 3,
        scratch_shapes=remote_scratch(heads // group, tokens, count),
        input_output_aliases={n + 2 + i: i for i in range(3)},
        compiler_params=pltpu.CompilerParams(vmem_limit_bytes=16 << 20),
        cost_estimate=pl.CostEstimate(
            flops=4 * wide * tokens * tokens * count * 4, transcendentals=heads * tokens * tokens * count, bytes_accessed=20 * wide * tokens
        ),
        name="remote",
    )(fqt, *arrays, meta, *state)


def last_kernel(group, shards, n, side, fqt, *refs):
    meta, peak_in, total_in, accum_in, held, mine, theirs = refs[n : n + 7]
    keys, s0, s1, x0, x1, peak, total, accum, mixed = refs[n + 7 :]
    remote_update(group, fqt, placed(shards, refs), meta, (peak_in, total_in, accum_in), (peak, total, accum), keys, s0, s1, x0, x1)
    wide, tokens = fqt.shape
    rows = tokens // 2
    for u in range(wide // HEAD_DIM):
        at = slice(u * HEAD_DIM, (u + 1) * HEAD_DIM)
        mixed[at, :] = (accum[at, :] / total[u : u + 1, :]).astype(bf16)
    first = side[0] == 0
    columns = held.shape[0]
    step = 4 * AUG
    for at in range(0, columns, step):
        size = min(step, columns - at)
        part = jnp.dot(held[at : at + size, :], mixed[...], preferred_element_type=f32).astype(bf16)
        low, high = part[:, :rows], part[:, rows:]
        mine[at : at + size, :] = jnp.where(first, low, high)
        theirs[at : at + size, :] = jnp.where(first, high, low)


def last(group, side, fqt, arrays, shards, meta, state, weight):
    wide, tokens = fqt.shape
    heads = wide // HEAD_DIM
    count = len(shards)
    n = len(arrays)
    return pl.pallas_call(
        functools.partial(last_kernel, group, shards, n),
        out_shape=(jax.ShapeDtypeStruct((weight.shape[0], tokens // 2), bf16),) * 2,
        in_specs=[pl.BlockSpec(memory_space=pltpu.SMEM)] + [VM] * (n + 6),
        out_specs=(VM, VM),
        scratch_shapes=remote_scratch(heads // group, tokens, count)
        + [
            pltpu.VMEM((heads, tokens), f32),
            pltpu.VMEM((heads, tokens), f32),
            pltpu.VMEM((wide, tokens), f32),
            pltpu.VMEM((wide, tokens), bf16),
        ],
        compiler_params=pltpu.CompilerParams(vmem_limit_bytes=28 << 20),
        cost_estimate=pl.CostEstimate(
            flops=4 * wide * tokens * tokens * count * 4, transcendentals=heads * tokens * tokens * count, bytes_accessed=20 * wide * tokens
        ),
        name="last",
    )(side, fqt, *arrays, meta, *state, weight)


def shifted_by(block, distance):
    size = lax.axis_size("ctx")
    return lax.ppermute(block, "ctx", [(i, i + distance) for i in range(size - distance)])


def swapped(block, bit):
    size = lax.axis_size("ctx")
    return lax.ppermute(block, "ctx", [(i, i ^ bit) for i in range(size)])


def body(banded_queries, banded_keys, banded_values, full_queries, full_keys, full_values, segment_ids, position_ids, out_weight):
    tokens = segment_ids.shape[0]
    width = full_keys.shape[1]
    height = 2 * width + PAD
    vrow = width + PAD
    group = banded_queries.shape[1] // banded_keys.shape[1]
    here = lax.axis_index("ctx")
    half = HEAD_DIM // 2
    frequency = theta_base ** (-2.0 * jnp.arange(half, dtype=f32) / HEAD_DIM)
    frequency = jnp.broadcast_to(frequency[:, None], (half, tokens))
    base = (here * tokens).astype(jnp.int32).reshape(1)
    side = lax.axis_index("head")

    kv = jnp.concatenate([full_keys, full_values, banded_keys, banded_values], axis=1)
    ids_pos = jnp.stack([segment_ids, position_ids])
    block, band_kv, rim, meta, cosine, sine = prepare(base, frequency, kv, ids_pos)
    z1 = shifted_by(block, PLANE)
    rim = shifted_by(rim, 1)
    z2 = shifted_by(block, 2 * PLANE)
    z3 = shifted_by(block, 3 * PLANE)
    banded_out = band(group, banded_queries, cosine, sine, band_kv, rim, meta)
    block, banded_out = lax.optimization_barrier((block, banded_out))
    fqt, *state = own(group, full_queries, cosine, sine, block, meta)
    z1, state = lax.optimization_barrier((z1, state))

    x1 = swapped(z1, 1)
    y1 = swapped(z1, 2)
    state = remote(group, fqt, [z1], ((0, 0, 0, vrow),), meta, state)
    z2, z3, state = lax.optimization_barrier((z2, z3, state))

    def farthest(bit):
        return jnp.where((here & bit) == 0, block, z3)

    x2 = swapped(jnp.concatenate([z2, farthest(1)]), 1)
    y2 = swapped(jnp.concatenate([z2, farthest(2)]), 2)
    z2, z3, x1, y1 = lax.optimization_barrier((z2, z3, x1, y1))
    state = remote(group, fqt, [x1, y1, z2, z3], tuple((a, 0, a, vrow) for a in range(4)), meta, state)
    x2, y2, state = lax.optimization_barrier((x2, y2, state))

    dx = swapped(jnp.concatenate([y1[:vrow], y2[height:]]), 1)
    dy = swapped(jnp.concatenate([x1[vrow:], x2[:height]]), 2)
    state = remote(
        group,
        fqt,
        [x2, y2],
        ((0, 0, 0, vrow), (0, height, 0, height + vrow), (1, 0, 1, vrow), (1, height, 1, height + vrow)),
        meta,
        state,
    )
    dx, dy, state = lax.optimization_barrier((dx, dy, state))
    mine, theirs = last(
        group,
        side.reshape(1).astype(jnp.int32),
        fqt,
        [dx, dy],
        ((0, 0, 1, 0), (0, vrow, 0, 2 * vrow), (1, width, 1, width + vrow)),
        meta,
        state,
        out_weight.T,
    )

    sides = lax.axis_size("head")
    if sides != 2:
        part = jnp.concatenate([jnp.where(side == 0, mine, theirs), jnp.where(side == 0, theirs, mine)], axis=1).T
        return banded_out, lax.psum_scatter(part, "head", scatter_dimension=0, tiled=True)
    theirs = lax.ppermute(theirs, "head", [(0, 1), (1, 0)])
    projected = (mine.astype(f32) + theirs.astype(f32)).astype(bf16)
    return banded_out, projected.T


def solution(mesh):
    return jax.shard_map(
        body,
        mesh=mesh,
        in_specs=(
            P("ctx", "head"),
            P("ctx", "head"),
            P("ctx", "head"),
            P("ctx", "head"),
            P("ctx", "head"),
            P("ctx", "head"),
            P("ctx"),
            P("ctx"),
            P("head", None),
        ),
        out_specs=(P("ctx", "head"), P(("ctx", "head"), None)),
        check_vma=False,
    )
```

```python
import functools

import jax
import jax.numpy as jnp
from jax import lax
from jax.experimental import pallas as pl
from jax.experimental.pallas import tpu as pltpu
from jax.sharding import PartitionSpec as P

HEAD_DIM = 64
WINDOW = 128
REACH = 12
PLANE = 4
PAD = 16
AUG = 2 * HEAD_DIM

theta_base = 150000.0
neg_fill = -1e30
to_log2 = HEAD_DIM ** (-0.5) * 1.4426950408889634

f32 = jnp.float32
bf16 = jnp.bfloat16
VM = pl.BlockSpec(memory_space=pltpu.VMEM)
SM = pl.BlockSpec(memory_space=pltpu.SMEM)


def al(start, size):
    return pl.ds(pl.multiple_of(start, size), size)


def rotate_rows(rows, cosine, sine_term):
    half = HEAD_DIM // 2
    out = []
    for at in range(0, rows.shape[0], HEAD_DIM):
        leading = rows[at : at + half]
        trailing = rows[at + half : at + HEAD_DIM]
        out.append(leading * cosine - trailing * sine_term)
        out.append(trailing * cosine + leading * sine_term)
    return jnp.concatenate(out, axis=0).astype(bf16)


def write_block(block, rows, id_rows, cos, sin):
    width = rows.shape[0] // 2
    block[0:width, :] = rotate_rows(rows[:width], cos, sin)
    block[width : width + PAD, :] = id_rows
    block[width + PAD :, :] = rows[width:].astype(bf16)


def prepare_kernel(base, frequency, kv, ids_pos, block, band_block, rim, meta, cosine, sine):
    tokens = kv.shape[0]
    angles = ids_pos[1:2, :].astype(f32) * frequency[...]
    cos, sin = jnp.cos(angles), jnp.sin(angles)
    cosine[...] = cos
    sine[...] = sin
    ids = ids_pos[0:1, :]
    shifted = ids + 1
    row = lax.broadcasted_iota(jnp.int32, (PAD, tokens), 0)
    high = jnp.broadcast_to(shifted >> 7, (PAD, tokens))
    low = jnp.broadcast_to(shifted & 127, (PAD, tokens))
    id_rows = jnp.where(row == 0, high, jnp.where(row == 1, low, 0)).astype(f32).astype(bf16)
    half = kv.shape[1] // 2
    write_block(block, kv[:, :half].astype(f32).T, id_rows, cos, sin)
    write_block(band_block, kv[:, half:].astype(f32).T, id_rows, cos, sin)
    rim[...] = band_block[:, tokens - WINDOW :]
    ids_f = ids.astype(f32)
    across = jnp.broadcast_to(ids_f, (tokens, tokens))
    down = across.T
    before = jnp.max(jnp.where(down < across, down, -1.0), axis=0, keepdims=True)
    first = before < 0.0
    begin = jnp.where(first, 0.0, before + 1.0 - base[0].astype(f32))
    mrow = lax.broadcasted_iota(jnp.int32, (8, tokens), 0)
    meta[...] = jnp.where(
        mrow == 0,
        jnp.broadcast_to(begin, (8, tokens)),
        jnp.where(mrow == 1, jnp.broadcast_to(first.astype(f32), (8, tokens)), jnp.broadcast_to(ids_f + 1.0, (8, tokens))),
    )


def prepare(base, frequency, kv, ids_pos):
    tokens, every = kv.shape
    height = every // 2 + PAD
    half = HEAD_DIM // 2
    return pl.pallas_call(
        prepare_kernel,
        out_shape=(
            jax.ShapeDtypeStruct((height, tokens), bf16),
            jax.ShapeDtypeStruct((height, tokens), bf16),
            jax.ShapeDtypeStruct((height, WINDOW), bf16),
            jax.ShapeDtypeStruct((8, tokens), f32),
            jax.ShapeDtypeStruct((half, tokens), f32),
            jax.ShapeDtypeStruct((half, tokens), f32),
        ),
        in_specs=[SM] + [VM] * 3,
        out_specs=(VM,) * 6,
        compiler_params=pltpu.CompilerParams(vmem_limit_bytes=8 << 20),
        name="prepare",
    )(base, frequency, kv, ids_pos)


def two_deep(units, scores, outs, s0, s1, x0, x1):
    scores(0, s0, x0)

    def pair(i, _):
        u = 2 * i
        scores(u + 1, s1, x1)
        outs(u, s0, x0)
        scores(jnp.minimum(u + 2, units - 1), s0, x0)
        outs(u + 1, s1, x1)
        return 0

    lax.fori_loop(0, units // 2, pair, 0)


def column_peak(s):
    return jnp.broadcast_to(jnp.max(s, axis=0, keepdims=True), (8, s.shape[1]))


def transposed_keys(rows, extra):
    return jnp.concatenate([rows.astype(f32), extra], axis=0).T.astype(bf16)


def ids_of(rows):
    rows = rows.astype(f32)
    return rows[0:1] * 128.0 + rows[1:2]


def mask_rows(ids, own_id, present):
    bar = jnp.where((ids < own_id) | jnp.logical_not(present), neg_fill, 0.0)
    row = lax.broadcasted_iota(jnp.int32, (HEAD_DIM, ids.shape[1]), 0)
    return jnp.where(row == 0, jnp.broadcast_to(bar, row.shape), jnp.where(row == 1, 1.0, 0.0))


def rotate_into(src, dst, cos, sin):
    wide = src.shape[1]
    step = min(wide, 4 * AUG)
    for at in range(0, wide, step):
        dst[at : at + step, :] = rotate_rows(src[:, at : at + step].astype(f32).T, cos, sin)


def own_kernel(group, fq, cosine, sine, block, meta, fqt, peak, total, accum, keys, bias, s0, s1, x0, x1):
    tokens, wide = fq.shape
    width = wide // group
    kv = width // HEAD_DIM
    rotate_into(fq, fqt, cosine[...], sine[...])
    zero = jnp.zeros((HEAD_DIM, tokens), f32)
    for h in range(kv):
        keys[h * tokens : (h + 1) * tokens, :] = transposed_keys(block[h * HEAD_DIM : (h + 1) * HEAD_DIM, :], zero)
    begin = jnp.broadcast_to(meta[0:1, :], (tokens, tokens)).astype(jnp.int32)
    r = lax.broadcasted_iota(jnp.int32, (tokens, tokens), 0)
    t = lax.broadcasted_iota(jnp.int32, (tokens, tokens), 1)
    bias[...] = jnp.where((r >= begin) & (r <= t), 0.0, neg_fill)
    several = s0.shape[0] // tokens

    def scores(u, buf, x):
        h = u * several // group
        k = keys[al(h * tokens, tokens), :][:, :HEAD_DIM]
        for g in range(several):
            q = fqt[al((u * several + g) * HEAD_DIM, HEAD_DIM), :]
            s = jnp.dot(k, q, preferred_element_type=f32) + bias[...]
            buf[g * tokens : (g + 1) * tokens, :] = s
            x[8 * g : 8 * g + 8, :] = column_peak(s)

    def outs(u, buf, x):
        h = u * several // group
        v = block[pl.ds(pl.multiple_of(width + PAD + h * HEAD_DIM, PAD), HEAD_DIM), :]
        for g in range(several):
            at = u * several + g
            m = x[8 * g : 8 * g + 1, :]
            p = jnp.exp2(buf[g * tokens : (g + 1) * tokens, :] * to_log2 - m * to_log2)
            peak[pl.ds(at, 1), :] = m
            total[pl.ds(at, 1), :] = jnp.sum(p, axis=0, keepdims=True)
            accum[al(at * HEAD_DIM, HEAD_DIM), :] = jnp.dot(v, p.astype(bf16), preferred_element_type=f32)

    two_deep(wide // HEAD_DIM // several, scores, outs, s0, s1, x0, x1)


def own(group, fq, cosine, sine, block, meta):
    tokens, wide = fq.shape
    heads = wide // HEAD_DIM
    kv = heads // group
    several = 4
    return pl.pallas_call(
        functools.partial(own_kernel, group),
        out_shape=(
            jax.ShapeDtypeStruct((wide, tokens), bf16),
            jax.ShapeDtypeStruct((heads, tokens), f32),
            jax.ShapeDtypeStruct((heads, tokens), f32),
            jax.ShapeDtypeStruct((wide, tokens), f32),
        ),
        in_specs=[VM] * 5,
        out_specs=(VM,) * 4,
        scratch_shapes=[
            pltpu.VMEM((kv * tokens, AUG), bf16),
            pltpu.VMEM((tokens, tokens), f32),
            pltpu.VMEM((several * tokens, tokens), f32),
            pltpu.VMEM((several * tokens, tokens), f32),
            pltpu.VMEM((8 * several, tokens), f32),
            pltpu.VMEM((8 * several, tokens), f32),
        ],
        compiler_params=pltpu.CompilerParams(vmem_limit_bytes=16 << 20),
        cost_estimate=pl.CostEstimate(
            flops=4 * heads * tokens * tokens * HEAD_DIM * 4, transcendentals=heads * tokens * tokens, bytes_accessed=12 * wide * tokens
        ),
        name="own",
    )(fq, cosine, sine, block, meta)


def band_kernel(group, base, bq, cosine, sine, block, rim, meta, out, bqt, keys, vals, bias, s0, s1, x0, x1):
    tokens, wide = bq.shape
    width = wide // group
    kv = width // HEAD_DIM
    span = tokens + WINDOW
    tile = 2 * WINDOW
    rotate_into(bq, bqt, cosine[...], sine[...])
    zero = jnp.zeros((HEAD_DIM, tokens), f32)
    for h in range(kv):
        rows = slice(h * HEAD_DIM, (h + 1) * HEAD_DIM)
        keys[h * span : h * span + WINDOW, :] = transposed_keys(rim[rows, :], zero[:, :WINDOW])
        keys[h * span + WINDOW : (h + 1) * span, :] = transposed_keys(block[rows, :], zero)
    vals[:, :WINDOW] = rim[width + PAD :, :]
    vals[:, WINDOW:] = block[width + PAD :, :]
    own_id = jnp.min(meta[2:3, :])
    barred = jnp.where(base[0] == 0, float(WINDOW), jnp.sum((ids_of(rim[width : width + PAD, :]) < own_id).astype(f32)))
    begin = meta[0:1, :]
    first = meta[1:2, :]
    r = lax.broadcasted_iota(jnp.int32, (tile, tile), 0).astype(f32)
    t = (lax.broadcasted_iota(jnp.int32, (1, tile), 1) & (WINDOW - 1)).astype(f32)
    halves = tokens // WINDOW
    for half in range(halves):
        lo = begin + float(WINDOW - half * WINDOW)
        if half == 0:
            lo = jnp.where(first > 0.0, barred, lo)
        lo = lo[:, half * WINDOW : (half + 1) * WINDOW]
        low = jnp.maximum(jnp.concatenate([lo, lo], axis=1), t + 1.0)
        bias[half * tile : (half + 1) * tile, :] = jnp.where((r >= low) & (r <= t + WINDOW), 0.0, neg_fill)
    pairs = group // 2
    several = s0.shape[0] // tile // halves

    def scores(u, buf, x):
        h = u * several // pairs
        for half in range(halves):
            k = keys[pl.ds(pl.multiple_of(h * span + half * WINDOW, WINDOW), tile), :][:, :HEAD_DIM]
            for g in range(several):
                q = bqt[al((u * several + g) * AUG, AUG), :][:, half * WINDOW : (half + 1) * WINDOW]
                q = jnp.concatenate([q[:HEAD_DIM], q[HEAD_DIM:]], axis=1)
                s = jnp.dot(k, q, preferred_element_type=f32) + bias[half * tile : (half + 1) * tile, :]
                at = half * several + g
                buf[at * tile : (at + 1) * tile, :] = s
                x[8 * at : 8 * at + 8, :] = column_peak(s)

    def outs(u, buf, x):
        h = u * several // pairs
        for half in range(halves):
            v = vals[al(h * HEAD_DIM, HEAD_DIM), half * WINDOW : half * WINDOW + tile]
            for g in range(several):
                at = half * several + g
                m = x[8 * at : 8 * at + 1, :]
                p = jnp.exp2(buf[at * tile : (at + 1) * tile, :] * to_log2 - m * to_log2)
                total = jnp.sum(p, axis=0, keepdims=True)
                o = jnp.dot(v, p.astype(bf16), preferred_element_type=f32) / total
                o = jnp.concatenate([o[:, :WINDOW], o[:, WINDOW:]], axis=0)
                out[half * WINDOW : (half + 1) * WINDOW, al((u * several + g) * AUG, AUG)] = o.T.astype(bf16)

    two_deep(kv * pairs // several, scores, outs, s0, s1, x0, x1)


def band(group, base, bq, cosine, sine, block, rim, meta):
    tokens, wide = bq.shape
    kv = wide // group // HEAD_DIM
    span = tokens + WINDOW
    several = 2
    tiles = several * (tokens // WINDOW)
    return pl.pallas_call(
        functools.partial(band_kernel, group),
        out_shape=jax.ShapeDtypeStruct((tokens, wide), bf16),
        in_specs=[SM] + [VM] * 6,
        out_specs=VM,
        scratch_shapes=[
            pltpu.VMEM((wide, tokens), bf16),
            pltpu.VMEM((kv * span, AUG), bf16),
            pltpu.VMEM((kv * HEAD_DIM, span), bf16),
            pltpu.VMEM((tokens // WINDOW * 2 * WINDOW, 2 * WINDOW), f32),
            pltpu.VMEM((tiles * 2 * WINDOW, 2 * WINDOW), f32),
            pltpu.VMEM((tiles * 2 * WINDOW, 2 * WINDOW), f32),
            pltpu.VMEM((8 * tiles, 2 * WINDOW), f32),
            pltpu.VMEM((8 * tiles, 2 * WINDOW), f32),
        ],
        compiler_params=pltpu.CompilerParams(vmem_limit_bytes=16 << 20),
        cost_estimate=pl.CostEstimate(
            flops=4 * wide * tokens * 2 * WINDOW * 4, transcendentals=wide // HEAD_DIM * tokens * 2 * WINDOW, bytes_accessed=4 * wide * tokens
        ),
        name="band",
    )(base, bq, cosine, sine, block, rim, meta)


def remote_update(group, flags, fqt, shards, meta, state_in, state_out, keys, s0, s1, x0, x1):
    wide, tokens = fqt.shape
    width = wide // group
    kv = width // HEAD_DIM
    span = len(shards) * tokens
    peak_in, total_in, accum_in = state_in
    peak, total, accum = state_out
    own_id = jnp.min(meta[2:3, :])
    for b, (kref, krow, _, _, flag) in enumerate(shards):
        extra = mask_rows(ids_of(kref[krow + width : krow + width + PAD, :]), own_id, flags[flag] > 0)
        for h in range(kv):
            rows = kref[krow + h * HEAD_DIM : krow + (h + 1) * HEAD_DIM, :]
            keys[h * span + b * tokens : h * span + (b + 1) * tokens, :] = transposed_keys(rows, extra)
    row = lax.broadcasted_iota(jnp.int32, (HEAD_DIM, tokens), 0)
    other = jnp.where(meta[1:2, :] > 0.0, 0.0, neg_fill)
    query_rows = jnp.where(row == 0, 1.0, jnp.where(row == 1, jnp.broadcast_to(other, row.shape), 0.0)).astype(bf16)

    several = s0.shape[0] // span

    def scores(u, buf, x):
        h = u * several // group
        k = keys[al(h * span, span), :]
        for g in range(several):
            q = jnp.concatenate([fqt[al((u * several + g) * HEAD_DIM, HEAD_DIM), :], query_rows], axis=0)
            s = jnp.dot(k, q, preferred_element_type=f32)
            buf[g * span : (g + 1) * span, :] = s
            x[8 * g : 8 * g + 8, :] = column_peak(s)

    def outs(u, buf, x):
        h = u * several // group
        for g in range(several):
            at = u * several + g
            old = peak_in[pl.ds(at, 1), :]
            m = jnp.maximum(old, x[8 * g : 8 * g + 1, :])
            scaled = m * to_log2
            factor = jnp.exp2(old * to_log2 - scaled)
            peak[pl.ds(at, 1), :] = m
            rows = al(at * HEAD_DIM, HEAD_DIM)
            t = total_in[pl.ds(at, 1), :] * factor
            a = accum_in[rows, :] * factor
            for b, (_, _, vref, vrow, _) in enumerate(shards):
                p = jnp.exp2(buf[g * span + b * tokens : g * span + (b + 1) * tokens, :] * to_log2 - scaled)
                t = t + jnp.sum(p, axis=0, keepdims=True)
                v = vref[pl.ds(pl.multiple_of(vrow + h * HEAD_DIM, PAD), HEAD_DIM), :]
                a = a + jnp.dot(v, p.astype(bf16), preferred_element_type=f32)
            total[pl.ds(at, 1), :] = t
            accum[rows, :] = a

    two_deep(wide // HEAD_DIM // several, scores, outs, s0, s1, x0, x1)


def remote_scratch(kv, tokens, count):
    span = count * tokens
    several = 4 if count < 3 else 2
    return [
        pltpu.VMEM((kv * span, AUG), bf16),
        pltpu.VMEM((several * span, tokens), f32),
        pltpu.VMEM((several * span, tokens), f32),
        pltpu.VMEM((8 * several, tokens), f32),
        pltpu.VMEM((8 * several, tokens), f32),
    ]


def placed(shards, refs):
    return [(refs[ka], kr, refs[va], vr, flag) for ka, kr, va, vr, flag in shards]


def remote_kernel(group, shards, n, flags, fqt, *refs):
    meta, peak_in, total_in, accum_in, peak, total, accum = refs[n : n + 7]
    remote_update(group, flags, fqt, placed(shards, refs), meta, (peak_in, total_in, accum_in), (peak, total, accum), *refs[n + 7 :])


def remote(group, flags, fqt, arrays, shards, meta, state):
    wide, tokens = fqt.shape
    heads = wide // HEAD_DIM
    count = len(shards)
    n = len(arrays)
    return pl.pallas_call(
        functools.partial(remote_kernel, group, shards, n),
        out_shape=tuple(jax.ShapeDtypeStruct(x.shape, x.dtype) for x in state),
        in_specs=[SM] + [VM] * (n + 5),
        out_specs=(VM,) * 3,
        scratch_shapes=remote_scratch(heads // group, tokens, count),
        input_output_aliases={n + 3 + i: i for i in range(3)},
        compiler_params=pltpu.CompilerParams(vmem_limit_bytes=16 << 20),
        cost_estimate=pl.CostEstimate(
            flops=4 * wide * tokens * tokens * count * 4, transcendentals=heads * tokens * tokens * count, bytes_accessed=20 * wide * tokens
        ),
        name="remote",
    )(flags, fqt, *arrays, meta, *state)


def last_kernel(group, shards, n, flags, side, fqt, *refs):
    meta, peak_in, total_in, accum_in, held, mine, theirs = refs[n : n + 7]
    keys, s0, s1, x0, x1, peak, total, accum, mixed = refs[n + 7 :]
    remote_update(group, flags, fqt, placed(shards, refs), meta, (peak_in, total_in, accum_in), (peak, total, accum), keys, s0, s1, x0, x1)
    wide, tokens = fqt.shape
    rows = tokens // 2
    for u in range(wide // HEAD_DIM):
        at = slice(u * HEAD_DIM, (u + 1) * HEAD_DIM)
        mixed[at, :] = (accum[at, :] / total[u : u + 1, :]).astype(bf16)
    first = side[0] == 0
    columns = held.shape[0]
    step = 4 * AUG
    for at in range(0, columns, step):
        size = min(step, columns - at)
        part = jnp.dot(held[at : at + size, :], mixed[...], preferred_element_type=f32).astype(bf16)
        low, high = part[:, :rows], part[:, rows:]
        mine[at : at + size, :] = jnp.where(first, low, high)
        theirs[at : at + size, :] = jnp.where(first, high, low)


def last(group, flags, side, fqt, arrays, shards, meta, state, weight):
    wide, tokens = fqt.shape
    heads = wide // HEAD_DIM
    count = len(shards)
    n = len(arrays)
    return pl.pallas_call(
        functools.partial(last_kernel, group, shards, n),
        out_shape=(jax.ShapeDtypeStruct((weight.shape[0], tokens // 2), bf16),) * 2,
        in_specs=[SM] * 2 + [VM] * (n + 6),
        out_specs=(VM, VM),
        scratch_shapes=remote_scratch(heads // group, tokens, count)
        + [
            pltpu.VMEM((heads, tokens), f32),
            pltpu.VMEM((heads, tokens), f32),
            pltpu.VMEM((wide, tokens), f32),
            pltpu.VMEM((wide, tokens), bf16),
        ],
        compiler_params=pltpu.CompilerParams(vmem_limit_bytes=28 << 20),
        cost_estimate=pl.CostEstimate(
            flops=4 * wide * tokens * tokens * count * 4, transcendentals=heads * tokens * tokens * count, bytes_accessed=20 * wide * tokens
        ),
        name="last",
    )(flags, side, fqt, *arrays, meta, *state, weight)


def shifted_by(block, distance, wrap=True):
    size = lax.axis_size("ctx")
    route = [(i, (i + distance) % size) for i in range(size) if wrap or i + distance < size]
    return lax.ppermute(block, "ctx", route)


def swapped(block, bit):
    size = lax.axis_size("ctx")
    return lax.ppermute(block, "ctx", [(i, i ^ bit) for i in range(size)])


def body(banded_queries, banded_keys, banded_values, full_queries, full_keys, full_values, segment_ids, position_ids, out_weight):
    tokens = segment_ids.shape[0]
    width = full_keys.shape[1]
    height = 2 * width + PAD
    vrow = width + PAD
    group = banded_queries.shape[1] // banded_keys.shape[1]
    here = lax.axis_index("ctx")
    half = HEAD_DIM // 2
    frequency = theta_base ** (-2.0 * jnp.arange(half, dtype=f32) / HEAD_DIM)
    frequency = jnp.broadcast_to(frequency[:, None], (half, tokens))
    base = (here * tokens).astype(jnp.int32).reshape(1)
    plane = here // PLANE
    beside = [((here & bit) != 0) | (plane >= REACH // PLANE) for bit in (1, 2)]
    flags = jnp.stack([plane >= back for back in range(REACH // PLANE + 1)] + beside).astype(jnp.int32)
    pick_x, pick_y = REACH // PLANE + 1, REACH // PLANE + 2
    side = lax.axis_index("head")

    kv = jnp.concatenate([full_keys, full_values, banded_keys, banded_values], axis=1)
    ids_pos = jnp.stack([segment_ids, position_ids])
    block, band_kv, rim, meta, cosine, sine = prepare(base, frequency, kv, ids_pos)
    z1 = shifted_by(block, PLANE)
    rim = shifted_by(rim, 1)
    fqt, *state = own(group, full_queries, cosine, sine, block, meta)
    z1, rim, block, state = lax.optimization_barrier((z1, rim, block, state))

    z2 = shifted_by(z1, PLANE)
    z3 = shifted_by(z1, 2 * PLANE, wrap=False)
    x1 = swapped(z1, 1)
    y1 = swapped(z1, 2)
    banded_out = band(group, base, banded_queries, cosine, sine, band_kv, rim, meta)
    state = remote(group, flags, fqt, [z1], ((0, 0, 0, vrow, 1),), meta, state)
    z2, z3, block, state, banded_out = lax.optimization_barrier((z2, z3, block, state, banded_out))

    def farthest(bit):
        return jnp.where((here & bit) == 0, block, z3)

    x2 = swapped(jnp.concatenate([z2, farthest(1)]), 1)
    y2 = swapped(jnp.concatenate([z2, farthest(2)]), 2)
    z2, z3, x1, y1 = lax.optimization_barrier((z2, z3, x1, y1))
    state = remote(group, flags, fqt, [x1, y1, z2, z3], tuple((a, 0, a, vrow, flag) for a, flag in enumerate((1, 1, 2, 3))), meta, state)
    x2, y2, state = lax.optimization_barrier((x2, y2, state))

    dx = swapped(jnp.concatenate([y1[:vrow], y2[height:]]), 1)
    dy = swapped(jnp.concatenate([x1[vrow:], x2[:height]]), 2)
    state = remote(
        group,
        flags,
        fqt,
        [x2, y2],
        ((0, 0, 0, vrow, 2), (0, height, 0, height + vrow, pick_x), (1, 0, 1, vrow, 2), (1, height, 1, height + vrow, pick_y)),
        meta,
        state,
    )
    dx, dy, state = lax.optimization_barrier((dx, dy, state))
    mine, theirs = last(
        group,
        flags,
        side.reshape(1).astype(jnp.int32),
        fqt,
        [dx, dy],
        ((0, 0, 1, 0, 1), (0, vrow, 0, 2 * vrow, pick_y), (1, width, 1, width + vrow, 2)),
        meta,
        state,
        out_weight.T,
    )

    sides = lax.axis_size("head")
    if sides != 2:
        part = jnp.concatenate([jnp.where(side == 0, mine, theirs), jnp.where(side == 0, theirs, mine)], axis=1).T
        return banded_out, lax.psum_scatter(part, "head", scatter_dimension=0, tiled=True)
    theirs = lax.ppermute(theirs, "head", [(0, 1), (1, 0)])
    projected = (mine.astype(f32) + theirs.astype(f32)).astype(bf16)
    return banded_out, projected.T


def solution(mesh):
    return jax.shard_map(
        body,
        mesh=mesh,
        in_specs=(
            P("ctx", "head"),
            P("ctx", "head"),
            P("ctx", "head"),
            P("ctx", "head"),
            P("ctx", "head"),
            P("ctx", "head"),
            P("ctx"),
            P("ctx"),
            P("head", None),
        ),
        out_specs=(P("ctx", "head"), P(("ctx", "head"), None)),
        check_vma=False,
    )
```

```python
import functools

import jax
import jax.numpy as jnp
from jax import lax
from jax.experimental import pallas as pl
from jax.experimental.pallas import tpu as pltpu
from jax.sharding import PartitionSpec as P

HEAD_DIM = 64
WINDOW = 128
REACH = 12
PLANE = 4
PAD = 16
AUG = 2 * HEAD_DIM
META = 16
BACK = 2
PICK_X = BACK + REACH // PLANE + 1
PICK_Y = PICK_X + 1
SIDE0 = PICK_X + 2
LATER = PICK_X + 3

theta_base = 150000.0
neg_fill = -1e30
to_log2 = HEAD_DIM ** (-0.5) * 1.4426950408889634

f32 = jnp.float32
bf16 = jnp.bfloat16
VM = pl.BlockSpec(memory_space=pltpu.VMEM)
SM = pl.BlockSpec(memory_space=pltpu.SMEM)


def al(start, size):
    return pl.ds(pl.multiple_of(start, size), size)


def rotate_rows(rows, cosine, sine_term):
    half = HEAD_DIM // 2
    out = []
    for at in range(0, rows.shape[0], HEAD_DIM):
        leading = rows[at : at + half]
        trailing = rows[at + half : at + HEAD_DIM]
        out.append(leading * cosine - trailing * sine_term)
        out.append(trailing * cosine + leading * sine_term)
    return jnp.concatenate(out, axis=0).astype(bf16)


def write_block(block, rows, id_rows, cos, sin):
    width = rows.shape[0] // 2
    block[0:width, :] = rotate_rows(rows[:width], cos, sin)
    block[width : width + PAD, :] = id_rows
    block[width + PAD :, :] = rows[width:].astype(bf16)


def prepare_kernel(base, side, frequency, kv, ids_pos, block, band_block, rim, meta, cosine, sine):
    tokens = kv.shape[0]
    angles = ids_pos[1:2, :].astype(f32) * frequency[...]
    cos, sin = jnp.cos(angles), jnp.sin(angles)
    cosine[...] = cos
    sine[...] = sin
    ids = ids_pos[0:1, :]
    shifted = ids + 1
    row = lax.broadcasted_iota(jnp.int32, (PAD, tokens), 0)
    high = jnp.broadcast_to(shifted >> 7, (PAD, tokens))
    low = jnp.broadcast_to(shifted & 127, (PAD, tokens))
    id_rows = jnp.where(row == 0, high, jnp.where(row == 1, low, 0)).astype(f32).astype(bf16)
    half = kv.shape[1] // 2
    write_block(block, kv[:, :half].astype(f32).T, id_rows, cos, sin)
    write_block(band_block, kv[:, half:].astype(f32).T, id_rows, cos, sin)
    rim[...] = band_block[:, tokens - WINDOW :]
    ids_f = ids.astype(f32)
    across = jnp.broadcast_to(ids_f, (tokens, tokens))
    down = across.T
    before = jnp.max(jnp.where(down < across, down, -1.0), axis=0, keepdims=True)
    first = before < 0.0
    begin = jnp.where(first, 0.0, before + 1.0 - base[0].astype(f32))
    here = base[0] // tokens
    plane = here // PLANE
    farthest = REACH // PLANE
    rows = [begin, first.astype(f32), ids_f + 1.0]
    rows += [plane >= back for back in range(1, farthest + 1)]
    rows += [(here % 2 == 1) | (plane >= farthest), (here // 2 % 2 == 1) | (plane >= farthest)]
    rows += [side[0] == 0, here > 0]
    mrow = lax.broadcasted_iota(jnp.int32, meta.shape, 0)
    total = jnp.zeros(meta.shape, f32)
    for i, value in enumerate(rows):
        value = jnp.where(value, 1.0, 0.0) if value.dtype == jnp.bool_ else value
        total = jnp.where(mrow == i, jnp.broadcast_to(value, meta.shape), total)
    meta[...] = total


def prepare(base, side, frequency, kv, ids_pos):
    tokens, every = kv.shape
    height = every // 2 + PAD
    half = HEAD_DIM // 2
    return pl.pallas_call(
        prepare_kernel,
        out_shape=(
            jax.ShapeDtypeStruct((height, tokens), bf16),
            jax.ShapeDtypeStruct((height, tokens), bf16),
            jax.ShapeDtypeStruct((height, WINDOW), bf16),
            jax.ShapeDtypeStruct((META, tokens), f32),
            jax.ShapeDtypeStruct((half, tokens), f32),
            jax.ShapeDtypeStruct((half, tokens), f32),
        ),
        in_specs=[SM] * 2 + [VM] * 3,
        out_specs=(VM,) * 6,
        compiler_params=pltpu.CompilerParams(vmem_limit_bytes=8 << 20),
        name="prepare",
    )(base, side, frequency, kv, ids_pos)


def two_deep(units, scores, outs, s0, s1, x0, x1):
    scores(0, s0, x0)

    def pair(i, _):
        u = 2 * i
        scores(u + 1, s1, x1)
        outs(u, s0, x0)
        scores(jnp.minimum(u + 2, units - 1), s0, x0)
        outs(u + 1, s1, x1)
        return 0

    lax.fori_loop(0, units // 2, pair, 0)


def column_peak(s):
    return jnp.broadcast_to(jnp.max(s, axis=0, keepdims=True), (8, s.shape[1]))


def transposed_keys(rows, extra):
    return jnp.concatenate([rows.astype(f32), extra], axis=0).T.astype(bf16)


def ids_of(rows):
    rows = rows.astype(f32)
    return rows[0:1] * 128.0 + rows[1:2]


def mask_rows(ids, own_id, present):
    bar = jnp.where((ids < own_id) | jnp.logical_not(present), neg_fill, 0.0)
    row = lax.broadcasted_iota(jnp.int32, (HEAD_DIM, ids.shape[1]), 0)
    return jnp.where(row == 0, jnp.broadcast_to(bar, row.shape), jnp.where(row == 1, 1.0, 0.0))


def rotate_into(src, dst, cos, sin):
    wide = src.shape[1]
    step = min(wide, 4 * AUG)
    for at in range(0, wide, step):
        dst[at : at + step, :] = rotate_rows(src[:, at : at + step].astype(f32).T, cos, sin)


def own_kernel(group, fq, bq, cosine, sine, block, meta, fqt, bqt, peak, total, accum, keys, bias, s0, s1, x0, x1):
    tokens, wide = fq.shape
    width = wide // group
    kv = width // HEAD_DIM
    rotate_into(fq, fqt, cosine[...], sine[...])
    zero = jnp.zeros((HEAD_DIM, tokens), f32)
    for h in range(kv):
        keys[h * tokens : (h + 1) * tokens, :] = transposed_keys(block[h * HEAD_DIM : (h + 1) * HEAD_DIM, :], zero)
    begin = jnp.broadcast_to(meta[0:1, :], (tokens, tokens)).astype(jnp.int32)
    r = lax.broadcasted_iota(jnp.int32, (tokens, tokens), 0)
    t = lax.broadcasted_iota(jnp.int32, (tokens, tokens), 1)
    bias[...] = jnp.where((r >= begin) & (r <= t), 0.0, neg_fill)
    several = s0.shape[0] // tokens

    def scores(u, buf, x):
        h = u * several // group
        k = keys[al(h * tokens, tokens), :][:, :HEAD_DIM]
        for g in range(several):
            q = fqt[al((u * several + g) * HEAD_DIM, HEAD_DIM), :]
            s = jnp.dot(k, q, preferred_element_type=f32) + bias[...]
            buf[g * tokens : (g + 1) * tokens, :] = s
            x[8 * g : 8 * g + 8, :] = column_peak(s)

    def outs(u, buf, x):
        h = u * several // group
        v = block[pl.ds(pl.multiple_of(width + PAD + h * HEAD_DIM, PAD), HEAD_DIM), :]
        for g in range(several):
            at = u * several + g
            m = x[8 * g : 8 * g + 1, :]
            p = jnp.exp2(buf[g * tokens : (g + 1) * tokens, :] * to_log2 - m * to_log2)
            peak[pl.ds(at, 1), :] = m
            total[pl.ds(at, 1), :] = jnp.sum(p, axis=0, keepdims=True)
            accum[al(at * HEAD_DIM, HEAD_DIM), :] = jnp.dot(v, p.astype(bf16), preferred_element_type=f32)

    two_deep(wide // HEAD_DIM // several, scores, outs, s0, s1, x0, x1)
    rotate_into(bq, bqt, cosine[...], sine[...])


def own(group, fq, bq, cosine, sine, block, meta):
    tokens, wide = fq.shape
    heads = wide // HEAD_DIM
    kv = heads // group
    several = 4
    return pl.pallas_call(
        functools.partial(own_kernel, group),
        out_shape=(
            jax.ShapeDtypeStruct((wide, tokens), bf16),
            jax.ShapeDtypeStruct((wide, tokens), bf16),
            jax.ShapeDtypeStruct((heads, tokens), f32),
            jax.ShapeDtypeStruct((heads, tokens), f32),
            jax.ShapeDtypeStruct((wide, tokens), f32),
        ),
        in_specs=[VM] * 6,
        out_specs=(VM,) * 5,
        scratch_shapes=[
            pltpu.VMEM((kv * tokens, AUG), bf16),
            pltpu.VMEM((tokens, tokens), f32),
            pltpu.VMEM((several * tokens, tokens), f32),
            pltpu.VMEM((several * tokens, tokens), f32),
            pltpu.VMEM((8 * several, tokens), f32),
            pltpu.VMEM((8 * several, tokens), f32),
        ],
        compiler_params=pltpu.CompilerParams(vmem_limit_bytes=16 << 20),
        cost_estimate=pl.CostEstimate(
            flops=4 * heads * tokens * tokens * HEAD_DIM * 4, transcendentals=heads * tokens * tokens, bytes_accessed=12 * wide * tokens
        ),
        name="own",
    )(fq, bq, cosine, sine, block, meta)


def band_kernel(group, bqt, block, rim, meta, out, keys, vals, bias, s0, s1, x0, x1):
    wide, tokens = bqt.shape
    width = wide // group
    kv = width // HEAD_DIM
    span = tokens + WINDOW
    tile = 2 * WINDOW
    zero = jnp.zeros((HEAD_DIM, tokens), f32)
    for h in range(kv):
        rows = slice(h * HEAD_DIM, (h + 1) * HEAD_DIM)
        keys[h * span : h * span + WINDOW, :] = transposed_keys(rim[rows, :], zero[:, :WINDOW])
        keys[h * span + WINDOW : (h + 1) * span, :] = transposed_keys(block[rows, :], zero)
    vals[:, :WINDOW] = rim[width + PAD :, :]
    vals[:, WINDOW:] = block[width + PAD :, :]
    own_id = jnp.min(meta[2:3, :])
    barred = (ids_of(rim[width : width + PAD, :]) < own_id) | (meta[LATER : LATER + 1, :WINDOW] == 0.0)
    barred = jnp.sum(barred.astype(f32))
    begin = meta[0:1, :]
    first = meta[1:2, :]
    r = lax.broadcasted_iota(jnp.int32, (tile, tile), 0).astype(f32)
    t = (lax.broadcasted_iota(jnp.int32, (1, tile), 1) & (WINDOW - 1)).astype(f32)
    halves = tokens // WINDOW
    for half in range(halves):
        lo = begin + float(WINDOW - half * WINDOW)
        if half == 0:
            lo = jnp.where(first > 0.0, barred, lo)
        lo = lo[:, half * WINDOW : (half + 1) * WINDOW]
        low = jnp.maximum(jnp.concatenate([lo, lo], axis=1), t + 1.0)
        bias[half * tile : (half + 1) * tile, :] = jnp.where((r >= low) & (r <= t + WINDOW), 0.0, neg_fill)
    pairs = group // 2
    several = s0.shape[0] // tile // halves

    def scores(u, buf, x):
        h = u * several // pairs
        for half in range(halves):
            k = keys[pl.ds(pl.multiple_of(h * span + half * WINDOW, WINDOW), tile), :][:, :HEAD_DIM]
            for g in range(several):
                q = bqt[al((u * several + g) * AUG, AUG), :][:, half * WINDOW : (half + 1) * WINDOW]
                q = jnp.concatenate([q[:HEAD_DIM], q[HEAD_DIM:]], axis=1)
                s = jnp.dot(k, q, preferred_element_type=f32) + bias[half * tile : (half + 1) * tile, :]
                at = half * several + g
                buf[at * tile : (at + 1) * tile, :] = s
                x[8 * at : 8 * at + 8, :] = column_peak(s)

    def outs(u, buf, x):
        h = u * several // pairs
        for half in range(halves):
            v = vals[al(h * HEAD_DIM, HEAD_DIM), half * WINDOW : half * WINDOW + tile]
            for g in range(several):
                at = half * several + g
                m = x[8 * at : 8 * at + 1, :]
                p = jnp.exp2(buf[at * tile : (at + 1) * tile, :] * to_log2 - m * to_log2)
                total = jnp.sum(p, axis=0, keepdims=True)
                o = jnp.dot(v, p.astype(bf16), preferred_element_type=f32) / total
                o = jnp.concatenate([o[:, :WINDOW], o[:, WINDOW:]], axis=0)
                out[half * WINDOW : (half + 1) * WINDOW, al((u * several + g) * AUG, AUG)] = o.T.astype(bf16)

    two_deep(kv * pairs // several, scores, outs, s0, s1, x0, x1)


def band(group, bqt, block, rim, meta):
    wide, tokens = bqt.shape
    kv = wide // group // HEAD_DIM
    span = tokens + WINDOW
    several = 2
    tiles = several * (tokens // WINDOW)
    return pl.pallas_call(
        functools.partial(band_kernel, group),
        out_shape=jax.ShapeDtypeStruct((tokens, wide), bf16),
        in_specs=[VM] * 4,
        out_specs=VM,
        scratch_shapes=[
            pltpu.VMEM((kv * span, AUG), bf16),
            pltpu.VMEM((kv * HEAD_DIM, span), bf16),
            pltpu.VMEM((tokens // WINDOW * 2 * WINDOW, 2 * WINDOW), f32),
            pltpu.VMEM((tiles * 2 * WINDOW, 2 * WINDOW), f32),
            pltpu.VMEM((tiles * 2 * WINDOW, 2 * WINDOW), f32),
            pltpu.VMEM((8 * tiles, 2 * WINDOW), f32),
            pltpu.VMEM((8 * tiles, 2 * WINDOW), f32),
        ],
        compiler_params=pltpu.CompilerParams(vmem_limit_bytes=16 << 20),
        cost_estimate=pl.CostEstimate(
            flops=4 * wide * tokens * 2 * WINDOW * 4, transcendentals=wide // HEAD_DIM * tokens * 2 * WINDOW, bytes_accessed=4 * wide * tokens
        ),
        name="band",
    )(bqt, block, rim, meta)


def remote_update(group, fqt, shards, meta, state_in, state_out, keys, s0, s1, x0, x1):
    wide, tokens = fqt.shape
    width = wide // group
    kv = width // HEAD_DIM
    span = len(shards) * tokens
    peak_in, total_in, accum_in = state_in
    peak, total, accum = state_out
    own_id = jnp.min(meta[2:3, :])
    for b, (kref, krow, _, _, flag) in enumerate(shards):
        extra = mask_rows(ids_of(kref[krow + width : krow + width + PAD, :]), own_id, meta[flag : flag + 1, :] > 0.0)
        for h in range(kv):
            rows = kref[krow + h * HEAD_DIM : krow + (h + 1) * HEAD_DIM, :]
            keys[h * span + b * tokens : h * span + (b + 1) * tokens, :] = transposed_keys(rows, extra)
    row = lax.broadcasted_iota(jnp.int32, (HEAD_DIM, tokens), 0)
    other = jnp.where(meta[1:2, :] > 0.0, 0.0, neg_fill)
    query_rows = jnp.where(row == 0, 1.0, jnp.where(row == 1, jnp.broadcast_to(other, row.shape), 0.0)).astype(bf16)

    several = s0.shape[0] // span

    def scores(u, buf, x):
        h = u * several // group
        k = keys[al(h * span, span), :]
        for g in range(several):
            q = jnp.concatenate([fqt[al((u * several + g) * HEAD_DIM, HEAD_DIM), :], query_rows], axis=0)
            s = jnp.dot(k, q, preferred_element_type=f32)
            buf[g * span : (g + 1) * span, :] = s
            x[8 * g : 8 * g + 8, :] = column_peak(s)

    def outs(u, buf, x):
        h = u * several // group
        for g in range(several):
            at = u * several + g
            old = peak_in[pl.ds(at, 1), :]
            m = jnp.maximum(old, x[8 * g : 8 * g + 1, :])
            scaled = m * to_log2
            factor = jnp.exp2(old * to_log2 - scaled)
            peak[pl.ds(at, 1), :] = m
            rows = al(at * HEAD_DIM, HEAD_DIM)
            t = total_in[pl.ds(at, 1), :] * factor
            a = accum_in[rows, :] * factor
            for b, (_, _, vref, vrow, _) in enumerate(shards):
                p = jnp.exp2(buf[g * span + b * tokens : g * span + (b + 1) * tokens, :] * to_log2 - scaled)
                t = t + jnp.sum(p, axis=0, keepdims=True)
                v = vref[pl.ds(pl.multiple_of(vrow + h * HEAD_DIM, PAD), HEAD_DIM), :]
                a = a + jnp.dot(v, p.astype(bf16), preferred_element_type=f32)
            total[pl.ds(at, 1), :] = t
            accum[rows, :] = a

    two_deep(wide // HEAD_DIM // several, scores, outs, s0, s1, x0, x1)


def remote_scratch(kv, tokens, count):
    span = count * tokens
    several = 4 if count < 3 else 2
    return [
        pltpu.VMEM((kv * span, AUG), bf16),
        pltpu.VMEM((several * span, tokens), f32),
        pltpu.VMEM((several * span, tokens), f32),
        pltpu.VMEM((8 * several, tokens), f32),
        pltpu.VMEM((8 * several, tokens), f32),
    ]


def placed(shards, refs):
    return [(refs[ka], kr, refs[va], vr, flag) for ka, kr, va, vr, flag in shards]


def remote_kernel(group, shards, n, fqt, *refs):
    meta, peak_in, total_in, accum_in, peak, total, accum = refs[n : n + 7]
    remote_update(group, fqt, placed(shards, refs), meta, (peak_in, total_in, accum_in), (peak, total, accum), *refs[n + 7 :])


def remote(group, fqt, arrays, shards, meta, state):
    wide, tokens = fqt.shape
    heads = wide // HEAD_DIM
    count = len(shards)
    n = len(arrays)
    return pl.pallas_call(
        functools.partial(remote_kernel, group, shards, n),
        out_shape=tuple(jax.ShapeDtypeStruct(x.shape, x.dtype) for x in state),
        in_specs=[VM] * (n + 5),
        out_specs=(VM,) * 3,
        scratch_shapes=remote_scratch(heads // group, tokens, count),
        input_output_aliases={n + 2 + i: i for i in range(3)},
        compiler_params=pltpu.CompilerParams(vmem_limit_bytes=16 << 20),
        cost_estimate=pl.CostEstimate(
            flops=4 * wide * tokens * tokens * count * 4, transcendentals=heads * tokens * tokens * count, bytes_accessed=20 * wide * tokens
        ),
        name="remote",
    )(fqt, *arrays, meta, *state)


def last_kernel(group, shards, n, fqt, *refs):
    meta, peak_in, total_in, accum_in, held, mine, theirs = refs[n : n + 7]
    keys, s0, s1, x0, x1, peak, total, accum, mixed = refs[n + 7 :]
    remote_update(group, fqt, placed(shards, refs), meta, (peak_in, total_in, accum_in), (peak, total, accum), keys, s0, s1, x0, x1)
    wide, tokens = fqt.shape
    rows = tokens // 2
    for u in range(wide // HEAD_DIM):
        at = slice(u * HEAD_DIM, (u + 1) * HEAD_DIM)
        mixed[at, :] = (accum[at, :] / total[u : u + 1, :]).astype(bf16)
    first = meta[SIDE0 : SIDE0 + 1, :rows] > 0.0
    columns = held.shape[0]
    step = 4 * AUG
    for at in range(0, columns, step):
        size = min(step, columns - at)
        part = jnp.dot(held[at : at + size, :], mixed[...], preferred_element_type=f32).astype(bf16)
        low, high = part[:, :rows], part[:, rows:]
        mine[at : at + size, :] = jnp.where(first, low, high)
        theirs[at : at + size, :] = jnp.where(first, high, low)


def last(group, fqt, arrays, shards, meta, state, weight):
    wide, tokens = fqt.shape
    heads = wide // HEAD_DIM
    count = len(shards)
    n = len(arrays)
    return pl.pallas_call(
        functools.partial(last_kernel, group, shards, n),
        out_shape=(jax.ShapeDtypeStruct((weight.shape[0], tokens // 2), bf16),) * 2,
        in_specs=[VM] * (n + 6),
        out_specs=(VM, VM),
        scratch_shapes=remote_scratch(heads // group, tokens, count)
        + [
            pltpu.VMEM((heads, tokens), f32),
            pltpu.VMEM((heads, tokens), f32),
            pltpu.VMEM((wide, tokens), f32),
            pltpu.VMEM((wide, tokens), bf16),
        ],
        compiler_params=pltpu.CompilerParams(vmem_limit_bytes=28 << 20),
        cost_estimate=pl.CostEstimate(
            flops=4 * wide * tokens * tokens * count * 4, transcendentals=heads * tokens * tokens * count, bytes_accessed=20 * wide * tokens
        ),
        name="last",
    )(fqt, *arrays, meta, *state, weight)


def shifted_by(block, distance, first=None):
    size = lax.axis_size("ctx")
    route = [(i, (i + distance) % size) for i in range(size) if first is None or first <= i < size - distance]
    return lax.ppermute(block, "ctx", route)


def swapped(block, bit):
    size = lax.axis_size("ctx")
    return lax.ppermute(block, "ctx", [(i, i ^ bit) for i in range(size)])


def body(banded_queries, banded_keys, banded_values, full_queries, full_keys, full_values, segment_ids, position_ids, out_weight):
    tokens = segment_ids.shape[0]
    width = full_keys.shape[1]
    height = 2 * width + PAD
    vrow = width + PAD
    group = banded_queries.shape[1] // banded_keys.shape[1]
    here = lax.axis_index("ctx")
    half = HEAD_DIM // 2
    frequency = theta_base ** (-2.0 * jnp.arange(half, dtype=f32) / HEAD_DIM)
    frequency = jnp.broadcast_to(frequency[:, None], (half, tokens))
    base = (here * tokens).astype(jnp.int32).reshape(1)
    side = lax.axis_index("head").astype(jnp.int32)

    kv = jnp.concatenate([full_keys, full_values, banded_keys, banded_values], axis=1)
    ids_pos = jnp.stack([segment_ids, position_ids])
    block, band_kv, rim, meta, cosine, sine = prepare(base, side.reshape(1), frequency, kv, ids_pos)
    z1 = shifted_by(block, PLANE)
    fqt, bqt, *state = own(group, full_queries, banded_queries, cosine, sine, block, meta)
    z1, rim, block, state = lax.optimization_barrier((z1, rim, block, state))

    z2 = shifted_by(z1, PLANE)
    z3 = shifted_by(z1, 2 * PLANE, PLANE)
    x1 = swapped(z1, 1)
    y1 = swapped(z1, 2)
    rim = shifted_by(rim, 1)
    state = remote(group, fqt, [z1], ((0, 0, 0, vrow, BACK + 1),), meta, state)
    rim, state = lax.optimization_barrier((rim, state))
    banded_out = band(group, bqt, band_kv, rim, meta)
    z2, z3, block, state, banded_out = lax.optimization_barrier((z2, z3, block, state, banded_out))

    def farthest(bit):
        return jnp.where((here & bit) == 0, block, z3)

    x2 = swapped(jnp.concatenate([z2, farthest(1)]), 1)
    y2 = swapped(jnp.concatenate([z2, farthest(2)]), 2)
    z2, z3, x1, y1 = lax.optimization_barrier((z2, z3, x1, y1))
    state = remote(group, fqt, [x1, y1, z2, z3], tuple((a, 0, a, vrow, flag) for a, flag in enumerate((BACK + 1, BACK + 1, BACK + 2, BACK + 3))), meta, state)
    x2, y2, state = lax.optimization_barrier((x2, y2, state))

    dx = swapped(jnp.concatenate([y1[:vrow], y2[height:]]), 1)
    dy = swapped(jnp.concatenate([x1[vrow:], x2[:height]]), 2)
    state = remote(
        group,
        fqt,
        [x2, y2],
        ((0, 0, 0, vrow, BACK + 2), (0, height, 0, height + vrow, PICK_X), (1, 0, 1, vrow, BACK + 2), (1, height, 1, height + vrow, PICK_Y)),
        meta,
        state,
    )
    dx, dy, state = lax.optimization_barrier((dx, dy, state))
    mine, theirs = last(
        group,
        fqt,
        [dx, dy],
        ((0, 0, 1, 0, BACK + 1), (0, vrow, 0, 2 * vrow, PICK_Y), (1, width, 1, width + vrow, BACK + 2)),
        meta,
        state,
        out_weight.T,
    )

    sides = lax.axis_size("head")
    if sides != 2:
        part = jnp.concatenate([jnp.where(side == 0, mine, theirs), jnp.where(side == 0, theirs, mine)], axis=1).T
        return banded_out, lax.psum_scatter(part, "head", scatter_dimension=0, tiled=True)
    theirs = lax.ppermute(theirs, "head", [(0, 1), (1, 0)])
    projected = (mine.astype(f32) + theirs.astype(f32)).astype(bf16)
    return banded_out, projected.T


def solution(mesh):
    return jax.shard_map(
        body,
        mesh=mesh,
        in_specs=(
            P("ctx", "head"),
            P("ctx", "head"),
            P("ctx", "head"),
            P("ctx", "head"),
            P("ctx", "head"),
            P("ctx", "head"),
            P("ctx"),
            P("ctx"),
            P("head", None),
        ),
        out_specs=(P("ctx", "head"), P(("ctx", "head"), None)),
        check_vma=False,
    )
```

```python
import functools

import jax
import jax.numpy as jnp
from jax import lax
from jax.experimental import pallas as pl
from jax.experimental.pallas import tpu as pltpu
from jax.sharding import PartitionSpec as P


HEAD_DIM = 64
WINDOW = 128
REACH = 12
PLANE = 4
PAD = 16
AUG = 2 * HEAD_DIM
META = 16
BACK = 2
PICK_X = BACK + REACH // PLANE + 1
PICK_Y = PICK_X + 1
SIDE0 = PICK_X + 2
LATER = PICK_X + 3

theta_base = 150000.0
neg_fill = -1e30
to_log2 = HEAD_DIM ** (-0.5) * 1.4426950408889634

f32 = jnp.float32
bf16 = jnp.bfloat16
VM = pl.BlockSpec(memory_space=pltpu.VMEM)
SM = pl.BlockSpec(memory_space=pltpu.SMEM)


def al(start, size):
    return pl.ds(pl.multiple_of(start, size), size)


def rotate_rows(rows, cosine, sine_term):
    half = HEAD_DIM // 2
    out = []
    for at in range(0, rows.shape[0], HEAD_DIM):
        leading = rows[at : at + half]
        trailing = rows[at + half : at + HEAD_DIM]
        out.append(leading * cosine - trailing * sine_term)
        out.append(trailing * cosine + leading * sine_term)
    return jnp.concatenate(out, axis=0).astype(bf16)


def write_block(block, rows, id_rows, cos, sin):
    width = rows.shape[0] // 2
    block[0:width, :] = rotate_rows(rows[:width], cos, sin)
    block[width : width + PAD, :] = id_rows
    block[width + PAD :, :] = rows[width:].astype(bf16)


def prepare_kernel(base, side, frequency, kv, ids_pos, block, band_block, rim, meta, cosine, sine):
    tokens = kv.shape[0]
    angles = ids_pos[1:2, :].astype(f32) * frequency[...]
    cos, sin = jnp.cos(angles), jnp.sin(angles)
    cosine[...] = cos
    sine[...] = sin
    ids = ids_pos[0:1, :]
    shifted = ids + 1
    row = lax.broadcasted_iota(jnp.int32, (PAD, tokens), 0)
    high = jnp.broadcast_to(shifted >> 7, (PAD, tokens))
    low = jnp.broadcast_to(shifted & 127, (PAD, tokens))
    id_rows = jnp.where(row == 0, high, jnp.where(row == 1, low, 0)).astype(f32).astype(bf16)
    half = kv.shape[1] // 2
    write_block(block, kv[:, :half].astype(f32).T, id_rows, cos, sin)
    write_block(band_block, kv[:, half:].astype(f32).T, id_rows, cos, sin)
    rim[...] = band_block[:, tokens - WINDOW :]
    ids_f = ids.astype(f32)
    across = jnp.broadcast_to(ids_f, (tokens, tokens))
    down = across.T
    before = jnp.max(jnp.where(down < across, down, -1.0), axis=0, keepdims=True)
    first = before < 0.0
    begin = jnp.where(first, 0.0, before + 1.0 - base[0].astype(f32))
    here = base[0] // tokens
    plane = here // PLANE
    farthest = REACH // PLANE
    rows = [begin, first.astype(f32), ids_f + 1.0]
    rows += [plane >= back for back in range(1, farthest + 1)]
    rows += [(here % 2 == 1) | (plane >= farthest), (here // 2 % 2 == 1) | (plane >= farthest)]
    rows += [side[0] == 0, here > 0]
    mrow = lax.broadcasted_iota(jnp.int32, meta.shape, 0)
    total = jnp.zeros(meta.shape, f32)
    for i, value in enumerate(rows):
        value = jnp.where(value, 1.0, 0.0) if value.dtype == jnp.bool_ else value
        total = jnp.where(mrow == i, jnp.broadcast_to(value, meta.shape), total)
    meta[...] = total


def prepare(base, side, frequency, kv, ids_pos):
    tokens, every = kv.shape
    height = every // 2 + PAD
    half = HEAD_DIM // 2
    return pl.pallas_call(
        prepare_kernel,
        out_shape=(
            jax.ShapeDtypeStruct((height, tokens), bf16),
            jax.ShapeDtypeStruct((height, tokens), bf16),
            jax.ShapeDtypeStruct((height, WINDOW), bf16),
            jax.ShapeDtypeStruct((META, tokens), f32),
            jax.ShapeDtypeStruct((half, tokens), f32),
            jax.ShapeDtypeStruct((half, tokens), f32),
        ),
        in_specs=[SM] * 2 + [VM] * 3,
        out_specs=(VM,) * 6,
        compiler_params=pltpu.CompilerParams(vmem_limit_bytes=8 << 20),
        name="prepare",
    )(base, side, frequency, kv, ids_pos)


def two_deep(units, step, s0, s1, x0, x1):
    even, odd = (s0, x0), (s1, x1)
    step(-1, None, even)

    def pair(i, _):
        step(2 * i, even, odd)
        step(2 * i + 1, odd, even)
        return 0

    lax.fori_loop(0, units // 2 - 1, pair, 0)
    step(units - 2, even, odd)
    step(units - 1, odd, None)


def by_tiles(tiles, scores, outs):
    def step(u, now, then):
        for tile in range(tiles):
            if then is not None:
                scores(u + 1, tile, *then)
            if now is not None:
                outs(u, tile, *now)

    return step


def column_peak(s):
    return jnp.broadcast_to(jnp.max(s, axis=0, keepdims=True), (8, s.shape[1]))


def transposed_keys(rows, extra):
    return jnp.concatenate([rows.astype(f32), extra], axis=0).T.astype(bf16)


def ids_of(rows):
    rows = rows.astype(f32)
    return rows[0:1] * 128.0 + rows[1:2]


def mask_rows(ids, own_id, present):
    bar = jnp.where((ids < own_id) | jnp.logical_not(present), neg_fill, 0.0)
    row = lax.broadcasted_iota(jnp.int32, (HEAD_DIM, ids.shape[1]), 0)
    return jnp.where(row == 0, jnp.broadcast_to(bar, row.shape), jnp.where(row == 1, 1.0, 0.0))


def rotate_into(src, dst, cos, sin):
    wide = src.shape[1]
    step = min(wide, 4 * AUG)
    for at in range(0, wide, step):
        dst[at : at + step, :] = rotate_rows(src[:, at : at + step].astype(f32).T, cos, sin)


def own_kernel(group, fq, bq, cosine, sine, block, meta, fqt, bqt, peak, total, accum, keys, bias, s0, s1, x0, x1):
    tokens, wide = fq.shape
    width = wide // group
    kv = width // HEAD_DIM
    rotate_into(fq, fqt, cosine[...], sine[...])
    zero = jnp.zeros((HEAD_DIM, tokens), f32)
    for h in range(kv):
        keys[h * tokens : (h + 1) * tokens, :] = transposed_keys(block[h * HEAD_DIM : (h + 1) * HEAD_DIM, :], zero)
    begin = jnp.broadcast_to(meta[0:1, :], (tokens, tokens)).astype(jnp.int32)
    r = lax.broadcasted_iota(jnp.int32, (tokens, tokens), 0)
    t = lax.broadcasted_iota(jnp.int32, (tokens, tokens), 1)
    bias[...] = jnp.where((r >= begin) & (r <= t), 0.0, neg_fill)
    several = s0.shape[0] // tokens

    def scores(u, g, buf, x):
        h = u * several // group
        k = keys[al(h * tokens, tokens), :][:, :HEAD_DIM]
        q = fqt[al((u * several + g) * HEAD_DIM, HEAD_DIM), :]
        s = jnp.dot(k, q, preferred_element_type=f32) + bias[...]
        buf[g * tokens : (g + 1) * tokens, :] = s
        x[8 * g : 8 * g + 8, :] = column_peak(s)

    def outs(u, g, buf, x):
        h = u * several // group
        v = block[pl.ds(pl.multiple_of(width + PAD + h * HEAD_DIM, PAD), HEAD_DIM), :]
        at = u * several + g
        m = x[8 * g : 8 * g + 1, :]
        p = jnp.exp2(buf[g * tokens : (g + 1) * tokens, :] * to_log2 - m * to_log2)
        peak[pl.ds(at, 1), :] = m
        total[pl.ds(at, 1), :] = jnp.sum(p, axis=0, keepdims=True)
        accum[al(at * HEAD_DIM, HEAD_DIM), :] = jnp.dot(v, p.astype(bf16), preferred_element_type=f32)

    two_deep(wide // HEAD_DIM // several, by_tiles(several, scores, outs), s0, s1, x0, x1)
    rotate_into(bq, bqt, cosine[...], sine[...])


def own(group, fq, bq, cosine, sine, block, meta):
    tokens, wide = fq.shape
    heads = wide // HEAD_DIM
    kv = heads // group
    several = 4
    return pl.pallas_call(
        functools.partial(own_kernel, group),
        out_shape=(
            jax.ShapeDtypeStruct((wide, tokens), bf16),
            jax.ShapeDtypeStruct((wide, tokens), bf16),
            jax.ShapeDtypeStruct((heads, tokens), f32),
            jax.ShapeDtypeStruct((heads, tokens), f32),
            jax.ShapeDtypeStruct((wide, tokens), f32),
        ),
        in_specs=[VM] * 6,
        out_specs=(VM,) * 5,
        scratch_shapes=[
            pltpu.VMEM((kv * tokens, AUG), bf16),
            pltpu.VMEM((tokens, tokens), f32),
            pltpu.VMEM((several * tokens, tokens), f32),
            pltpu.VMEM((several * tokens, tokens), f32),
            pltpu.VMEM((8 * several, tokens), f32),
            pltpu.VMEM((8 * several, tokens), f32),
        ],
        compiler_params=pltpu.CompilerParams(vmem_limit_bytes=16 << 20),
        cost_estimate=pl.CostEstimate(
            flops=4 * heads * tokens * tokens * HEAD_DIM * 4, transcendentals=heads * tokens * tokens, bytes_accessed=12 * wide * tokens
        ),
        name="own",
    )(fq, bq, cosine, sine, block, meta)


def band_kernel(group, bqt, block, rim, meta, out, keys, vals, bias, s0, s1, x0, x1):
    wide, tokens = bqt.shape
    width = wide // group
    kv = width // HEAD_DIM
    span = tokens + WINDOW
    tile = 2 * WINDOW
    zero = jnp.zeros((HEAD_DIM, tokens), f32)
    for h in range(kv):
        rows = slice(h * HEAD_DIM, (h + 1) * HEAD_DIM)
        keys[h * span : h * span + WINDOW, :] = transposed_keys(rim[rows, :], zero[:, :WINDOW])
        keys[h * span + WINDOW : (h + 1) * span, :] = transposed_keys(block[rows, :], zero)
    vals[:, :WINDOW] = rim[width + PAD :, :]
    vals[:, WINDOW:] = block[width + PAD :, :]
    own_id = jnp.min(meta[2:3, :])
    barred = (ids_of(rim[width : width + PAD, :]) < own_id) | (meta[LATER : LATER + 1, :WINDOW] == 0.0)
    barred = jnp.sum(barred.astype(f32))
    begin = meta[0:1, :]
    first = meta[1:2, :]
    r = lax.broadcasted_iota(jnp.int32, (tile, tile), 0).astype(f32)
    t = (lax.broadcasted_iota(jnp.int32, (1, tile), 1) & (WINDOW - 1)).astype(f32)
    halves = tokens // WINDOW
    for half in range(halves):
        lo = begin + float(WINDOW - half * WINDOW)
        if half == 0:
            lo = jnp.where(first > 0.0, barred, lo)
        lo = lo[:, half * WINDOW : (half + 1) * WINDOW]
        low = jnp.maximum(jnp.concatenate([lo, lo], axis=1), t + 1.0)
        bias[half * tile : (half + 1) * tile, :] = jnp.where((r >= low) & (r <= t + WINDOW), 0.0, neg_fill)
    pairs = group // 2
    several = s0.shape[0] // tile // halves

    def scores(u, at, buf, x):
        half, g = divmod(at, several)
        h = u * several // pairs
        k = keys[pl.ds(pl.multiple_of(h * span + half * WINDOW, WINDOW), tile), :][:, :HEAD_DIM]
        q = bqt[al((u * several + g) * AUG, AUG), :][:, half * WINDOW : (half + 1) * WINDOW]
        q = jnp.concatenate([q[:HEAD_DIM], q[HEAD_DIM:]], axis=1)
        s = jnp.dot(k, q, preferred_element_type=f32) + bias[half * tile : (half + 1) * tile, :]
        buf[at * tile : (at + 1) * tile, :] = s
        x[8 * at : 8 * at + 8, :] = column_peak(s)

    def outs(u, at, buf, x):
        half, g = divmod(at, several)
        h = u * several // pairs
        v = vals[al(h * HEAD_DIM, HEAD_DIM), half * WINDOW : half * WINDOW + tile]
        m = x[8 * at : 8 * at + 1, :]
        p = jnp.exp2(buf[at * tile : (at + 1) * tile, :] * to_log2 - m * to_log2)
        total = jnp.sum(p, axis=0, keepdims=True)
        o = jnp.dot(v, p.astype(bf16), preferred_element_type=f32) / total
        o = jnp.concatenate([o[:, :WINDOW], o[:, WINDOW:]], axis=0)
        out[half * WINDOW : (half + 1) * WINDOW, al((u * several + g) * AUG, AUG)] = o.T.astype(bf16)

    two_deep(kv * pairs // several, by_tiles(halves * several, scores, outs), s0, s1, x0, x1)


def band(group, bqt, block, rim, meta):
    wide, tokens = bqt.shape
    kv = wide // group // HEAD_DIM
    span = tokens + WINDOW
    several = 2
    tiles = several * (tokens // WINDOW)
    return pl.pallas_call(
        functools.partial(band_kernel, group),
        out_shape=jax.ShapeDtypeStruct((tokens, wide), bf16),
        in_specs=[VM] * 4,
        out_specs=VM,
        scratch_shapes=[
            pltpu.VMEM((kv * span, AUG), bf16),
            pltpu.VMEM((kv * HEAD_DIM, span), bf16),
            pltpu.VMEM((tokens // WINDOW * 2 * WINDOW, 2 * WINDOW), f32),
            pltpu.VMEM((tiles * 2 * WINDOW, 2 * WINDOW), f32),
            pltpu.VMEM((tiles * 2 * WINDOW, 2 * WINDOW), f32),
            pltpu.VMEM((8 * tiles, 2 * WINDOW), f32),
            pltpu.VMEM((8 * tiles, 2 * WINDOW), f32),
        ],
        compiler_params=pltpu.CompilerParams(vmem_limit_bytes=16 << 20),
        cost_estimate=pl.CostEstimate(
            flops=4 * wide * tokens * 2 * WINDOW * 4, transcendentals=wide // HEAD_DIM * tokens * 2 * WINDOW, bytes_accessed=4 * wide * tokens
        ),
        name="band",
    )(bqt, block, rim, meta)


def remote_update(group, fqt, shards, meta, state_in, state_out, keys, s0, s1, x0, x1):
    wide, tokens = fqt.shape
    width = wide // group
    kv = width // HEAD_DIM
    span = len(shards) * tokens
    peak_in, total_in, accum_in = state_in
    peak, total, accum = state_out
    own_id = jnp.min(meta[2:3, :])
    for b, (kref, krow, _, _, flag) in enumerate(shards):
        extra = mask_rows(ids_of(kref[krow + width : krow + width + PAD, :]), own_id, meta[flag : flag + 1, :] > 0.0)
        for h in range(kv):
            rows = kref[krow + h * HEAD_DIM : krow + (h + 1) * HEAD_DIM, :]
            keys[h * span + b * tokens : h * span + (b + 1) * tokens, :] = transposed_keys(rows, extra)
    row = lax.broadcasted_iota(jnp.int32, (HEAD_DIM, tokens), 0)
    other = jnp.where(meta[1:2, :] > 0.0, 0.0, neg_fill)
    query_rows = jnp.where(row == 0, 1.0, jnp.where(row == 1, jnp.broadcast_to(other, row.shape), 0.0)).astype(bf16)

    several = s0.shape[0] // span

    def step(u, now, then):
        h = u * several // group
        h_then = (u + 1) * several // group
        for g in range(several):
            top = None
            if then is not None:
                at = (u + 1) * several + g
                q = jnp.concatenate([fqt[al(at * HEAD_DIM, HEAD_DIM), :], query_rows], axis=0)
            if now is not None:
                buf, x = now
                at = u * several + g
                rows = al(at * HEAD_DIM, HEAD_DIM)
                old = peak_in[pl.ds(at, 1), :]
                m = jnp.maximum(old, x[8 * g : 8 * g + 1, :])
                scaled = m * to_log2
                factor = jnp.exp2(old * to_log2 - scaled)
                peak[pl.ds(at, 1), :] = m
                t = total_in[pl.ds(at, 1), :] * factor
                a = accum_in[rows, :] * factor
            for b, (_, _, vref, vrow, _) in enumerate(shards):
                where = slice(g * span + b * tokens, g * span + (b + 1) * tokens)
                if then is not None:
                    k = keys[pl.ds(pl.multiple_of(h_then * span + b * tokens, tokens), tokens), :]
                    s = jnp.dot(k, q, preferred_element_type=f32)
                    then[0][where, :] = s
                    high = jnp.max(s.reshape(tokens // 8, 8, tokens), axis=0)
                    top = high if top is None else jnp.maximum(top, high)
                if now is not None:
                    p = jnp.exp2(buf[where, :] * to_log2 - scaled)
                    t = t + jnp.sum(p, axis=0, keepdims=True)
                    v = vref[pl.ds(pl.multiple_of(vrow + h * HEAD_DIM, PAD), HEAD_DIM), :]
                    a = a + jnp.dot(v, p.astype(bf16), preferred_element_type=f32)
            if then is not None:
                then[1][8 * g : 8 * g + 8, :] = column_peak(top)
            if now is not None:
                total[pl.ds(at, 1), :] = t
                accum[rows, :] = a

    two_deep(wide // HEAD_DIM // several, step, s0, s1, x0, x1)


def remote_scratch(kv, tokens, count):
    span = count * tokens
    several = 4 if count < 3 else 2
    return [
        pltpu.VMEM((kv * span, AUG), bf16),
        pltpu.VMEM((several * span, tokens), f32),
        pltpu.VMEM((several * span, tokens), f32),
        pltpu.VMEM((8 * several, tokens), f32),
        pltpu.VMEM((8 * several, tokens), f32),
    ]


def placed(shards, refs):
    return [(refs[ka], kr, refs[va], vr, flag) for ka, kr, va, vr, flag in shards]


def remote_kernel(group, shards, n, fqt, *refs):
    meta, peak_in, total_in, accum_in, peak, total, accum = refs[n : n + 7]
    remote_update(group, fqt, placed(shards, refs), meta, (peak_in, total_in, accum_in), (peak, total, accum), *refs[n + 7 :])


def remote(group, fqt, arrays, shards, meta, state):
    wide, tokens = fqt.shape
    heads = wide // HEAD_DIM
    count = len(shards)
    n = len(arrays)
    return pl.pallas_call(
        functools.partial(remote_kernel, group, shards, n),
        out_shape=tuple(jax.ShapeDtypeStruct(x.shape, x.dtype) for x in state),
        in_specs=[VM] * (n + 5),
        out_specs=(VM,) * 3,
        scratch_shapes=remote_scratch(heads // group, tokens, count),
        input_output_aliases={n + 2 + i: i for i in range(3)},
        compiler_params=pltpu.CompilerParams(vmem_limit_bytes=16 << 20),
        cost_estimate=pl.CostEstimate(
            flops=4 * wide * tokens * tokens * count * 4, transcendentals=heads * tokens * tokens * count, bytes_accessed=20 * wide * tokens
        ),
        name="remote",
    )(fqt, *arrays, meta, *state)


def last_kernel(group, shards, n, fqt, *refs):
    meta, peak_in, total_in, accum_in, held, mine, theirs = refs[n : n + 7]
    keys, s0, s1, x0, x1, peak, total, accum, mixed = refs[n + 7 :]
    remote_update(group, fqt, placed(shards, refs), meta, (peak_in, total_in, accum_in), (peak, total, accum), keys, s0, s1, x0, x1)
    wide, tokens = fqt.shape
    rows = tokens // 2
    for u in range(wide // HEAD_DIM):
        at = slice(u * HEAD_DIM, (u + 1) * HEAD_DIM)
        mixed[at, :] = (accum[at, :] / total[u : u + 1, :]).astype(bf16)
    first = meta[SIDE0 : SIDE0 + 1, :rows] > 0.0
    columns = held.shape[0]
    step = 4 * AUG
    for at in range(0, columns, step):
        size = min(step, columns - at)
        part = jnp.dot(held[at : at + size, :], mixed[...], preferred_element_type=f32).astype(bf16)
        low, high = part[:, :rows], part[:, rows:]
        mine[at : at + size, :] = jnp.where(first, low, high)
        theirs[at : at + size, :] = jnp.where(first, high, low)


def last(group, fqt, arrays, shards, meta, state, weight):
    wide, tokens = fqt.shape
    heads = wide // HEAD_DIM
    count = len(shards)
    n = len(arrays)
    return pl.pallas_call(
        functools.partial(last_kernel, group, shards, n),
        out_shape=(jax.ShapeDtypeStruct((weight.shape[0], tokens // 2), bf16),) * 2,
        in_specs=[VM] * (n + 6),
        out_specs=(VM, VM),
        scratch_shapes=remote_scratch(heads // group, tokens, count)
        + [
            pltpu.VMEM((heads, tokens), f32),
            pltpu.VMEM((heads, tokens), f32),
            pltpu.VMEM((wide, tokens), f32),
            pltpu.VMEM((wide, tokens), bf16),
        ],
        compiler_params=pltpu.CompilerParams(vmem_limit_bytes=28 << 20),
        cost_estimate=pl.CostEstimate(
            flops=4 * wide * tokens * tokens * count * 4, transcendentals=heads * tokens * tokens * count, bytes_accessed=20 * wide * tokens
        ),
        name="last",
    )(fqt, *arrays, meta, *state, weight)


def shifted_by(block, distance):
    size = lax.axis_size("ctx")
    return lax.ppermute(block, "ctx", [(i, (i + distance) % size) for i in range(size)])


def relayed(block):
    size = lax.axis_size("ctx")
    planes = size // PLANE
    target = {plane: plane + 2 for plane in range(1, planes - 2)}
    target.update({0: 0, planes - 1: 1, planes - 2: 2} if planes > 3 else {plane: plane for plane in range(planes)})
    return lax.ppermute(block, "ctx", [(i, target[i // PLANE] * PLANE + i % PLANE) for i in range(size)])


def swapped(block, bit):
    size = lax.axis_size("ctx")
    return lax.ppermute(block, "ctx", [(i, i ^ bit) for i in range(size)])


def body(banded_queries, banded_keys, banded_values, full_queries, full_keys, full_values, segment_ids, position_ids, out_weight):
    tokens = segment_ids.shape[0]
    width = full_keys.shape[1]
    height = 2 * width + PAD
    vrow = width + PAD
    group = banded_queries.shape[1] // banded_keys.shape[1]
    here = lax.axis_index("ctx")
    half = HEAD_DIM // 2
    frequency = theta_base ** (-2.0 * jnp.arange(half, dtype=f32) / HEAD_DIM)
    frequency = jnp.broadcast_to(frequency[:, None], (half, tokens))
    base = (here * tokens).astype(jnp.int32).reshape(1)
    side = lax.axis_index("head").astype(jnp.int32)

    kv = jnp.concatenate([full_keys, full_values, banded_keys, banded_values], axis=1)
    ids_pos = jnp.stack([segment_ids, position_ids])
    block, band_kv, rim, meta, cosine, sine = prepare(base, side.reshape(1), frequency, kv, ids_pos)
    z1 = shifted_by(block, PLANE)
    fqt, bqt, *state = own(group, full_queries, banded_queries, cosine, sine, block, meta)
    z1, rim, block, state = lax.optimization_barrier((z1, rim, block, state))

    rim = shifted_by(rim, 1)
    z3 = relayed(z1)
    z2 = shifted_by(z1, PLANE)
    x1 = swapped(z1, 1)
    y1 = swapped(z1, 2)
    state = remote(group, fqt, [z1], ((0, 0, 0, vrow, BACK + 1),), meta, state)
    rim, state = lax.optimization_barrier((rim, state))
    banded_out = band(group, bqt, band_kv, rim, meta)
    z2, z3, block, state, banded_out = lax.optimization_barrier((z2, z3, block, state, banded_out))

    def farthest(bit):
        return jnp.where((here & bit) == 0, block, z3)

    x2 = swapped(jnp.concatenate([z2, farthest(1)]), 1)
    y2 = swapped(jnp.concatenate([z2, farthest(2)]), 2)
    z2, z3, x1, y1 = lax.optimization_barrier((z2, z3, x1, y1))
    state = remote(group, fqt, [x1, y1, z2, z3], tuple((a, 0, a, vrow, flag) for a, flag in enumerate((BACK + 1, BACK + 1, BACK + 2, BACK + 3))), meta, state)
    x2, y2, state = lax.optimization_barrier((x2, y2, state))

    dx = swapped(jnp.concatenate([y1[:vrow], y2[height:]]), 1)
    dy = swapped(jnp.concatenate([x1[vrow:], x2[:height]]), 2)
    state = remote(
        group,
        fqt,
        [x2, y2],
        ((0, 0, 0, vrow, BACK + 2), (0, height, 0, height + vrow, PICK_X), (1, 0, 1, vrow, BACK + 2), (1, height, 1, height + vrow, PICK_Y)),
        meta,
        state,
    )
    dx, dy, state = lax.optimization_barrier((dx, dy, state))
    mine, theirs = last(
        group,
        fqt,
        [dx, dy],
        ((0, 0, 1, 0, BACK + 1), (0, vrow, 0, 2 * vrow, PICK_Y), (1, width, 1, width + vrow, BACK + 2)),
        meta,
        state,
        out_weight.T,
    )

    sides = lax.axis_size("head")
    if sides != 2:
        part = jnp.concatenate([jnp.where(side == 0, mine, theirs), jnp.where(side == 0, theirs, mine)], axis=1).T
        return banded_out, lax.psum_scatter(part, "head", scatter_dimension=0, tiled=True)
    theirs = lax.ppermute(theirs, "head", [(0, 1), (1, 0)])
    projected = (mine.astype(f32) + theirs.astype(f32)).astype(bf16)
    return banded_out, projected.T


def solution(mesh):
    return jax.shard_map(
        body,
        mesh=mesh,
        in_specs=(
            P("ctx", "head"),
            P("ctx", "head"),
            P("ctx", "head"),
            P("ctx", "head"),
            P("ctx", "head"),
            P("ctx", "head"),
            P("ctx"),
            P("ctx"),
            P("head", None),
        ),
        out_specs=(P("ctx", "head"), P(("ctx", "head"), None)),
        check_vma=False,
    )
```

```python
import functools

import jax
import jax.numpy as jnp
from jax import lax
from jax.experimental import pallas as pl
from jax.experimental.pallas import tpu as pltpu
from jax.sharding import PartitionSpec as P


HEAD_DIM = 64
WINDOW = 128
REACH = 12
PLANE = 4
PAD = 16
AUG = 2 * HEAD_DIM
META = 16
BACK = 2
PICK_X = BACK + REACH // PLANE + 1
PICK_Y = PICK_X + 1
SIDE0 = PICK_X + 2
LATER = PICK_X + 3

theta_base = 150000.0
neg_fill = -1e30
to_log2 = HEAD_DIM ** (-0.5) * 1.4426950408889634

f32 = jnp.float32
bf16 = jnp.bfloat16
VM = pl.BlockSpec(memory_space=pltpu.VMEM)
SM = pl.BlockSpec(memory_space=pltpu.SMEM)


def al(start, size):
    return pl.ds(pl.multiple_of(start, size), size)


def rotate_rows(rows, cosine, sine_term):
    half = HEAD_DIM // 2
    out = []
    for at in range(0, rows.shape[0], HEAD_DIM):
        leading = rows[at : at + half]
        trailing = rows[at + half : at + HEAD_DIM]
        out.append(leading * cosine - trailing * sine_term)
        out.append(trailing * cosine + leading * sine_term)
    return jnp.concatenate(out, axis=0).astype(bf16)


def write_block(block, rows, id_rows, cos, sin):
    width = rows.shape[0] // 2
    block[0:width, :] = rotate_rows(rows[:width], cos, sin)
    block[width : width + PAD, :] = id_rows
    block[width + PAD :, :] = rows[width:].astype(bf16)


def prepare_kernel(base, side, frequency, kv, ids_pos, block, band_block, rim, meta, cosine, sine):
    tokens = kv.shape[0]
    angles = ids_pos[1:2, :].astype(f32) * frequency[...]
    cos, sin = jnp.cos(angles), jnp.sin(angles)
    cosine[...] = cos
    sine[...] = sin
    ids = ids_pos[0:1, :]
    shifted = ids + 1
    row = lax.broadcasted_iota(jnp.int32, (PAD, tokens), 0)
    high = jnp.broadcast_to(shifted >> 7, (PAD, tokens))
    low = jnp.broadcast_to(shifted & 127, (PAD, tokens))
    id_rows = jnp.where(row == 0, high, jnp.where(row == 1, low, 0)).astype(f32).astype(bf16)
    half = kv.shape[1] // 2
    write_block(block, kv[:, :half].astype(f32).T, id_rows, cos, sin)
    write_block(band_block, kv[:, half:].astype(f32).T, id_rows, cos, sin)
    rim[...] = band_block[:, tokens - WINDOW :]
    ids_f = ids.astype(f32)
    across = jnp.broadcast_to(ids_f, (tokens, tokens))
    down = across.T
    before = jnp.max(jnp.where(down < across, down, -1.0), axis=0, keepdims=True)
    first = before < 0.0
    begin = jnp.where(first, 0.0, before + 1.0 - base[0].astype(f32))
    here = base[0] // tokens
    plane = here // PLANE
    farthest = REACH // PLANE
    rows = [begin, first.astype(f32), ids_f + 1.0]
    rows += [plane >= back for back in range(1, farthest + 1)]
    rows += [(here % 2 == 1) | (plane >= farthest), (here // 2 % 2 == 1) | (plane >= farthest)]
    rows += [side[0] == 0, here > 0]
    mrow = lax.broadcasted_iota(jnp.int32, meta.shape, 0)
    total = jnp.zeros(meta.shape, f32)
    for i, value in enumerate(rows):
        value = jnp.where(value, 1.0, 0.0) if value.dtype == jnp.bool_ else value
        total = jnp.where(mrow == i, jnp.broadcast_to(value, meta.shape), total)
    meta[...] = total


def prepare(base, side, frequency, kv, ids_pos):
    tokens, every = kv.shape
    height = every // 2 + PAD
    half = HEAD_DIM // 2
    return pl.pallas_call(
        prepare_kernel,
        out_shape=(
            jax.ShapeDtypeStruct((height, tokens), bf16),
            jax.ShapeDtypeStruct((height, tokens), bf16),
            jax.ShapeDtypeStruct((height, WINDOW), bf16),
            jax.ShapeDtypeStruct((META, tokens), f32),
            jax.ShapeDtypeStruct((half, tokens), f32),
            jax.ShapeDtypeStruct((half, tokens), f32),
        ),
        in_specs=[SM] * 2 + [VM] * 3,
        out_specs=(VM,) * 6,
        compiler_params=pltpu.CompilerParams(vmem_limit_bytes=8 << 20),
        name="prepare",
    )(base, side, frequency, kv, ids_pos)


def two_deep(units, step, s0, s1, x0, x1):
    even, odd = (s0, x0), (s1, x1)
    step(-1, None, even)

    def pair(i, _):
        step(2 * i, even, odd)
        step(2 * i + 1, odd, even)
        return 0

    lax.fori_loop(0, units // 2 - 1, pair, 0)
    step(units - 2, even, odd)
    step(units - 1, odd, None)


def by_tiles(tiles, scores, outs):
    def step(u, now, then):
        for tile in range(tiles):
            if then is not None:
                scores(u + 1, tile, *then)
            if now is not None:
                outs(u, tile, *now)

    return step


def column_peak(s):
    return jnp.broadcast_to(jnp.max(s, axis=0, keepdims=True), (8, s.shape[1]))


def transposed_keys(rows, extra):
    return jnp.concatenate([rows.astype(f32), extra], axis=0).T.astype(bf16)


def ids_of(rows):
    rows = rows.astype(f32)
    return rows[0:1] * 128.0 + rows[1:2]


def mask_rows(ids, own_id, present):
    bar = jnp.where((ids < own_id) | jnp.logical_not(present), neg_fill, 0.0)
    row = lax.broadcasted_iota(jnp.int32, (HEAD_DIM, ids.shape[1]), 0)
    return jnp.where(row == 0, jnp.broadcast_to(bar, row.shape), jnp.where(row == 1, 1.0, 0.0))


def rotate_into(src, dst, cos, sin):
    wide = src.shape[1]
    step = min(wide, 4 * AUG)
    for at in range(0, wide, step):
        dst[at : at + step, :] = rotate_rows(src[:, at : at + step].astype(f32).T, cos, sin)


def own_kernel(group, fq, bq, cosine, sine, block, meta, fqt, bqt, peak, total, accum, keys, bias, s0, s1, x0, x1):
    tokens, wide = fq.shape
    width = wide // group
    kv = width // HEAD_DIM
    rotate_into(fq, fqt, cosine[...], sine[...])
    zero = jnp.zeros((HEAD_DIM, tokens), f32)
    for h in range(kv):
        keys[h * tokens : (h + 1) * tokens, :] = transposed_keys(block[h * HEAD_DIM : (h + 1) * HEAD_DIM, :], zero)
    begin = jnp.broadcast_to(meta[0:1, :], (tokens, tokens)).astype(jnp.int32)
    r = lax.broadcasted_iota(jnp.int32, (tokens, tokens), 0)
    t = lax.broadcasted_iota(jnp.int32, (tokens, tokens), 1)
    bias[...] = jnp.where((r >= begin) & (r <= t), 0.0, neg_fill)
    several = s0.shape[0] // tokens

    def scores(u, g, buf, x):
        h = u * several // group
        k = keys[al(h * tokens, tokens), :][:, :HEAD_DIM]
        q = fqt[al((u * several + g) * HEAD_DIM, HEAD_DIM), :]
        s = jnp.dot(k, q, preferred_element_type=f32) + bias[...]
        buf[g * tokens : (g + 1) * tokens, :] = s
        x[8 * g : 8 * g + 8, :] = column_peak(s)

    def outs(u, g, buf, x):
        h = u * several // group
        v = block[pl.ds(pl.multiple_of(width + PAD + h * HEAD_DIM, PAD), HEAD_DIM), :]
        at = u * several + g
        m = x[8 * g : 8 * g + 1, :]
        p = jnp.exp2(buf[g * tokens : (g + 1) * tokens, :] * to_log2 - m * to_log2)
        peak[pl.ds(at, 1), :] = m
        total[pl.ds(at, 1), :] = jnp.sum(p, axis=0, keepdims=True)
        accum[al(at * HEAD_DIM, HEAD_DIM), :] = jnp.dot(v, p.astype(bf16), preferred_element_type=f32)

    two_deep(wide // HEAD_DIM // several, by_tiles(several, scores, outs), s0, s1, x0, x1)
    rotate_into(bq, bqt, cosine[...], sine[...])


def own(group, fq, bq, cosine, sine, block, meta):
    tokens, wide = fq.shape
    heads = wide // HEAD_DIM
    kv = heads // group
    several = 4
    return pl.pallas_call(
        functools.partial(own_kernel, group),
        out_shape=(
            jax.ShapeDtypeStruct((wide, tokens), bf16),
            jax.ShapeDtypeStruct((wide, tokens), bf16),
            jax.ShapeDtypeStruct((heads, tokens), f32),
            jax.ShapeDtypeStruct((heads, tokens), f32),
            jax.ShapeDtypeStruct((wide, tokens), f32),
        ),
        in_specs=[VM] * 6,
        out_specs=(VM,) * 5,
        scratch_shapes=[
            pltpu.VMEM((kv * tokens, AUG), bf16),
            pltpu.VMEM((tokens, tokens), f32),
            pltpu.VMEM((several * tokens, tokens), f32),
            pltpu.VMEM((several * tokens, tokens), f32),
            pltpu.VMEM((8 * several, tokens), f32),
            pltpu.VMEM((8 * several, tokens), f32),
        ],
        compiler_params=pltpu.CompilerParams(vmem_limit_bytes=16 << 20),
        cost_estimate=pl.CostEstimate(
            flops=4 * heads * tokens * tokens * HEAD_DIM * 4, transcendentals=heads * tokens * tokens, bytes_accessed=12 * wide * tokens
        ),
        name="own",
    )(fq, bq, cosine, sine, block, meta)


def band_kernel(group, bqt, block, rim, meta, out, keys, vals, bias, s0, s1, x0, x1):
    wide, tokens = bqt.shape
    width = wide // group
    kv = width // HEAD_DIM
    span = tokens + WINDOW
    tile = 2 * WINDOW
    zero = jnp.zeros((HEAD_DIM, tokens), f32)
    for h in range(kv):
        rows = slice(h * HEAD_DIM, (h + 1) * HEAD_DIM)
        keys[h * span : h * span + WINDOW, :] = transposed_keys(rim[rows, :], zero[:, :WINDOW])
        keys[h * span + WINDOW : (h + 1) * span, :] = transposed_keys(block[rows, :], zero)
    vals[:, :WINDOW] = rim[width + PAD :, :]
    vals[:, WINDOW:] = block[width + PAD :, :]
    own_id = jnp.min(meta[2:3, :])
    barred = (ids_of(rim[width : width + PAD, :]) < own_id) | (meta[LATER : LATER + 1, :WINDOW] == 0.0)
    barred = jnp.sum(barred.astype(f32))
    begin = meta[0:1, :]
    first = meta[1:2, :]
    r = lax.broadcasted_iota(jnp.int32, (tile, tile), 0).astype(f32)
    t = (lax.broadcasted_iota(jnp.int32, (1, tile), 1) & (WINDOW - 1)).astype(f32)
    halves = tokens // WINDOW
    for half in range(halves):
        lo = begin + float(WINDOW - half * WINDOW)
        if half == 0:
            lo = jnp.where(first > 0.0, barred, lo)
        lo = lo[:, half * WINDOW : (half + 1) * WINDOW]
        low = jnp.maximum(jnp.concatenate([lo, lo], axis=1), t + 1.0)
        bias[half * tile : (half + 1) * tile, :] = jnp.where((r >= low) & (r <= t + WINDOW), 0.0, neg_fill)
    pairs = group // 2
    several = s0.shape[0] // tile // halves

    def scores(u, at, buf, x):
        half, g = divmod(at, several)
        h = u * several // pairs
        k = keys[pl.ds(pl.multiple_of(h * span + half * WINDOW, WINDOW), tile), :][:, :HEAD_DIM]
        q = bqt[al((u * several + g) * AUG, AUG), :][:, half * WINDOW : (half + 1) * WINDOW]
        q = jnp.concatenate([q[:HEAD_DIM], q[HEAD_DIM:]], axis=1)
        s = jnp.dot(k, q, preferred_element_type=f32) + bias[half * tile : (half + 1) * tile, :]
        buf[at * tile : (at + 1) * tile, :] = s
        x[8 * at : 8 * at + 8, :] = column_peak(s)

    def outs(u, at, buf, x):
        half, g = divmod(at, several)
        h = u * several // pairs
        v = vals[al(h * HEAD_DIM, HEAD_DIM), half * WINDOW : half * WINDOW + tile]
        m = x[8 * at : 8 * at + 1, :]
        p = jnp.exp2(buf[at * tile : (at + 1) * tile, :] * to_log2 - m * to_log2)
        total = jnp.sum(p, axis=0, keepdims=True)
        o = jnp.dot(v, p.astype(bf16), preferred_element_type=f32) / total
        o = jnp.concatenate([o[:, :WINDOW], o[:, WINDOW:]], axis=0)
        out[half * WINDOW : (half + 1) * WINDOW, al((u * several + g) * AUG, AUG)] = o.T.astype(bf16)

    two_deep(kv * pairs // several, by_tiles(halves * several, scores, outs), s0, s1, x0, x1)


def band(group, bqt, block, rim, meta):
    wide, tokens = bqt.shape
    kv = wide // group // HEAD_DIM
    span = tokens + WINDOW
    several = 2
    tiles = several * (tokens // WINDOW)
    return pl.pallas_call(
        functools.partial(band_kernel, group),
        out_shape=jax.ShapeDtypeStruct((tokens, wide), bf16),
        in_specs=[VM] * 4,
        out_specs=VM,
        scratch_shapes=[
            pltpu.VMEM((kv * span, AUG), bf16),
            pltpu.VMEM((kv * HEAD_DIM, span), bf16),
            pltpu.VMEM((tokens // WINDOW * 2 * WINDOW, 2 * WINDOW), f32),
            pltpu.VMEM((tiles * 2 * WINDOW, 2 * WINDOW), f32),
            pltpu.VMEM((tiles * 2 * WINDOW, 2 * WINDOW), f32),
            pltpu.VMEM((8 * tiles, 2 * WINDOW), f32),
            pltpu.VMEM((8 * tiles, 2 * WINDOW), f32),
        ],
        compiler_params=pltpu.CompilerParams(vmem_limit_bytes=16 << 20),
        cost_estimate=pl.CostEstimate(
            flops=4 * wide * tokens * 2 * WINDOW * 4, transcendentals=wide // HEAD_DIM * tokens * 2 * WINDOW, bytes_accessed=4 * wide * tokens
        ),
        name="band",
    )(bqt, block, rim, meta)


def remote_update(group, fqt, shards, meta, state_in, state_out, keys, s0, s1, x0, x1):
    wide, tokens = fqt.shape
    width = wide // group
    kv = width // HEAD_DIM
    span = len(shards) * tokens
    peak_in, total_in, accum_in = state_in
    peak, total, accum = state_out
    own_id = jnp.min(meta[2:3, :])
    for b, (kref, krow, _, _, flag) in enumerate(shards):
        extra = mask_rows(ids_of(kref[krow + width : krow + width + PAD, :]), own_id, meta[flag : flag + 1, :] > 0.0)
        for h in range(kv):
            rows = kref[krow + h * HEAD_DIM : krow + (h + 1) * HEAD_DIM, :]
            keys[h * span + b * tokens : h * span + (b + 1) * tokens, :] = transposed_keys(rows, extra)
    row = lax.broadcasted_iota(jnp.int32, (HEAD_DIM, tokens), 0)
    other = jnp.where(meta[1:2, :] > 0.0, 0.0, neg_fill)
    query_rows = jnp.where(row == 0, 1.0, jnp.where(row == 1, jnp.broadcast_to(other, row.shape), 0.0)).astype(bf16)

    several = s0.shape[0] // span

    def step(u, now, then):
        h = u * several // group
        h_then = (u + 1) * several // group
        for g in range(several):
            top = None
            if then is not None:
                at = (u + 1) * several + g
                q = jnp.concatenate([fqt[al(at * HEAD_DIM, HEAD_DIM), :], query_rows], axis=0)
            if now is not None:
                buf, x = now
                at = u * several + g
                rows = al(at * HEAD_DIM, HEAD_DIM)
                old = peak_in[pl.ds(at, 1), :]
                m = jnp.maximum(old, x[8 * g : 8 * g + 1, :])
                scaled = m * to_log2
                factor = jnp.exp2(old * to_log2 - scaled)
                peak[pl.ds(at, 1), :] = m
                t = total_in[pl.ds(at, 1), :] * factor
                a = accum_in[rows, :] * factor
            for b, (_, _, vref, vrow, _) in enumerate(shards):
                where = slice(g * span + b * tokens, g * span + (b + 1) * tokens)
                if then is not None:
                    k = keys[pl.ds(pl.multiple_of(h_then * span + b * tokens, tokens), tokens), :]
                    s = jnp.dot(k, q, preferred_element_type=f32)
                    then[0][where, :] = s
                    high = jnp.max(s.reshape(tokens // 8, 8, tokens), axis=0)
                    top = high if top is None else jnp.maximum(top, high)
                if now is not None:
                    p = jnp.exp2(buf[where, :] * to_log2 - scaled)
                    t = t + jnp.sum(p, axis=0, keepdims=True)
                    v = vref[pl.ds(pl.multiple_of(vrow + h * HEAD_DIM, PAD), HEAD_DIM), :]
                    a = a + jnp.dot(v, p.astype(bf16), preferred_element_type=f32)
            if then is not None:
                then[1][8 * g : 8 * g + 8, :] = column_peak(top)
            if now is not None:
                total[pl.ds(at, 1), :] = t
                accum[rows, :] = a

    two_deep(wide // HEAD_DIM // several, step, s0, s1, x0, x1)


def remote_scratch(kv, tokens, count):
    span = count * tokens
    several = 4
    return [
        pltpu.VMEM((kv * span, AUG), bf16),
        pltpu.VMEM((several * span, tokens), f32),
        pltpu.VMEM((several * span, tokens), f32),
        pltpu.VMEM((8 * several, tokens), f32),
        pltpu.VMEM((8 * several, tokens), f32),
    ]


def placed(shards, refs):
    return [(refs[ka], kr, refs[va], vr, flag) for ka, kr, va, vr, flag in shards]


def remote_kernel(group, shards, n, fqt, *refs):
    meta, peak_in, total_in, accum_in, peak, total, accum = refs[n : n + 7]
    remote_update(group, fqt, placed(shards, refs), meta, (peak_in, total_in, accum_in), (peak, total, accum), *refs[n + 7 :])


def remote(group, fqt, arrays, shards, meta, state):
    wide, tokens = fqt.shape
    heads = wide // HEAD_DIM
    count = len(shards)
    n = len(arrays)
    return pl.pallas_call(
        functools.partial(remote_kernel, group, shards, n),
        out_shape=tuple(jax.ShapeDtypeStruct(x.shape, x.dtype) for x in state),
        in_specs=[VM] * (n + 5),
        out_specs=(VM,) * 3,
        scratch_shapes=remote_scratch(heads // group, tokens, count),
        input_output_aliases={n + 2 + i: i for i in range(3)},
        compiler_params=pltpu.CompilerParams(vmem_limit_bytes=16 << 20),
        cost_estimate=pl.CostEstimate(
            flops=4 * wide * tokens * tokens * count * 4, transcendentals=heads * tokens * tokens * count, bytes_accessed=20 * wide * tokens
        ),
        name="remote",
    )(fqt, *arrays, meta, *state)


def last_kernel(group, shards, n, fqt, *refs):
    meta, peak_in, total_in, accum_in, held, mine, theirs = refs[n : n + 7]
    keys, s0, s1, x0, x1, peak, total, accum, mixed = refs[n + 7 :]
    remote_update(group, fqt, placed(shards, refs), meta, (peak_in, total_in, accum_in), (peak, total, accum), keys, s0, s1, x0, x1)
    wide, tokens = fqt.shape
    rows = tokens // 2
    for u in range(wide // HEAD_DIM):
        at = slice(u * HEAD_DIM, (u + 1) * HEAD_DIM)
        mixed[at, :] = (accum[at, :] / total[u : u + 1, :]).astype(bf16)
    first = meta[SIDE0 : SIDE0 + 1, :rows] > 0.0
    columns = held.shape[0]
    step = 4 * AUG
    for at in range(0, columns, step):
        size = min(step, columns - at)
        part = jnp.dot(held[at : at + size, :], mixed[...], preferred_element_type=f32).astype(bf16)
        low, high = part[:, :rows], part[:, rows:]
        mine[at : at + size, :] = jnp.where(first, low, high)
        theirs[at : at + size, :] = jnp.where(first, high, low)


def last(group, fqt, arrays, shards, meta, state, weight):
    wide, tokens = fqt.shape
    heads = wide // HEAD_DIM
    count = len(shards)
    n = len(arrays)
    return pl.pallas_call(
        functools.partial(last_kernel, group, shards, n),
        out_shape=(jax.ShapeDtypeStruct((weight.shape[0], tokens // 2), bf16),) * 2,
        in_specs=[VM] * (n + 6),
        out_specs=(VM, VM),
        scratch_shapes=remote_scratch(heads // group, tokens, count)
        + [
            pltpu.VMEM((heads, tokens), f32),
            pltpu.VMEM((heads, tokens), f32),
            pltpu.VMEM((wide, tokens), f32),
            pltpu.VMEM((wide, tokens), bf16),
        ],
        compiler_params=pltpu.CompilerParams(vmem_limit_bytes=28 << 20),
        cost_estimate=pl.CostEstimate(
            flops=4 * wide * tokens * tokens * count * 4, transcendentals=heads * tokens * tokens * count, bytes_accessed=20 * wide * tokens
        ),
        name="last",
    )(fqt, *arrays, meta, *state, weight)


def shifted_by(block, distance, first=None):
    size = lax.axis_size("ctx")
    route = [(i, (i + distance) % size) for i in range(size) if first is None or first <= i < size - distance]
    return lax.ppermute(block, "ctx", route)


def swapped(block, bit):
    size = lax.axis_size("ctx")
    return lax.ppermute(block, "ctx", [(i, i ^ bit) for i in range(size)])


def body(banded_queries, banded_keys, banded_values, full_queries, full_keys, full_values, segment_ids, position_ids, out_weight):
    tokens = segment_ids.shape[0]
    width = full_keys.shape[1]
    height = 2 * width + PAD
    vrow = width + PAD
    group = banded_queries.shape[1] // banded_keys.shape[1]
    here = lax.axis_index("ctx")
    half = HEAD_DIM // 2
    frequency = theta_base ** (-2.0 * jnp.arange(half, dtype=f32) / HEAD_DIM)
    frequency = jnp.broadcast_to(frequency[:, None], (half, tokens))
    base = (here * tokens).astype(jnp.int32).reshape(1)
    side = lax.axis_index("head").astype(jnp.int32)

    kv = jnp.concatenate([full_keys, full_values, banded_keys, banded_values], axis=1)
    ids_pos = jnp.stack([segment_ids, position_ids])
    block, band_kv, rim, meta, cosine, sine = prepare(base, side.reshape(1), frequency, kv, ids_pos)
    z1 = shifted_by(block, PLANE)
    fqt, bqt, *state = own(group, full_queries, banded_queries, cosine, sine, block, meta)
    z1, rim, block, state = lax.optimization_barrier((z1, rim, block, state))

    rim = shifted_by(rim, 1)
    z3 = shifted_by(z1, 2 * PLANE, PLANE)
    z2 = shifted_by(z1, PLANE, PLANE)
    x1 = swapped(z1, 1)
    y1 = swapped(z1, 2)
    state = remote(group, fqt, [z1], ((0, 0, 0, vrow, BACK + 1),), meta, state)
    rim, state = lax.optimization_barrier((rim, state))
    banded_out = band(group, bqt, band_kv, rim, meta)
    z2, z3, block, state, banded_out = lax.optimization_barrier((z2, z3, block, state, banded_out))

    def farthest(bit):
        return jnp.where((here & bit) == 0, block, z3)

    x2 = swapped(jnp.concatenate([z2, farthest(1)]), 1)
    y2 = swapped(jnp.concatenate([z2, farthest(2)]), 2)
    z2, z3, x1, y1 = lax.optimization_barrier((z2, z3, x1, y1))
    state = remote(group, fqt, [x1, y1, z2, z3], tuple((a, 0, a, vrow, flag) for a, flag in enumerate((BACK + 1, BACK + 1, BACK + 2, BACK + 3))), meta, state)
    x2, y2, state = lax.optimization_barrier((x2, y2, state))

    dx = swapped(jnp.concatenate([y1[:vrow], y2[height:]]), 1)
    dy = swapped(jnp.concatenate([x1[vrow:], x2[:height]]), 2)
    state = remote(
        group,
        fqt,
        [x2, y2],
        ((0, 0, 0, vrow, BACK + 2), (0, height, 0, height + vrow, PICK_X), (1, 0, 1, vrow, BACK + 2), (1, height, 1, height + vrow, PICK_Y)),
        meta,
        state,
    )
    dx, dy, state = lax.optimization_barrier((dx, dy, state))
    mine, theirs = last(
        group,
        fqt,
        [dx, dy],
        ((0, 0, 1, 0, BACK + 1), (0, vrow, 0, 2 * vrow, PICK_Y), (1, width, 1, width + vrow, BACK + 2)),
        meta,
        state,
        out_weight.T,
    )

    sides = lax.axis_size("head")
    if sides != 2:
        part = jnp.concatenate([jnp.where(side == 0, mine, theirs), jnp.where(side == 0, theirs, mine)], axis=1).T
        return banded_out, lax.psum_scatter(part, "head", scatter_dimension=0, tiled=True)
    theirs = lax.ppermute(theirs, "head", [(0, 1), (1, 0)])
    projected = (mine.astype(f32) + theirs.astype(f32)).astype(bf16)
    return banded_out, projected.T


def solution(mesh):
    return jax.shard_map(
        body,
        mesh=mesh,
        in_specs=(
            P("ctx", "head"),
            P("ctx", "head"),
            P("ctx", "head"),
            P("ctx", "head"),
            P("ctx", "head"),
            P("ctx", "head"),
            P("ctx"),
            P("ctx"),
            P("head", None),
        ),
        out_specs=(P("ctx", "head"), P(("ctx", "head"), None)),
        check_vma=False,
    )
```

```python
import functools

import jax
import jax.numpy as jnp
from jax import lax
from jax.experimental import pallas as pl
from jax.experimental.pallas import tpu as pltpu
from jax.sharding import PartitionSpec as P


HEAD_DIM = 64
WINDOW = 128
REACH = 12
PLANE = 4
PAD = 16
AUG = 2 * HEAD_DIM
META = 16
BACK = 2
PICK_X = BACK + REACH // PLANE + 1
PICK_Y = PICK_X + 1
SIDE0 = PICK_X + 2
LATER = PICK_X + 3

theta_base = 150000.0
neg_fill = -1e30
to_log2 = HEAD_DIM ** (-0.5) * 1.4426950408889634

f32 = jnp.float32
bf16 = jnp.bfloat16
VM = pl.BlockSpec(memory_space=pltpu.VMEM)
SM = pl.BlockSpec(memory_space=pltpu.SMEM)


def al(start, size):
    return pl.ds(pl.multiple_of(start, size), size)


def rotate_rows(rows, cosine, sine_term):
    half = HEAD_DIM // 2
    out = []
    for at in range(0, rows.shape[0], HEAD_DIM):
        leading = rows[at : at + half]
        trailing = rows[at + half : at + HEAD_DIM]
        out.append(leading * cosine - trailing * sine_term)
        out.append(trailing * cosine + leading * sine_term)
    return jnp.concatenate(out, axis=0).astype(bf16)


def write_block(block, rows, id_rows, cos, sin):
    width = rows.shape[0] // 2
    block[0:width, :] = rotate_rows(rows[:width], cos, sin)
    block[width : width + PAD, :] = id_rows
    block[width + PAD :, :] = rows[width:].astype(bf16)


def prepare_kernel(base, side, frequency, kv, ids_pos, block, band_block, rim, meta, cosine, sine):
    tokens = kv.shape[0]
    angles = ids_pos[1:2, :].astype(f32) * frequency[...]
    cos, sin = jnp.cos(angles), jnp.sin(angles)
    cosine[...] = cos
    sine[...] = sin
    ids = ids_pos[0:1, :]
    shifted = ids + 1
    row = lax.broadcasted_iota(jnp.int32, (PAD, tokens), 0)
    high = jnp.broadcast_to(shifted >> 7, (PAD, tokens))
    low = jnp.broadcast_to(shifted & 127, (PAD, tokens))
    id_rows = jnp.where(row == 0, high, jnp.where(row == 1, low, 0)).astype(f32).astype(bf16)
    half = kv.shape[1] // 2
    write_block(block, kv[:, :half].astype(f32).T, id_rows, cos, sin)
    write_block(band_block, kv[:, half:].astype(f32).T, id_rows, cos, sin)
    rim[...] = band_block[:, tokens - WINDOW :]
    ids_f = ids.astype(f32)
    across = jnp.broadcast_to(ids_f, (tokens, tokens))
    down = across.T
    before = jnp.max(jnp.where(down < across, down, -1.0), axis=0, keepdims=True)
    first = before < 0.0
    begin = jnp.where(first, 0.0, before + 1.0 - base[0].astype(f32))
    here = base[0] // tokens
    plane = here // PLANE
    farthest = REACH // PLANE
    rows = [begin, first.astype(f32), ids_f + 1.0]
    rows += [plane >= back for back in range(1, farthest + 1)]
    rows += [(here % 2 == 1) | (plane >= farthest), (here // 2 % 2 == 1) | (plane >= farthest)]
    rows += [side[0] == 0, here > 0]
    mrow = lax.broadcasted_iota(jnp.int32, meta.shape, 0)
    total = jnp.zeros(meta.shape, f32)
    for i, value in enumerate(rows):
        value = jnp.where(value, 1.0, 0.0) if value.dtype == jnp.bool_ else value
        total = jnp.where(mrow == i, jnp.broadcast_to(value, meta.shape), total)
    meta[...] = total


def prepare(base, side, frequency, kv, ids_pos):
    tokens, every = kv.shape
    height = every // 2 + PAD
    half = HEAD_DIM // 2
    return pl.pallas_call(
        prepare_kernel,
        out_shape=(
            jax.ShapeDtypeStruct((height, tokens), bf16),
            jax.ShapeDtypeStruct((height, tokens), bf16),
            jax.ShapeDtypeStruct((height, WINDOW), bf16),
            jax.ShapeDtypeStruct((META, tokens), f32),
            jax.ShapeDtypeStruct((half, tokens), f32),
            jax.ShapeDtypeStruct((half, tokens), f32),
        ),
        in_specs=[SM] * 2 + [VM] * 3,
        out_specs=(VM,) * 6,
        compiler_params=pltpu.CompilerParams(vmem_limit_bytes=8 << 20),
        name="prepare",
    )(base, side, frequency, kv, ids_pos)


def two_deep(units, step, s0, s1, x0, x1):
    even, odd = (s0, x0), (s1, x1)
    step(-1, None, even)

    def pair(i, _):
        step(2 * i, even, odd)
        step(2 * i + 1, odd, even)
        return 0

    lax.fori_loop(0, units // 2 - 1, pair, 0)
    step(units - 2, even, odd)
    step(units - 1, odd, None)


def by_tiles(tiles, scores, outs):
    def step(u, now, then):
        for tile in range(tiles):
            if then is not None:
                scores(u + 1, tile, *then)
            if now is not None:
                outs(u, tile, *now)

    return step


def column_peak(s):
    return jnp.broadcast_to(jnp.max(s, axis=0, keepdims=True), (8, s.shape[1]))


def transposed_keys(rows, extra):
    return jnp.concatenate([rows.astype(f32), extra], axis=0).T.astype(bf16)


def ids_of(rows):
    rows = rows.astype(f32)
    return rows[0:1] * 128.0 + rows[1:2]


def mask_rows(ids, own_id, present):
    bar = jnp.where((ids < own_id) | jnp.logical_not(present), neg_fill, 0.0)
    row = lax.broadcasted_iota(jnp.int32, (HEAD_DIM, ids.shape[1]), 0)
    return jnp.where(row == 0, jnp.broadcast_to(bar, row.shape), jnp.where(row == 1, 1.0, 0.0))


def rotate_into(src, dst, cos, sin):
    wide = src.shape[1]
    step = min(wide, 4 * AUG)
    for at in range(0, wide, step):
        dst[at : at + step, :] = rotate_rows(src[:, at : at + step].astype(f32).T, cos, sin)


def own_kernel(group, fq, bq, cosine, sine, block, meta, fqt, bqt, peak, total, accum, keys, bias, s0, s1, x0, x1):
    tokens, wide = fq.shape
    width = wide // group
    kv = width // HEAD_DIM
    rotate_into(fq, fqt, cosine[...], sine[...])
    zero = jnp.zeros((HEAD_DIM, tokens), f32)
    for h in range(kv):
        keys[h * tokens : (h + 1) * tokens, :] = transposed_keys(block[h * HEAD_DIM : (h + 1) * HEAD_DIM, :], zero)
    begin = jnp.broadcast_to(meta[0:1, :], (tokens, tokens)).astype(jnp.int32)
    r = lax.broadcasted_iota(jnp.int32, (tokens, tokens), 0)
    t = lax.broadcasted_iota(jnp.int32, (tokens, tokens), 1)
    bias[...] = jnp.where((r >= begin) & (r <= t), 0.0, neg_fill)
    several = s0.shape[0] // tokens

    def scores(u, g, buf, x):
        h = u * several // group
        k = keys[al(h * tokens, tokens), :][:, :HEAD_DIM]
        q = fqt[al((u * several + g) * HEAD_DIM, HEAD_DIM), :]
        s = jnp.dot(k, q, preferred_element_type=f32) + bias[...]
        buf[g * tokens : (g + 1) * tokens, :] = s
        x[8 * g : 8 * g + 8, :] = column_peak(s)

    def outs(u, g, buf, x):
        h = u * several // group
        v = block[pl.ds(pl.multiple_of(width + PAD + h * HEAD_DIM, PAD), HEAD_DIM), :]
        at = u * several + g
        m = x[8 * g : 8 * g + 1, :]
        p = jnp.exp2(buf[g * tokens : (g + 1) * tokens, :] * to_log2 - m * to_log2)
        peak[pl.ds(at, 1), :] = m
        total[pl.ds(at, 1), :] = jnp.sum(p, axis=0, keepdims=True)
        accum[al(at * HEAD_DIM, HEAD_DIM), :] = jnp.dot(v, p.astype(bf16), preferred_element_type=f32)

    two_deep(wide // HEAD_DIM // several, by_tiles(several, scores, outs), s0, s1, x0, x1)
    rotate_into(bq, bqt, cosine[...], sine[...])


def own(group, fq, bq, cosine, sine, block, meta):
    tokens, wide = fq.shape
    heads = wide // HEAD_DIM
    kv = heads // group
    several = 4
    return pl.pallas_call(
        functools.partial(own_kernel, group),
        out_shape=(
            jax.ShapeDtypeStruct((wide, tokens), bf16),
            jax.ShapeDtypeStruct((wide, tokens), bf16),
            jax.ShapeDtypeStruct((heads, tokens), f32),
            jax.ShapeDtypeStruct((heads, tokens), f32),
            jax.ShapeDtypeStruct((wide, tokens), f32),
        ),
        in_specs=[VM] * 6,
        out_specs=(VM,) * 5,
        scratch_shapes=[
            pltpu.VMEM((kv * tokens, AUG), bf16),
            pltpu.VMEM((tokens, tokens), f32),
            pltpu.VMEM((several * tokens, tokens), f32),
            pltpu.VMEM((several * tokens, tokens), f32),
            pltpu.VMEM((8 * several, tokens), f32),
            pltpu.VMEM((8 * several, tokens), f32),
        ],
        compiler_params=pltpu.CompilerParams(vmem_limit_bytes=16 << 20),
        cost_estimate=pl.CostEstimate(
            flops=4 * heads * tokens * tokens * HEAD_DIM * 4, transcendentals=heads * tokens * tokens, bytes_accessed=12 * wide * tokens
        ),
        name="own",
    )(fq, bq, cosine, sine, block, meta)


def band_kernel(group, bqt, block, rim, meta, out, keys, vals, bias, s0, s1, x0, x1):
    wide, tokens = bqt.shape
    width = wide // group
    kv = width // HEAD_DIM
    span = tokens + WINDOW
    tile = 2 * WINDOW
    zero = jnp.zeros((HEAD_DIM, tokens), f32)
    for h in range(kv):
        rows = slice(h * HEAD_DIM, (h + 1) * HEAD_DIM)
        keys[h * span : h * span + WINDOW, :] = transposed_keys(rim[rows, :], zero[:, :WINDOW])
        keys[h * span + WINDOW : (h + 1) * span, :] = transposed_keys(block[rows, :], zero)
    vals[:, :WINDOW] = rim[width + PAD :, :]
    vals[:, WINDOW:] = block[width + PAD :, :]
    own_id = jnp.min(meta[2:3, :])
    barred = (ids_of(rim[width : width + PAD, :]) < own_id) | (meta[LATER : LATER + 1, :WINDOW] == 0.0)
    barred = jnp.sum(barred.astype(f32))
    begin = meta[0:1, :]
    first = meta[1:2, :]
    r = lax.broadcasted_iota(jnp.int32, (tile, tile), 0).astype(f32)
    t = (lax.broadcasted_iota(jnp.int32, (1, tile), 1) & (WINDOW - 1)).astype(f32)
    halves = tokens // WINDOW
    for half in range(halves):
        lo = begin + float(WINDOW - half * WINDOW)
        if half == 0:
            lo = jnp.where(first > 0.0, barred, lo)
        lo = lo[:, half * WINDOW : (half + 1) * WINDOW]
        low = jnp.maximum(jnp.concatenate([lo, lo], axis=1), t + 1.0)
        bias[half * tile : (half + 1) * tile, :] = jnp.where((r >= low) & (r <= t + WINDOW), 0.0, neg_fill)
    pairs = group // 2
    several = s0.shape[0] // tile // halves

    def scores(u, at, buf, x):
        half, g = divmod(at, several)
        h = u * several // pairs
        k = keys[pl.ds(pl.multiple_of(h * span + half * WINDOW, WINDOW), tile), :][:, :HEAD_DIM]
        q = bqt[al((u * several + g) * AUG, AUG), :][:, half * WINDOW : (half + 1) * WINDOW]
        q = jnp.concatenate([q[:HEAD_DIM], q[HEAD_DIM:]], axis=1)
        s = jnp.dot(k, q, preferred_element_type=f32) + bias[half * tile : (half + 1) * tile, :]
        buf[at * tile : (at + 1) * tile, :] = s
        x[8 * at : 8 * at + 8, :] = column_peak(s)

    def outs(u, at, buf, x):
        half, g = divmod(at, several)
        h = u * several // pairs
        v = vals[al(h * HEAD_DIM, HEAD_DIM), half * WINDOW : half * WINDOW + tile]
        m = x[8 * at : 8 * at + 1, :]
        p = jnp.exp2(buf[at * tile : (at + 1) * tile, :] * to_log2 - m * to_log2)
        total = jnp.sum(p, axis=0, keepdims=True)
        o = jnp.dot(v, p.astype(bf16), preferred_element_type=f32) / total
        o = jnp.concatenate([o[:, :WINDOW], o[:, WINDOW:]], axis=0)
        out[half * WINDOW : (half + 1) * WINDOW, al((u * several + g) * AUG, AUG)] = o.T.astype(bf16)

    two_deep(kv * pairs // several, by_tiles(halves * several, scores, outs), s0, s1, x0, x1)


def band(group, bqt, block, rim, meta):
    wide, tokens = bqt.shape
    kv = wide // group // HEAD_DIM
    span = tokens + WINDOW
    several = 2
    tiles = several * (tokens // WINDOW)
    return pl.pallas_call(
        functools.partial(band_kernel, group),
        out_shape=jax.ShapeDtypeStruct((tokens, wide), bf16),
        in_specs=[VM] * 4,
        out_specs=VM,
        scratch_shapes=[
            pltpu.VMEM((kv * span, AUG), bf16),
            pltpu.VMEM((kv * HEAD_DIM, span), bf16),
            pltpu.VMEM((tokens // WINDOW * 2 * WINDOW, 2 * WINDOW), f32),
            pltpu.VMEM((tiles * 2 * WINDOW, 2 * WINDOW), f32),
            pltpu.VMEM((tiles * 2 * WINDOW, 2 * WINDOW), f32),
            pltpu.VMEM((8 * tiles, 2 * WINDOW), f32),
            pltpu.VMEM((8 * tiles, 2 * WINDOW), f32),
        ],
        compiler_params=pltpu.CompilerParams(vmem_limit_bytes=16 << 20),
        cost_estimate=pl.CostEstimate(
            flops=4 * wide * tokens * 2 * WINDOW * 4, transcendentals=wide // HEAD_DIM * tokens * 2 * WINDOW, bytes_accessed=4 * wide * tokens
        ),
        name="band",
    )(bqt, block, rim, meta)


def remote_update(group, fqt, shards, meta, state_in, state_out, keys, s0, s1, x0, x1):
    wide, tokens = fqt.shape
    width = wide // group
    kv = width // HEAD_DIM
    span = len(shards) * tokens
    peak_in, total_in, accum_in = state_in
    peak, total, accum = state_out
    own_id = jnp.min(meta[2:3, :])
    for b, (kref, krow, _, _, flag) in enumerate(shards):
        extra = mask_rows(ids_of(kref[krow + width : krow + width + PAD, :]), own_id, meta[flag : flag + 1, :] > 0.0)
        for h in range(kv):
            rows = kref[krow + h * HEAD_DIM : krow + (h + 1) * HEAD_DIM, :]
            keys[h * span + b * tokens : h * span + (b + 1) * tokens, :] = transposed_keys(rows, extra)
    row = lax.broadcasted_iota(jnp.int32, (HEAD_DIM, tokens), 0)
    other = jnp.where(meta[1:2, :] > 0.0, 0.0, neg_fill)
    query_rows = jnp.where(row == 0, 1.0, jnp.where(row == 1, jnp.broadcast_to(other, row.shape), 0.0)).astype(bf16)

    several = s0.shape[0] // span

    def step(u, now, then):
        h = u * several // group
        h_then = (u + 1) * several // group
        for g in range(several):
            top = None
            if then is not None:
                at = (u + 1) * several + g
                q = jnp.concatenate([fqt[al(at * HEAD_DIM, HEAD_DIM), :], query_rows], axis=0)
            if now is not None:
                buf, x = now
                at = u * several + g
                rows = al(at * HEAD_DIM, HEAD_DIM)
                old = peak_in[pl.ds(at, 1), :]
                m = jnp.maximum(old, x[8 * g : 8 * g + 1, :])
                scaled = m * to_log2
                factor = jnp.exp2(old * to_log2 - scaled)
                peak[pl.ds(at, 1), :] = m
                t = total_in[pl.ds(at, 1), :] * factor
                a = accum_in[rows, :] * factor
            for b, (_, _, vref, vrow, _) in enumerate(shards):
                where = slice(g * span + b * tokens, g * span + (b + 1) * tokens)
                if then is not None:
                    k = keys[pl.ds(pl.multiple_of(h_then * span + b * tokens, tokens), tokens), :]
                    s = jnp.dot(k, q, preferred_element_type=f32)
                    then[0][where, :] = s
                    high = jnp.max(s.reshape(tokens // 8, 8, tokens), axis=0)
                    top = high if top is None else jnp.maximum(top, high)
                if now is not None:
                    p = jnp.exp2(buf[where, :] * to_log2 - scaled)
                    t = t + jnp.sum(p, axis=0, keepdims=True)
                    v = vref[pl.ds(pl.multiple_of(vrow + h * HEAD_DIM, PAD), HEAD_DIM), :]
                    a = a + jnp.dot(v, p.astype(bf16), preferred_element_type=f32)
            if then is not None:
                then[1][8 * g : 8 * g + 8, :] = column_peak(top)
            if now is not None:
                total[pl.ds(at, 1), :] = t
                accum[rows, :] = a

    two_deep(wide // HEAD_DIM // several, step, s0, s1, x0, x1)


def remote_scratch(kv, tokens, count):
    span = count * tokens
    several = 4
    return [
        pltpu.VMEM((kv * span, AUG), bf16),
        pltpu.VMEM((several * span, tokens), f32),
        pltpu.VMEM((several * span, tokens), f32),
        pltpu.VMEM((8 * several, tokens), f32),
        pltpu.VMEM((8 * several, tokens), f32),
    ]


def placed(shards, refs):
    return [(refs[ka], kr, refs[va], vr, flag) for ka, kr, va, vr, flag in shards]


def remote_kernel(group, shards, n, fqt, *refs):
    meta, peak_in, total_in, accum_in, peak, total, accum = refs[n : n + 7]
    remote_update(group, fqt, placed(shards, refs), meta, (peak_in, total_in, accum_in), (peak, total, accum), *refs[n + 7 :])


def remote(group, fqt, arrays, shards, meta, state):
    wide, tokens = fqt.shape
    heads = wide // HEAD_DIM
    count = len(shards)
    n = len(arrays)
    return pl.pallas_call(
        functools.partial(remote_kernel, group, shards, n),
        out_shape=tuple(jax.ShapeDtypeStruct(x.shape, x.dtype) for x in state),
        in_specs=[VM] * (n + 5),
        out_specs=(VM,) * 3,
        scratch_shapes=remote_scratch(heads // group, tokens, count),
        input_output_aliases={n + 2 + i: i for i in range(3)},
        compiler_params=pltpu.CompilerParams(vmem_limit_bytes=16 << 20),
        cost_estimate=pl.CostEstimate(
            flops=4 * wide * tokens * tokens * count * 4, transcendentals=heads * tokens * tokens * count, bytes_accessed=20 * wide * tokens
        ),
        name="remote",
    )(fqt, *arrays, meta, *state)


def last_kernel(group, shards, n, fqt, *refs):
    meta, peak_in, total_in, accum_in, held, mine, theirs = refs[n : n + 7]
    keys, s0, s1, x0, x1, peak, total, accum, mixed = refs[n + 7 :]
    remote_update(group, fqt, placed(shards, refs), meta, (peak_in, total_in, accum_in), (peak, total, accum), keys, s0, s1, x0, x1)
    wide, tokens = fqt.shape
    rows = tokens // 2
    for u in range(wide // HEAD_DIM):
        at = slice(u * HEAD_DIM, (u + 1) * HEAD_DIM)
        mixed[at, :] = (accum[at, :] / total[u : u + 1, :]).astype(bf16)
    first = meta[SIDE0 : SIDE0 + 1, :rows] > 0.0
    columns = held.shape[0]
    step = 4 * AUG
    for at in range(0, columns, step):
        size = min(step, columns - at)
        part = jnp.dot(held[at : at + size, :], mixed[...], preferred_element_type=f32).astype(bf16)
        low, high = part[:, :rows], part[:, rows:]
        mine[at : at + size, :] = jnp.where(first, low, high)
        theirs[at : at + size, :] = jnp.where(first, high, low)


def last(group, fqt, arrays, shards, meta, state, weight):
    wide, tokens = fqt.shape
    heads = wide // HEAD_DIM
    count = len(shards)
    n = len(arrays)
    return pl.pallas_call(
        functools.partial(last_kernel, group, shards, n),
        out_shape=(jax.ShapeDtypeStruct((weight.shape[0], tokens // 2), bf16),) * 2,
        in_specs=[VM] * (n + 6),
        out_specs=(VM, VM),
        scratch_shapes=remote_scratch(heads // group, tokens, count)
        + [
            pltpu.VMEM((heads, tokens), f32),
            pltpu.VMEM((heads, tokens), f32),
            pltpu.VMEM((wide, tokens), f32),
            pltpu.VMEM((wide, tokens), bf16),
        ],
        compiler_params=pltpu.CompilerParams(vmem_limit_bytes=28 << 20),
        cost_estimate=pl.CostEstimate(
            flops=4 * wide * tokens * tokens * count * 4, transcendentals=heads * tokens * tokens * count, bytes_accessed=20 * wide * tokens
        ),
        name="last",
    )(fqt, *arrays, meta, *state, weight)


def shifted_by(block, distance, first=None):
    size = lax.axis_size("ctx")
    route = [(i, (i + distance) % size) for i in range(size) if first is None or first <= i < size - distance]
    return lax.ppermute(block, "ctx", route)


def swapped(block, bit):
    size = lax.axis_size("ctx")
    return lax.ppermute(block, "ctx", [(i, i ^ bit) for i in range(size)])


def body(banded_queries, banded_keys, banded_values, full_queries, full_keys, full_values, segment_ids, position_ids, out_weight):
    tokens = segment_ids.shape[0]
    width = full_keys.shape[1]
    height = 2 * width + PAD
    vrow = width + PAD
    group = banded_queries.shape[1] // banded_keys.shape[1]
    here = lax.axis_index("ctx")
    half = HEAD_DIM // 2
    frequency = theta_base ** (-2.0 * jnp.arange(half, dtype=f32) / HEAD_DIM)
    frequency = jnp.broadcast_to(frequency[:, None], (half, tokens))
    base = (here * tokens).astype(jnp.int32).reshape(1)
    side = lax.axis_index("head").astype(jnp.int32)

    kv = jnp.concatenate([full_keys, full_values, banded_keys, banded_values], axis=1)
    ids_pos = jnp.stack([segment_ids, position_ids])
    block, band_kv, rim, meta, cosine, sine = prepare(base, side.reshape(1), frequency, kv, ids_pos)
    z1 = shifted_by(block, PLANE)
    fqt, bqt, *state = own(group, full_queries, banded_queries, cosine, sine, block, meta)
    z1, rim, block, state = lax.optimization_barrier((z1, rim, block, state))

    rim = shifted_by(rim, 1)
    z3 = shifted_by(z1, 2 * PLANE, PLANE)
    z2 = shifted_by(z1, PLANE, PLANE)
    x1 = swapped(z1, 1)
    y1 = swapped(z1, 2)
    banded_out = band(group, bqt, band_kv, rim, meta)
    z2, z3, block, banded_out = lax.optimization_barrier((z2, z3, block, banded_out))

    def farthest(bit):
        return jnp.where((here & bit) == 0, block, z3)

    x2 = swapped(jnp.concatenate([z2, farthest(1)]), 1)
    y2 = swapped(jnp.concatenate([z2, farthest(2)]), 2)
    z1, z2, z3, x1, y1 = lax.optimization_barrier((z1, z2, z3, x1, y1))
    back = (BACK + 1, BACK + 1, BACK + 1, BACK + 2, BACK + 3)
    state = remote(group, fqt, [z1, x1, y1, z2, z3], tuple((a, 0, a, vrow, flag) for a, flag in enumerate(back)), meta, state)
    x2, y2, state = lax.optimization_barrier((x2, y2, state))

    dx = swapped(jnp.concatenate([y1[:vrow], y2[height:]]), 1)
    dy = swapped(jnp.concatenate([x1[vrow:], x2[:height]]), 2)
    state = remote(
        group,
        fqt,
        [x2, y2],
        ((0, 0, 0, vrow, BACK + 2), (0, height, 0, height + vrow, PICK_X), (1, 0, 1, vrow, BACK + 2), (1, height, 1, height + vrow, PICK_Y)),
        meta,
        state,
    )
    dx, dy, state = lax.optimization_barrier((dx, dy, state))
    mine, theirs = last(
        group,
        fqt,
        [dx, dy],
        ((0, 0, 1, 0, BACK + 1), (0, vrow, 0, 2 * vrow, PICK_Y), (1, width, 1, width + vrow, BACK + 2)),
        meta,
        state,
        out_weight.T,
    )

    sides = lax.axis_size("head")
    if sides != 2:
        part = jnp.concatenate([jnp.where(side == 0, mine, theirs), jnp.where(side == 0, theirs, mine)], axis=1).T
        return banded_out, lax.psum_scatter(part, "head", scatter_dimension=0, tiled=True)
    theirs = lax.ppermute(theirs, "head", [(0, 1), (1, 0)])
    projected = (mine.astype(f32) + theirs.astype(f32)).astype(bf16)
    return banded_out, projected.T


def solution(mesh):
    return jax.shard_map(
        body,
        mesh=mesh,
        in_specs=(
            P("ctx", "head"),
            P("ctx", "head"),
            P("ctx", "head"),
            P("ctx", "head"),
            P("ctx", "head"),
            P("ctx", "head"),
            P("ctx"),
            P("ctx"),
            P("head", None),
        ),
        out_specs=(P("ctx", "head"), P(("ctx", "head"), None)),
        check_vma=False,
    )
```

```python
import functools

import jax
import jax.numpy as jnp
from jax import lax
from jax.experimental import pallas as pl
from jax.experimental.pallas import tpu as pltpu
from jax.sharding import PartitionSpec as P


HEAD_DIM = 64
WINDOW = 128
REACH = 12
PLANE = 4
PAD = 16
AUG = 2 * HEAD_DIM
META = 16
BACK = 2
PICK_X = BACK + REACH // PLANE + 1
PICK_Y = PICK_X + 1
SIDE0 = PICK_X + 2
LATER = PICK_X + 3

theta_base = 150000.0
neg_fill = -1e30
to_log2 = HEAD_DIM ** (-0.5) * 1.4426950408889634

f32 = jnp.float32
bf16 = jnp.bfloat16
VM = pl.BlockSpec(memory_space=pltpu.VMEM)
SM = pl.BlockSpec(memory_space=pltpu.SMEM)
FAR = pl.BlockSpec(memory_space=pltpu.HBM)


def al(start, size):
    return pl.ds(pl.multiple_of(start, size), size)


def rotate_rows(rows, cosine, sine_term):
    half = HEAD_DIM // 2
    out = []
    for at in range(0, rows.shape[0], HEAD_DIM):
        leading = rows[at : at + half]
        trailing = rows[at + half : at + HEAD_DIM]
        out.append(leading * cosine - trailing * sine_term)
        out.append(trailing * cosine + leading * sine_term)
    return jnp.concatenate(out, axis=0).astype(bf16)


def write_block(block, rows, id_rows, cos, sin):
    width = rows.shape[0] // 2
    block[0:width, :] = rotate_rows(rows[:width], cos, sin)
    block[width : width + PAD, :] = id_rows
    block[width + PAD :, :] = rows[width:].astype(bf16)


def prepare_kernel(base, side, frequency, kv, ids_pos, block, band_block, rim, meta, cosine, sine):
    tokens = kv.shape[0]
    angles = ids_pos[1:2, :].astype(f32) * frequency[...]
    cos, sin = jnp.cos(angles), jnp.sin(angles)
    cosine[...] = cos
    sine[...] = sin
    ids = ids_pos[0:1, :]
    shifted = ids + 1
    row = lax.broadcasted_iota(jnp.int32, (PAD, tokens), 0)
    high = jnp.broadcast_to(shifted >> 7, (PAD, tokens))
    low = jnp.broadcast_to(shifted & 127, (PAD, tokens))
    id_rows = jnp.where(row == 0, high, jnp.where(row == 1, low, 0)).astype(f32).astype(bf16)
    half = kv.shape[1] // 2
    write_block(block, kv[:, :half].astype(f32).T, id_rows, cos, sin)
    write_block(band_block, kv[:, half:].astype(f32).T, id_rows, cos, sin)
    rim[...] = band_block[:, tokens - WINDOW :]
    ids_f = ids.astype(f32)
    across = jnp.broadcast_to(ids_f, (tokens, tokens))
    down = across.T
    before = jnp.max(jnp.where(down < across, down, -1.0), axis=0, keepdims=True)
    first = before < 0.0
    begin = jnp.where(first, 0.0, before + 1.0 - base[0].astype(f32))
    here = base[0] // tokens
    plane = here // PLANE
    farthest = REACH // PLANE
    rows = [begin, first.astype(f32), ids_f + 1.0]
    rows += [plane >= back for back in range(1, farthest + 1)]
    rows += [(here % 2 == 1) | (plane >= farthest), (here // 2 % 2 == 1) | (plane >= farthest)]
    rows += [side[0] == 0, here > 0]
    mrow = lax.broadcasted_iota(jnp.int32, meta.shape, 0)
    total = jnp.zeros(meta.shape, f32)
    for i, value in enumerate(rows):
        value = jnp.where(value, 1.0, 0.0) if value.dtype == jnp.bool_ else value
        total = jnp.where(mrow == i, jnp.broadcast_to(value, meta.shape), total)
    meta[...] = total


def prepare(base, side, frequency, kv, ids_pos):
    tokens, every = kv.shape
    height = every // 2 + PAD
    half = HEAD_DIM // 2
    return pl.pallas_call(
        prepare_kernel,
        out_shape=(
            jax.ShapeDtypeStruct((height, tokens), bf16),
            jax.ShapeDtypeStruct((height, tokens), bf16),
            jax.ShapeDtypeStruct((height, WINDOW), bf16),
            jax.ShapeDtypeStruct((META, tokens), f32),
            jax.ShapeDtypeStruct((half, tokens), f32),
            jax.ShapeDtypeStruct((half, tokens), f32),
        ),
        in_specs=[SM] * 2 + [VM] * 3,
        out_specs=(VM,) * 6,
        compiler_params=pltpu.CompilerParams(vmem_limit_bytes=8 << 20),
        name="prepare",
    )(base, side, frequency, kv, ids_pos)


def two_deep(units, step, s0, s1, x0, x1):
    even, odd = (s0, x0), (s1, x1)
    step(-1, None, even)

    def pair(i, _):
        step(2 * i, even, odd)
        step(2 * i + 1, odd, even)
        return 0

    lax.fori_loop(0, units // 2 - 1, pair, 0)
    step(units - 2, even, odd)
    step(units - 1, odd, None)


def by_tiles(tiles, scores, outs):
    def step(u, now, then):
        for tile in range(tiles):
            if then is not None:
                scores(u + 1, tile, *then)
            if now is not None:
                outs(u, tile, *now)

    return step


def column_peak(s):
    return jnp.broadcast_to(jnp.max(s, axis=0, keepdims=True), (8, s.shape[1]))


def transposed_keys(rows, extra):
    return jnp.concatenate([rows.astype(f32), extra], axis=0).T.astype(bf16)


def ids_of(rows):
    rows = rows.astype(f32)
    return rows[0:1] * 128.0 + rows[1:2]


def mask_rows(ids, own_id, present):
    bar = jnp.where((ids < own_id) | jnp.logical_not(present), neg_fill, 0.0)
    row = lax.broadcasted_iota(jnp.int32, (HEAD_DIM, ids.shape[1]), 0)
    return jnp.where(row == 0, jnp.broadcast_to(bar, row.shape), jnp.where(row == 1, 1.0, 0.0))


def rotate_into(src, dst, cos, sin):
    wide = src.shape[1]
    step = min(wide, 4 * AUG)
    for at in range(0, wide, step):
        dst[at : at + step, :] = rotate_rows(src[:, at : at + step].astype(f32).T, cos, sin)


def band_bias(half, begin, first, barred):
    tile = 2 * WINDOW
    r = lax.broadcasted_iota(jnp.int32, (tile, tile), 0).astype(f32)
    t = (lax.broadcasted_iota(jnp.int32, (1, tile), 1) & (WINDOW - 1)).astype(f32)
    lo = begin + float(WINDOW - half * WINDOW)
    if half == 0:
        lo = jnp.where(first > 0.0, barred, lo)
    lo = lo[:, half * WINDOW : (half + 1) * WINDOW]
    low = jnp.maximum(jnp.concatenate([lo, lo], axis=1), t + 1.0)
    return jnp.where((r >= low) & (r <= t + WINDOW), 0.0, neg_fill)


def band_several(wide):
    return 4 if wide // AUG >= 8 else 2


def band_half(group, half, bqt, bias, key_of, value_of, stage, s0, s1, x0, x1):
    wide = bqt.shape[0]
    tile = 2 * WINDOW
    pairs = group // 2
    several = band_several(wide)

    def scores(u, g, buf, x):
        h = u * several // pairs
        q = bqt[al((u * several + g) * AUG, AUG), :][:, half * WINDOW : (half + 1) * WINDOW]
        q = jnp.concatenate([q[:HEAD_DIM], q[HEAD_DIM:]], axis=1)
        s = jnp.dot(key_of(h)[:, :HEAD_DIM], q, preferred_element_type=f32) + bias[...]
        buf[g * tile : (g + 1) * tile, :] = s
        x[8 * g : 8 * g + 8, :] = column_peak(s)

    def outs(u, g, buf, x):
        h = u * several // pairs
        m = x[8 * g : 8 * g + 1, :]
        p = jnp.exp2(buf[g * tile : (g + 1) * tile, :] * to_log2 - m * to_log2)
        total = jnp.sum(p, axis=0, keepdims=True)
        o = jnp.dot(value_of(h), p.astype(bf16), preferred_element_type=f32) / total
        o = jnp.concatenate([o[:, :WINDOW], o[:, WINDOW:]], axis=0)
        stage[:, al((u * several + g) * AUG, AUG)] = o.T.astype(bf16)

    two_deep(wide // AUG // several, by_tiles(several, scores, outs), s0, s1, x0, x1)


def band_scratch(wide):
    tile = 2 * WINDOW
    rows = band_several(wide)
    return [
        pltpu.VMEM((WINDOW, wide), bf16),
        pltpu.VMEM((tile, tile), f32),
        pltpu.VMEM((rows * tile, tile), f32),
        pltpu.VMEM((rows * tile, tile), f32),
        pltpu.VMEM((8 * rows, tile), f32),
        pltpu.VMEM((8 * rows, tile), f32),
    ]


def own_kernel(
    group, fq, bq, cosine, sine, block, band_block, meta, fqt, bqt, peak, total, accum, out, keys, bias, s0, s1, x0, x1, band_keys, sem, stage, *scratch
):
    tokens, wide = fq.shape
    width = wide // group
    kv = width // HEAD_DIM
    rotate_into(fq, fqt, cosine[...], sine[...])
    zero = jnp.zeros((HEAD_DIM, tokens), f32)
    for h in range(kv):
        keys[h * tokens : (h + 1) * tokens, :] = transposed_keys(block[h * HEAD_DIM : (h + 1) * HEAD_DIM, :], zero)
    begin = jnp.broadcast_to(meta[0:1, :], (tokens, tokens)).astype(jnp.int32)
    r = lax.broadcasted_iota(jnp.int32, (tokens, tokens), 0)
    t = lax.broadcasted_iota(jnp.int32, (tokens, tokens), 1)
    bias[...] = jnp.where((r >= begin) & (r <= t), 0.0, neg_fill)
    several = s0.shape[0] // tokens

    def scores(u, g, buf, x):
        h = u * several // group
        k = keys[al(h * tokens, tokens), :][:, :HEAD_DIM]
        q = fqt[al((u * several + g) * HEAD_DIM, HEAD_DIM), :]
        s = jnp.dot(k, q, preferred_element_type=f32) + bias[...]
        buf[g * tokens : (g + 1) * tokens, :] = s
        x[8 * g : 8 * g + 8, :] = column_peak(s)

    def outs(u, g, buf, x):
        h = u * several // group
        v = block[pl.ds(pl.multiple_of(width + PAD + h * HEAD_DIM, PAD), HEAD_DIM), :]
        at = u * several + g
        m = x[8 * g : 8 * g + 1, :]
        p = jnp.exp2(buf[g * tokens : (g + 1) * tokens, :] * to_log2 - m * to_log2)
        peak[pl.ds(at, 1), :] = m
        total[pl.ds(at, 1), :] = jnp.sum(p, axis=0, keepdims=True)
        accum[al(at * HEAD_DIM, HEAD_DIM), :] = jnp.dot(v, p.astype(bf16), preferred_element_type=f32)

    two_deep(wide // HEAD_DIM // several, by_tiles(several, scores, outs), s0, s1, x0, x1)
    rotate_into(bq, bqt, cosine[...], sine[...])
    for h in range(kv):
        band_keys[h * tokens : (h + 1) * tokens, :] = transposed_keys(band_block[h * HEAD_DIM : (h + 1) * HEAD_DIM, :], zero)
    for half in range(1, tokens // WINDOW):
        at = (half - 1) * WINDOW
        scratch[0][...] = band_bias(half, meta[0:1, :], None, None)
        band_half(
            group,
            half,
            bqt,
            scratch[0],
            lambda h: band_keys[pl.ds(pl.multiple_of(h * tokens + at, WINDOW), 2 * WINDOW), :],
            lambda h: band_block[pl.ds(pl.multiple_of(width + PAD + h * HEAD_DIM, PAD), HEAD_DIM), at : at + 2 * WINDOW],
            stage,
            *scratch[1:],
        )
        copy = pltpu.make_async_copy(stage, out.at[half * WINDOW : (half + 1) * WINDOW, :], sem)
        copy.start()
        copy.wait()


def own(group, fq, bq, cosine, sine, block, band_block, meta):
    tokens, wide = fq.shape
    heads = wide // HEAD_DIM
    kv = heads // group
    several = 4
    return pl.pallas_call(
        functools.partial(own_kernel, group),
        out_shape=(
            jax.ShapeDtypeStruct((wide, tokens), bf16),
            jax.ShapeDtypeStruct((wide, tokens), bf16),
            jax.ShapeDtypeStruct((heads, tokens), f32),
            jax.ShapeDtypeStruct((heads, tokens), f32),
            jax.ShapeDtypeStruct((wide, tokens), f32),
            jax.ShapeDtypeStruct((tokens, wide), bf16),
        ),
        in_specs=[VM] * 7,
        out_specs=(VM,) * 5 + (FAR,),
        scratch_shapes=[
            pltpu.VMEM((kv * tokens, AUG), bf16),
            pltpu.VMEM((tokens, tokens), f32),
            pltpu.VMEM((several * tokens, tokens), f32),
            pltpu.VMEM((several * tokens, tokens), f32),
            pltpu.VMEM((8 * several, tokens), f32),
            pltpu.VMEM((8 * several, tokens), f32),
            pltpu.VMEM((kv * tokens, AUG), bf16),
            pltpu.SemaphoreType.DMA,
            *band_scratch(wide),
        ],
        compiler_params=pltpu.CompilerParams(vmem_limit_bytes=16 << 20),
        cost_estimate=pl.CostEstimate(
            flops=4 * heads * tokens * tokens * HEAD_DIM * 4, transcendentals=heads * tokens * tokens, bytes_accessed=12 * wide * tokens
        ),
        name="own",
    )(fq, bq, cosine, sine, block, band_block, meta)


def band_kernel(group, bqt, block, rim, meta, _, out, keys, vals, sem, stage, bias, s0, s1, x0, x1):
    wide, _ = bqt.shape
    width = wide // group
    kv = width // HEAD_DIM
    tile = 2 * WINDOW
    zero = jnp.zeros((HEAD_DIM, WINDOW), f32)
    for h in range(kv):
        rows = slice(h * HEAD_DIM, (h + 1) * HEAD_DIM)
        keys[h * tile : h * tile + WINDOW, :] = transposed_keys(rim[rows, :], zero)
        keys[h * tile + WINDOW : (h + 1) * tile, :] = transposed_keys(block[rows, :WINDOW], zero)
    vals[:, :WINDOW] = rim[width + PAD :, :]
    vals[:, WINDOW:] = block[width + PAD :, :WINDOW]
    own_id = jnp.min(meta[2:3, :])
    barred = (ids_of(rim[width : width + PAD, :]) < own_id) | (meta[LATER : LATER + 1, :WINDOW] == 0.0)
    bias[...] = band_bias(0, meta[0:1, :], meta[1:2, :], jnp.sum(barred.astype(f32)))
    band_half(
        group, 0, bqt, bias, lambda h: keys[al(h * tile, tile), :], lambda h: vals[al(h * HEAD_DIM, HEAD_DIM), :], stage, s0, s1, x0, x1
    )
    copy = pltpu.make_async_copy(stage, out.at[:WINDOW, :], sem)
    copy.start()
    copy.wait()


def band(group, bqt, block, rim, meta, rest):
    wide, tokens = bqt.shape
    kv = wide // group // HEAD_DIM
    tile = 2 * WINDOW
    return pl.pallas_call(
        functools.partial(band_kernel, group),
        out_shape=jax.ShapeDtypeStruct((tokens, wide), bf16),
        in_specs=[VM] * 4 + [FAR],
        out_specs=FAR,
        input_output_aliases={4: 0},
        scratch_shapes=[
            pltpu.VMEM((kv * tile, AUG), bf16),
            pltpu.VMEM((kv * HEAD_DIM, tile), bf16),
            pltpu.SemaphoreType.DMA,
            *band_scratch(wide),
        ],
        compiler_params=pltpu.CompilerParams(vmem_limit_bytes=16 << 20),
        cost_estimate=pl.CostEstimate(
            flops=4 * wide * WINDOW * tile * 4, transcendentals=wide // HEAD_DIM * WINDOW * tile, bytes_accessed=4 * wide * tokens
        ),
        name="band",
    )(bqt, block, rim, meta, rest)


def remote_update(group, fqt, shards, meta, state_in, state_out, keys, s0, s1, x0, x1):
    wide, tokens = fqt.shape
    width = wide // group
    kv = width // HEAD_DIM
    span = len(shards) * tokens
    peak_in, total_in, accum_in = state_in
    peak, total, accum = state_out
    own_id = jnp.min(meta[2:3, :])
    for b, (kref, krow, _, _, flag) in enumerate(shards):
        extra = mask_rows(ids_of(kref[krow + width : krow + width + PAD, :]), own_id, meta[flag : flag + 1, :] > 0.0)
        for h in range(kv):
            rows = kref[krow + h * HEAD_DIM : krow + (h + 1) * HEAD_DIM, :]
            keys[h * span + b * tokens : h * span + (b + 1) * tokens, :] = transposed_keys(rows, extra)
    row = lax.broadcasted_iota(jnp.int32, (HEAD_DIM, tokens), 0)
    other = jnp.where(meta[1:2, :] > 0.0, 0.0, neg_fill)
    query_rows = jnp.where(row == 0, 1.0, jnp.where(row == 1, jnp.broadcast_to(other, row.shape), 0.0)).astype(bf16)

    several = s0.shape[0] // span

    def step(u, now, then):
        h = u * several // group
        h_then = (u + 1) * several // group
        for g in range(several):
            top = None
            if then is not None:
                at = (u + 1) * several + g
                q = jnp.concatenate([fqt[al(at * HEAD_DIM, HEAD_DIM), :], query_rows], axis=0)
            if now is not None:
                buf, x = now
                at = u * several + g
                rows = al(at * HEAD_DIM, HEAD_DIM)
                old = peak_in[pl.ds(at, 1), :]
                m = jnp.maximum(old, x[8 * g : 8 * g + 1, :])
                scaled = m * to_log2
                factor = jnp.exp2(old * to_log2 - scaled)
                peak[pl.ds(at, 1), :] = m
                t = total_in[pl.ds(at, 1), :] * factor
                a = accum_in[rows, :] * factor
            for b, (_, _, vref, vrow, _) in enumerate(shards):
                where = slice(g * span + b * tokens, g * span + (b + 1) * tokens)
                if then is not None:
                    k = keys[pl.ds(pl.multiple_of(h_then * span + b * tokens, tokens), tokens), :]
                    s = jnp.dot(k, q, preferred_element_type=f32)
                    then[0][where, :] = s
                    high = jnp.max(s.reshape(tokens // 8, 8, tokens), axis=0)
                    top = high if top is None else jnp.maximum(top, high)
                if now is not None:
                    p = jnp.exp2(buf[where, :] * to_log2 - scaled)
                    t = t + jnp.sum(p, axis=0, keepdims=True)
                    v = vref[pl.ds(pl.multiple_of(vrow + h * HEAD_DIM, PAD), HEAD_DIM), :]
                    a = a + jnp.dot(v, p.astype(bf16), preferred_element_type=f32)
            if then is not None:
                then[1][8 * g : 8 * g + 8, :] = column_peak(top)
            if now is not None:
                total[pl.ds(at, 1), :] = t
                accum[rows, :] = a

    two_deep(wide // HEAD_DIM // several, step, s0, s1, x0, x1)


def remote_scratch(kv, tokens, count):
    span = count * tokens
    several = 4
    return [
        pltpu.VMEM((kv * span, AUG), bf16),
        pltpu.VMEM((several * span, tokens), f32),
        pltpu.VMEM((several * span, tokens), f32),
        pltpu.VMEM((8 * several, tokens), f32),
        pltpu.VMEM((8 * several, tokens), f32),
    ]


def placed(shards, refs):
    return [(refs[ka], kr, refs[va], vr, flag) for ka, kr, va, vr, flag in shards]


def remote_kernel(group, shards, n, fqt, *refs):
    meta, peak_in, total_in, accum_in, peak, total, accum = refs[n : n + 7]
    remote_update(group, fqt, placed(shards, refs), meta, (peak_in, total_in, accum_in), (peak, total, accum), *refs[n + 7 :])


def remote(group, fqt, arrays, shards, meta, state):
    wide, tokens = fqt.shape
    heads = wide // HEAD_DIM
    count = len(shards)
    n = len(arrays)
    return pl.pallas_call(
        functools.partial(remote_kernel, group, shards, n),
        out_shape=tuple(jax.ShapeDtypeStruct(x.shape, x.dtype) for x in state),
        in_specs=[VM] * (n + 5),
        out_specs=(VM,) * 3,
        scratch_shapes=remote_scratch(heads // group, tokens, count),
        input_output_aliases={n + 2 + i: i for i in range(3)},
        compiler_params=pltpu.CompilerParams(vmem_limit_bytes=16 << 20),
        cost_estimate=pl.CostEstimate(
            flops=4 * wide * tokens * tokens * count * 4, transcendentals=heads * tokens * tokens * count, bytes_accessed=20 * wide * tokens
        ),
        name="remote",
    )(fqt, *arrays, meta, *state)


def last_kernel(group, shards, n, fqt, *refs):
    meta, peak_in, total_in, accum_in, held, mine, theirs = refs[n : n + 7]
    keys, s0, s1, x0, x1, peak, total, accum, mixed = refs[n + 7 :]
    remote_update(group, fqt, placed(shards, refs), meta, (peak_in, total_in, accum_in), (peak, total, accum), keys, s0, s1, x0, x1)
    wide, tokens = fqt.shape
    rows = tokens // 2
    for u in range(wide // HEAD_DIM):
        at = slice(u * HEAD_DIM, (u + 1) * HEAD_DIM)
        mixed[at, :] = (accum[at, :] / total[u : u + 1, :]).astype(bf16)
    first = meta[SIDE0 : SIDE0 + 1, :rows] > 0.0
    columns = held.shape[0]
    step = 4 * AUG
    for at in range(0, columns, step):
        size = min(step, columns - at)
        part = jnp.dot(held[at : at + size, :], mixed[...], preferred_element_type=f32).astype(bf16)
        low, high = part[:, :rows], part[:, rows:]
        mine[at : at + size, :] = jnp.where(first, low, high)
        theirs[at : at + size, :] = jnp.where(first, high, low)


def last(group, fqt, arrays, shards, meta, state, weight):
    wide, tokens = fqt.shape
    heads = wide // HEAD_DIM
    count = len(shards)
    n = len(arrays)
    return pl.pallas_call(
        functools.partial(last_kernel, group, shards, n),
        out_shape=(jax.ShapeDtypeStruct((weight.shape[0], tokens // 2), bf16),) * 2,
        in_specs=[VM] * (n + 6),
        out_specs=(VM, VM),
        scratch_shapes=remote_scratch(heads // group, tokens, count)
        + [
            pltpu.VMEM((heads, tokens), f32),
            pltpu.VMEM((heads, tokens), f32),
            pltpu.VMEM((wide, tokens), f32),
            pltpu.VMEM((wide, tokens), bf16),
        ],
        compiler_params=pltpu.CompilerParams(vmem_limit_bytes=28 << 20),
        cost_estimate=pl.CostEstimate(
            flops=4 * wide * tokens * tokens * count * 4, transcendentals=heads * tokens * tokens * count, bytes_accessed=20 * wide * tokens
        ),
        name="last",
    )(fqt, *arrays, meta, *state, weight)


def shifted_by(block, distance, first=None):
    size = lax.axis_size("ctx")
    route = [(i, (i + distance) % size) for i in range(size) if first is None or first <= i < size - distance]
    return lax.ppermute(block, "ctx", route)


def swapped(block, bit):
    size = lax.axis_size("ctx")
    return lax.ppermute(block, "ctx", [(i, i ^ bit) for i in range(size)])


def body(banded_queries, banded_keys, banded_values, full_queries, full_keys, full_values, segment_ids, position_ids, out_weight):
    tokens = segment_ids.shape[0]
    width = full_keys.shape[1]
    height = 2 * width + PAD
    vrow = width + PAD
    group = banded_queries.shape[1] // banded_keys.shape[1]
    here = lax.axis_index("ctx")
    half = HEAD_DIM // 2
    frequency = theta_base ** (-2.0 * jnp.arange(half, dtype=f32) / HEAD_DIM)
    frequency = jnp.broadcast_to(frequency[:, None], (half, tokens))
    base = (here * tokens).astype(jnp.int32).reshape(1)
    side = lax.axis_index("head").astype(jnp.int32)

    kv = jnp.concatenate([full_keys, full_values, banded_keys, banded_values], axis=1)
    ids_pos = jnp.stack([segment_ids, position_ids])
    block, band_kv, rim, meta, cosine, sine = prepare(base, side.reshape(1), frequency, kv, ids_pos)
    z1 = shifted_by(block, PLANE)
    fqt, bqt, *state, banded_out = own(group, full_queries, banded_queries, cosine, sine, block, band_kv, meta)
    z1, rim, block, state = lax.optimization_barrier((z1, rim, block, state))

    rim = shifted_by(rim, 1)
    z3 = shifted_by(z1, 2 * PLANE, PLANE)
    z2 = shifted_by(z1, PLANE, PLANE)
    x1 = swapped(z1, 1)
    y1 = swapped(z1, 2)
    state = remote(group, fqt, [z1], ((0, 0, 0, vrow, BACK + 1),), meta, state)
    rim, state = lax.optimization_barrier((rim, state))
    banded_out = band(group, bqt, band_kv, rim, meta, banded_out)
    z2, z3, block, state, banded_out = lax.optimization_barrier((z2, z3, block, state, banded_out))

    def farthest(bit):
        return jnp.where((here & bit) == 0, block, z3)

    x2 = swapped(jnp.concatenate([z2, farthest(1)]), 1)
    y2 = swapped(jnp.concatenate([z2, farthest(2)]), 2)
    z2, z3, x1, y1 = lax.optimization_barrier((z2, z3, x1, y1))
    state = remote(group, fqt, [x1, y1, z2, z3], tuple((a, 0, a, vrow, flag) for a, flag in enumerate((BACK + 1, BACK + 1, BACK + 2, BACK + 3))), meta, state)
    x2, y2, state = lax.optimization_barrier((x2, y2, state))

    dx = swapped(jnp.concatenate([y1[:vrow], y2[height:]]), 1)
    dy = swapped(jnp.concatenate([x1[vrow:], x2[:height]]), 2)
    state = remote(
        group,
        fqt,
        [x2, y2],
        ((0, 0, 0, vrow, BACK + 2), (0, height, 0, height + vrow, PICK_X), (1, 0, 1, vrow, BACK + 2), (1, height, 1, height + vrow, PICK_Y)),
        meta,
        state,
    )
    dx, dy, state = lax.optimization_barrier((dx, dy, state))
    mine, theirs = last(
        group,
        fqt,
        [dx, dy],
        ((0, 0, 1, 0, BACK + 1), (0, vrow, 0, 2 * vrow, PICK_Y), (1, width, 1, width + vrow, BACK + 2)),
        meta,
        state,
        out_weight.T,
    )

    sides = lax.axis_size("head")
    if sides != 2:
        part = jnp.concatenate([jnp.where(side == 0, mine, theirs), jnp.where(side == 0, theirs, mine)], axis=1).T
        return banded_out, lax.psum_scatter(part, "head", scatter_dimension=0, tiled=True)
    theirs = lax.ppermute(theirs, "head", [(0, 1), (1, 0)])
    projected = (mine.astype(f32) + theirs.astype(f32)).astype(bf16)
    return banded_out, projected.T


def solution(mesh):
    return jax.shard_map(
        body,
        mesh=mesh,
        in_specs=(
            P("ctx", "head"),
            P("ctx", "head"),
            P("ctx", "head"),
            P("ctx", "head"),
            P("ctx", "head"),
            P("ctx", "head"),
            P("ctx"),
            P("ctx"),
            P("head", None),
        ),
        out_specs=(P("ctx", "head"), P(("ctx", "head"), None)),
        check_vma=False,
    )
```
